32 devices in a mesh: samp: 16 (over z, y, x), mark: 2 (over core).
Axes of the slice: x: 2, y: 2, z: 4, core: 2. Of those that a mesh axis runs over, the one named last changes fastest.
Arguments:
- genotypes: bfloat16 [16000, 12288], P('mark', 'samp'), may hold values from -6 to 6
- variants: bfloat16 [2048, 12288], P('mark', 'samp'), may hold values from -6 to 6
- weights: float32 [12288], P('samp'), may hold values from 0.05 to 0.25
- variance_ratio: float32 [1], replicated, may hold values from 1 to 4
- panel: float32 [24, 12288], P(None, 'samp'), may hold values from -24 to 24
- gene_sizes: int32 [2, 24], P('mark'), may hold values from 1 to 400, 1024 in all within a row
Outputs:
- solution: float32 [24, 12288], P(None, 'samp')
- residual: float32 [24, 12288], P(None, 'samp')
- direction: float32 [24, 12288], P(None, 'samp')
- gene_gram: float32 [2, 1024, 1024], P('mark', 'samp')
The draws below stay inside these ranges and needn't reach their ends.
Inputs may be any that keep to these rules, and one draw needn't show every extreme that they name: `gene_sizes`: row j lists in order the sizes of the genes that partition the 1024 test variants of block j, and sums to 1024.
All inputs are finite; a program needn't handle non-finite values.
Results may differ from the reference program's by a relative error of at most 0.0044.
Values sent between devices are 32-bit elements; how exact they have to be, the bound alone decides.
No kernel may reach another device: no remote copies, remote signals or barrier semaphores. Data moves between devices by JAX's collectives and lax.ppermute only.
A program may use at most 64 MiB of HBM per device.

```python
import math
import jax
import jax.numpy as jnp
import numpy as np
from jax import lax

MARKERS = 16000
K = 24
VAR_DEV = 1024
GENES = 24
GMAX = 400
NSAMP = 12288
NV = 2048
N_MARK = 2


def steps_of(own_key, shape, cuts, low, top_value):
    def one(axis_at, parts):
        draws = jax.random.uniform(jax.random.fold_in(jax.random.fold_in(own_key, 6), axis_at), (parts,), jnp.float32, low / len(cuts), top_value / len(cuts))
        return jnp.repeat(jnp.exp(draws), shape[axis_at] // parts).reshape((-1,) + (1,) * (len(shape) - axis_at - 1))

    loudness = one(*cuts[0])
    for cut in cuts[1:]:
        loudness = loudness * one(*cut)
    return loudness


def profile(count, total, bound, lean):
    weights = [(1 << 20) // math.isqrt(rank ** lean) + 1 for rank in range(2, count + 1)]
    spare, given = total - bound - (count - 1), [1] * (count - 1)
    while spare > 0:
        free = [i for i in range(count - 1) if given[i] < bound]
        mass, remaining = sum([weights[i] for i in free]), spare
        for i in free:
            more = min(bound - given[i], max(1, remaining * weights[i] // mass), spare)
            given[i] = given[i] + more
            spare = spare - more
    return np.array([bound] + given)


def uneven(key, count, total, reach, lean):
    if count == 2:
        one = jax.random.randint(key, (), max(1, total - reach), min(reach, total - 1) + 1)
        return jnp.stack([one, total - one])
    sizes = jnp.asarray(profile(count, total, reach, lean), jnp.int32)
    twos = (count - 1) // 2
    donor, sink = sizes[1:1 + 2 * twos:2], sizes[2:2 + 2 * twos:2]
    margin = jnp.minimum(donor - 1, reach - sink)
    moved = jax.random.randint(jax.random.fold_in(key, 1), (twos,), 0, 1 << 20) % (margin + 1)
    sizes = sizes.at[1:1 + 2 * twos:2].set(donor - moved).at[2:2 + 2 * twos:2].set(sink + moved)
    return sizes[jax.random.permutation(jax.random.fold_in(key, 2), count)]


def bell_draw(key, dims, width, bound, shards=(), kind=jnp.bfloat16):
    gain = steps_of(key, dims, shards, -0.22, 0.18) if shards else 1.0
    drawn = jax.random.normal(key, dims, jnp.float32) * width * gain
    return jnp.minimum(jnp.maximum(drawn, -bound), bound).astype(kind)


def setup_inputs(seed: int = 0) -> dict:
    key_list = jax.random.split(jax.random.key(seed), 7)
    return {
        "genotypes": bell_draw(key_list[0], (MARKERS, NSAMP), 1.0, 6.0, ((0, 2), (1, 16))),
        "variants": bell_draw(key_list[1], (NV, NSAMP), 1.0, 6.0, ((0, 2), (1, 16))),
        "weights": jnp.clip(jnp.exp(math.log(0.25) - 1.609438 * jax.random.uniform(key_list[2], (NSAMP,), jnp.float32) ** steps_of(key_list[2], (NSAMP,), ((0, 16),), -0.2, 0.2)), 0.05, 0.25),
        "variance_ratio": jnp.clip(jax.random.uniform(key_list[3], (1,), jnp.float32, 1.0, 4.0), 1.0, 4.0),
        "panel": bell_draw(key_list[4], (K, NSAMP), 4.0, 24.0, ((1, 16),), jnp.float32),
        "gene_sizes": jax.vmap(lambda own: uneven(own, GENES, VAR_DEV, GMAX, 2))(jax.random.split(key_list[5], N_MARK)).reshape((N_MARK, GENES)).astype(jnp.int32),
    }


def reference(genotypes, variants, weights, variance_ratio, panel, gene_sizes):
    ratio = variance_ratio[0]
    diag = 1.0 / weights + ratio
    start_dir = panel / diag
    start_norm = jnp.sum(panel * start_dir, axis=1)
    raw_scores = lax.dot_general(start_dir.astype(jnp.bfloat16), genotypes, (((1,), (1,)), ((), ())), preferred_element_type=jnp.float32)
    scores = (ratio / MARKERS) * raw_scores
    sample_terms = jnp.dot(scores.astype(jnp.bfloat16), genotypes, preferred_element_type=jnp.float32)
    image = start_dir / weights + sample_terms
    curvature = jnp.sum(start_dir * image, axis=1)
    alpha = (start_norm / curvature)[:, None]
    solution = alpha * start_dir
    residual = panel - alpha * image
    precond = residual / diag
    new_norm = jnp.sum(residual * precond, axis=1)
    direction = precond + (new_norm / start_norm)[:, None] * start_dir
    weighted = (weights * solution).astype(jnp.bfloat16)
    var_scores = lax.dot_general(weighted, variants, (((1,), (1,)), ((), ())), preferred_element_type=jnp.float32)
    positions = jnp.arange(VAR_DEV, dtype=jnp.int32)

    def one_block(index):
        offset = (index * VAR_DEV).astype(jnp.int32)
        block = lax.dynamic_slice_in_dim(variants, offset, VAR_DEV, 0)
        scaled = (block * weights).astype(jnp.bfloat16)
        cross = lax.dot_general(scaled, block, (((1,), (1,)), ((), ())), preferred_element_type=jnp.float32)
        local_scores = lax.dynamic_slice_in_dim(var_scores, offset, VAR_DEV, 1)
        correction = jnp.dot(local_scores.T, local_scores, precision=lax.Precision.HIGHEST)
        ends = jnp.cumsum(gene_sizes[index], dtype=jnp.int32)
        gene_index = jnp.sum((ends[None, :] <= positions[:, None]).astype(jnp.int32), axis=1)
        same_gene = gene_index[:, None] == gene_index[None, :]
        return jnp.where(same_gene, (cross - correction) / NSAMP, jnp.zeros_like(cross))

    gene_gram = lax.map(one_block, jnp.arange(N_MARK, dtype=jnp.int32))
    return solution, residual, direction, gene_gram
```

```python
import functools

import jax
import jax.numpy as jnp
from jax import lax
from jax.experimental import pallas as pl
from jax.experimental.pallas import tpu as pltpu
from jax.sharding import PartitionSpec as P

GENE_MAX = 400
LANES = 128
F32 = jnp.float32
BF16 = jnp.bfloat16
VMEM = pltpu.VMEM
NT = (((1,), (1,)), ((), ()))


def up(value, step):
    return -(-value // step) * step


def stages_of(count):
    found, stride = [], 1
    while stride < count:
        radix = 4 if count // stride % 4 == 0 else 2
        found.append((radix, stride))
        stride *= radix
    return found


def offsets_of(stages):
    found = [0]
    for radix, stride in stages:
        found = [base ^ (digit * stride) for base in found for digit in range(radix)]
    return found


def swap(array, count, offset, axis="samp"):
    return lax.ppermute(array, axis, [(i, i ^ offset) for i in range(count)])


def start_dir_of(ratio_ref, weights_ref, panel_ref):
    diag = 1.0 / weights_ref[...] + ratio_ref[0]
    return diag, panel_ref[...] / diag


def chunk_start(chunk, width, total):
    return pl.multiple_of(jnp.minimum(chunk * width, total - width), 16)


def fresh_lanes(chunk, width, total, rows):
    lane = lax.broadcasted_iota(jnp.int32, (rows, width), 1)
    return lane + jnp.minimum(chunk * width, total - width) >= chunk * width


def scores_kernel(width, total, count, ids, quarter, ratio, weights, panel, geno, variants, out, dir_bf):
    step = pl.program_id(0)
    steps = pl.num_programs(0)

    @pl.when(step == 0)
    def _():
        _, start_dir = start_dir_of(ratio, weights, panel)
        dir_bf[...] = start_dir.astype(BF16)
        weighted = (weights[...] * start_dir).astype(BF16)
        out[:, ids.shape[0] * width :] = lax.dot_general(
            weighted, variants[...], NT, preferred_element_type=F32
        )

    chunk = ids[step]
    part = lax.dot_general(dir_bf[...], geno[...], NT, preferred_element_type=F32)
    part = jnp.where(fresh_lanes(chunk, width, total, part.shape[0]), part, 0.0)
    at = pl.multiple_of(step * width, LANES)
    out[:, pl.ds(at, width)] = part

    @pl.when(chunk == count - 1)
    def _():
        _, start_dir = start_dir_of(ratio, weights, panel)
        norm = jnp.sum(panel[...] * start_dir, axis=1, keepdims=True)
        own = jnp.sum(start_dir * (start_dir / weights[...]), axis=1, keepdims=True)
        lane = lax.broadcasted_iota(jnp.int32, (part.shape[0], LANES), 1)
        head = part[:, :LANES]
        head = jnp.where(lane == 0, norm, jnp.where(lane == 1, own, head))
        out[:, pl.ds(at, LANES)] = head


def scores_call(ids, quarter, ratio, weights, panel, geno, variants, width, count, share):
    total, samples = geno.shape
    rows = panel.shape[0]
    chunks = ids.shape[0]
    return pl.pallas_call(
        functools.partial(scores_kernel, width, total, count),
        out_shape=jax.ShapeDtypeStruct((rows, chunks * width + share), F32),
        grid_spec=pltpu.PrefetchScalarGridSpec(
            num_scalar_prefetch=2,
            grid=(chunks,),
            in_specs=[
                pl.BlockSpec(memory_space=pltpu.SMEM),
                pl.BlockSpec((1, samples), lambda j, ids, q: (0, 0)),
                pl.BlockSpec((rows, samples), lambda j, ids, q: (0, 0)),
                pl.BlockSpec(
                    (pl.Element(width), pl.Element(samples)),
                    lambda j, ids, q: (chunk_start(ids[j], width, total), 0),
                ),
                pl.BlockSpec((share, samples), lambda j, ids, q: (q[0], 0)),
            ],
            out_specs=pl.BlockSpec(memory_space=VMEM),
            scratch_shapes=[VMEM((rows, samples), BF16)],
        ),
        name="scores",
    )(ids, quarter, ratio, weights, panel, geno, variants)


def terms_kernel(width, total, count, markers, ids, ratio, scores, geno, before, out):
    step = pl.program_id(0)
    samples = geno.shape[1]

    @pl.when(step == 0)
    def _():
        out[...] = before[...]

    chunk = ids[step]
    raw = scores[:, pl.ds(pl.multiple_of(step * width, LANES), width)]
    fresh = fresh_lanes(chunk, width, total, raw.shape[0])
    scaled = jnp.where(fresh, (ratio[0] / markers) * raw, 0.0)
    out[:, :samples] += jnp.dot(scaled.astype(BF16), geno[...], preferred_element_type=F32)
    square = jnp.sum(scaled * raw, axis=1, keepdims=True)
    lane = lax.broadcasted_iota(jnp.int32, (raw.shape[0], LANES), 1)
    stats = jnp.where((lane < 2) & (chunk == count - 1), raw[:, :LANES], 0.0)
    out[:, samples:] += jnp.where(lane == 2, square, stats)


def terms_call(ids, ratio, scores, geno, before, width, count, markers):
    total, samples = geno.shape
    rows = scores.shape[0]
    chunks = ids.shape[0]
    return pl.pallas_call(
        functools.partial(terms_kernel, width, total, count, markers),
        out_shape=jax.ShapeDtypeStruct((rows, samples + LANES), F32),
        grid_spec=pltpu.PrefetchScalarGridSpec(
            num_scalar_prefetch=1,
            grid=(chunks,),
            in_specs=[
                pl.BlockSpec(memory_space=pltpu.SMEM),
                pl.BlockSpec(memory_space=VMEM),
                pl.BlockSpec(
                    (pl.Element(width), pl.Element(samples)),
                    lambda j, ids: (chunk_start(ids[j], width, total), 0),
                ),
                pl.BlockSpec(memory_space=VMEM),
            ],
            out_specs=pl.BlockSpec(memory_space=VMEM),
        ),
        name="terms",
    )(ids, ratio, scores, geno, before)


def update_kernel(ratio, weights, panel, own, other, solution, residual, norm, alpha_out):
    samples = panel.shape[1]
    diag, start_dir = start_dir_of(ratio, weights, panel)
    total = own[...] + other[...]
    terms = total[:, :samples]
    start_norm = own[:, samples : samples + 1]
    curvature = own[:, samples + 1 : samples + 2] + total[:, samples + 2 : samples + 3]
    alpha = start_norm / curvature
    image = start_dir / weights[...] + terms
    left = panel[...] - alpha * image
    solution[...] = alpha * start_dir
    residual[...] = left
    norm[...] = jnp.broadcast_to(jnp.sum(left * (left / diag), axis=1, keepdims=True), norm.shape)
    alpha_out[...] = jnp.broadcast_to(alpha, alpha_out.shape)


def direction_kernel(ratio, weights, panel, own, residual, norm, out):
    samples = panel.shape[1]
    diag, start_dir = start_dir_of(ratio, weights, panel)
    start_norm = own[:, samples : samples + 1]
    out[...] = residual[...] / diag + (norm[:, :1] / start_norm) * start_dir


def genes_of(sizes, index):
    gene = jnp.zeros(index.shape, jnp.int32)
    end = jnp.int32(0)
    for g in range(sizes.shape[1]):
        end = end + sizes[0, g]
        gene = gene + (end <= index).astype(jnp.int32)
    return gene


def cross_kernel(block, span, ids, sizes, weights, variants, *outs):
    count = variants.shape[0]
    cols = genes_of(sizes, lax.broadcasted_iota(jnp.int32, (1, count), 1))
    per = ids.shape[0] // len(outs)
    row = lax.broadcasted_iota(jnp.int32, (block, LANES), 0)
    for at, out in enumerate(outs):
        for j in range(per):
            first = pl.multiple_of(ids[at * per + j] * block, block)
            mine = variants[pl.ds(first, block), :]
            scaled = (mine.astype(F32) * weights[...]).astype(BF16)
            cross = lax.dot_general(scaled, variants[...], NT, preferred_element_type=F32)
            rows = genes_of(sizes, first + row)[:, :1]
            cross = jnp.where(rows == cols, cross, 0.0)
            folded = cross[:, :span]
            for low in range(span, count, span):
                folded = folded + cross[:, low : low + span]
            out[j * block : (j + 1) * block, :] = folded


def gram_kernel(samples, where, sizes, alpha, *refs):
    *parts, out, full = refs
    shares, sums = parts[: where.shape[0] - 1], parts[where.shape[0] - 1 :]
    count = out.shape[2]
    block = out.shape[1]
    share = shares[0].shape[1]
    for at, ref in enumerate(shares):
        place = pl.multiple_of(where[1 + at] * share, LANES)
        full[:, pl.ds(place, share)] = ref[...] * alpha[:, :1]
    cross = sums[0][...]
    for ref in sums[1:]:
        cross = cross + ref[...]
    first = where[0] * block
    window = max(block, LANES)
    base = pl.multiple_of(first // window * window, window)
    wide = lax.dot_general(
        full[:, pl.ds(base, window)],
        full[...],
        (((0,), (0,)), ((), ())),
        precision=lax.Precision.HIGHEST,
        preferred_element_type=F32,
    )
    correction = wide[:block]
    for step in range(1, window // block):
        correction = jnp.where(first - base == step * block, wide[step * block : (step + 1) * block], correction)
    cols = genes_of(sizes, lax.broadcasted_iota(jnp.int32, (1, count), 1))
    rows = genes_of(sizes, first + lax.broadcasted_iota(jnp.int32, (block, LANES), 0))[:, :1]
    span = cross.shape[1]
    for low in range(0, count, span):
        piece = (cross - correction[:, low : low + span]) / samples
        out[0, :, low : low + span] = jnp.where(rows == cols[:, low : low + span], piece, 0.0)


def body(genotypes, variants, weights, variance_ratio, panel, gene_sizes):
    count = lax.axis_size("samp")
    marks = lax.axis_size("mark")
    me = lax.axis_index("samp").astype(jnp.int32)
    stages = stages_of(count)
    (radix, stride), later = stages[0], stages[1:]
    firsts = [digit * stride for digit in range(radix)]
    rest = offsets_of(later)
    ids = [me ^ jnp.array([first ^ r for r in rest], jnp.int32) for first in firsts]
    quarters = [(me // stride % radix ^ d).reshape(1).astype(jnp.int32) for d in range(radix)]

    local, samples = genotypes.shape
    markers = local * marks
    width = up(-(-local // count), LANES)
    if count * width - local < 2:
        width += LANES
    num_variants = variants.shape[0]
    share = num_variants // radix
    row_weights = weights.reshape(1, samples)
    rows = panel.shape[0]

    sent = {}
    for d in (*range(radix - 1, 0, -1), 0):
        sent[d] = scores_call(
            ids[d], quarters[d], variance_ratio, row_weights, panel, genotypes, variants, width, count, share
        )
    got = sent[0]
    for d in range(1, radix):
        got = got + swap(sent[d], count, firsts[d])
    shared, got = got[:, -share:], got[:, :-share]
    for r, s in later:
        wide = got.shape[1] // r
        pieces = [jnp.concatenate([got[:, d * wide : (d + 1) * wide], shared], axis=1) for d in range(r)]
        total = pieces[0]
        for d in range(1, r):
            total = total + swap(pieces[d], count, d * s)
        got, shared = total[:, :wide], total[:, wide:]
    for r, s in reversed(later):
        got = jnp.concatenate([got] + [swap(got, count, d * s) for d in range(1, r)], axis=1)
    everything = jnp.concatenate([got, shared], axis=1)
    arrays = [everything] + [swap(everything, count, first) for first in firsts[1:]]

    block = num_variants // count
    span = up(GENE_MAX, LANES)
    if num_variants % span or num_variants <= span:
        span = num_variants
    crosses = pl.pallas_call(
        functools.partial(cross_kernel, block, span),
        out_shape=[jax.ShapeDtypeStruct((block * len(rest), span), F32)] * radix,
        in_specs=[pl.BlockSpec(memory_space=pltpu.SMEM)] * 2 + [pl.BlockSpec(memory_space=VMEM)] * 2,
        out_specs=[pl.BlockSpec(memory_space=VMEM)] * radix,
        name="cross",
    )(jnp.concatenate(ids), gene_sizes, row_weights, variants)
    held = crosses[0]
    for d in range(1, radix):
        held = held + swap(crosses[d], count, firsts[d])
    sums = [held]
    for r, s in later:
        held = sums[0]
        for other in sums[1:]:
            held = held + other
        tall = held.shape[0] // r
        sums = [held[:tall]] + [swap(held[d * tall : (d + 1) * tall], count, d * s) for d in range(1, r)]

    own = jnp.zeros((rows, samples + LANES), F32)
    for d in range(radix):
        own = terms_call(ids[d], variance_ratio, arrays[d], genotypes, own, width, count, markers)
    assert marks & (marks - 1) == 0
    other = None
    held = own
    offset = 1
    while offset < marks:
        other = swap(held, marks, offset, "mark")
        offset *= 2
        if offset < marks:
            stats = held[:, samples : samples + 2]
            held = held + other
            held = jnp.concatenate([held[:, :samples], stats, held[:, samples + 2 :]], axis=1)
    vmem = pl.BlockSpec(memory_space=VMEM)
    smem = pl.BlockSpec(memory_space=pltpu.SMEM)
    wide = jax.ShapeDtypeStruct((rows, LANES), F32)
    full = jax.ShapeDtypeStruct((rows, samples), F32)
    solution, residual, norm, alpha = pl.pallas_call(
        update_kernel,
        out_shape=[full, full, wide, wide],
        in_specs=[smem] + [vmem] * 4,
        out_specs=[vmem] * 4,
        name="update",
    )(variance_ratio, row_weights, panel, held, other)
    for r, s in stages:
        total = norm
        for d in range(1, r):
            total = total + swap(norm, count, d * s)
        norm = total
    direction = pl.pallas_call(
        direction_kernel,
        out_shape=full,
        in_specs=[smem] + [vmem] * 5,
        out_specs=vmem,
        name="direction",
    )(variance_ratio, row_weights, panel, held, residual, norm)

    shares = [array[:, -share:] for array in arrays]
    gram = pl.pallas_call(
        functools.partial(gram_kernel, samples * count),
        out_shape=jax.ShapeDtypeStruct((1, block, num_variants), F32),
        in_specs=[smem] * 2 + [vmem] * (1 + len(shares) + len(sums)),
        out_specs=vmem,
        scratch_shapes=[VMEM((rows, num_variants), F32)],
        name="gram",
    )(jnp.concatenate([me.reshape(1)] + quarters), gene_sizes, alpha, *shares, *sums)
    return solution, residual, direction, gram


def solution(mesh):
    return jax.shard_map(
        body,
        mesh=mesh,
        in_specs=(
            P("mark", "samp"),
            P("mark", "samp"),
            P("samp"),
            P(),
            P(None, "samp"),
            P("mark", None),
        ),
        out_specs=(P(None, "samp"), P(None, "samp"), P(None, "samp"), P("mark", "samp", None)),
        check_vma=False,
    )
```

```python
import dataclasses
import functools

import jax
import jax.numpy as jnp
from jax import lax
from jax.experimental import pallas as pl
from jax.experimental.pallas import tpu as pltpu
from jax.sharding import PartitionSpec as P


GENE_MAX = 400
LANES = 128
F32 = jnp.float32
BF16 = jnp.bfloat16
VMEM = pltpu.VMEM
NT = (((1,), (1,)), ((), ()))


def up(value, step):
    return -(-value // step) * step


def stages_of(count):
    found, stride = [], 1
    while stride < count:
        radix = 4 if count // stride % 4 == 0 else 2
        found.append((radix, stride))
        stride *= radix
    return found


def offsets_of(stages):
    found = [0]
    for radix, stride in stages:
        found = [base ^ (digit * stride) for base in found for digit in range(radix)]
    return found


def swap(array, count, offset, axis="samp"):
    return lax.ppermute(array, axis, [(i, i ^ offset) for i in range(count)])


def chunk_start(chunk, width, total):
    return pl.multiple_of(jnp.minimum(chunk * width, total - width), 16)


def fresh_lanes(chunk, width, total, rows):
    lane = lax.broadcasted_iota(jnp.int32, (rows, width), 1)
    return lane + jnp.minimum(chunk * width, total - width) >= chunk * width


def in_vmem(array):
    return pltpu.with_memory_space_constraint(array, pltpu.VMEM)


def fetch(copies):
    for copy in copies:
        copy.start()
    return copies


def geno_copies(plan, chunks, geno, held, sems):
    width, total = plan.width, plan.total
    return [
        pltpu.make_async_copy(
            geno.at[pl.ds(chunk_start(chunk, width, total), width), :],
            held.at[pl.ds(j * width, width), :],
            sems.at[j],
        )
        for j, chunk in enumerate(chunks)
    ]


def scores_body(plan, digit, me, ready, geno, variants, out, held, rows_held, sems):
    width, total = plan.width, plan.total
    chunks = [me ^ (digit * plan.stride) ^ r for r in plan.rest]
    copies = fetch(geno_copies(plan, chunks, geno, held, sems))
    share = rows_held.shape[0]
    quarter = (me // plan.stride % plan.radix) ^ digit
    rows_copy = pltpu.make_async_copy(
        variants.at[pl.ds(pl.multiple_of(quarter * share, 16), share), :], rows_held, sems.at[len(chunks)]
    )
    rows_copy.start()
    start_bf, weighted, stats = ready()
    for j, copy in enumerate(copies):
        copy.wait()
        part = lax.dot_general(
            start_bf, held[j * width : (j + 1) * width, :], NT, preferred_element_type=F32
        )
        part = jnp.where(fresh_lanes(chunks[j], width, total, part.shape[0]), part, 0.0)
        out[:, j * width : (j + 1) * width] = part
        lane = lax.broadcasted_iota(jnp.int32, stats.shape, 1)
        head = jnp.where((lane < 2) & (chunks[j] == plan.count - 1), stats, part[:, :LANES])
        out[:, j * width : j * width + LANES] = head
    rows_copy.wait()
    both = lax.dot_general(weighted, rows_held[...], NT, preferred_element_type=F32)
    high = both.shape[0] // 2
    out[:, len(chunks) * width :] = both[:high] + both[high:]


def lead_kernel(plan, digit, ratio, weights, panel, geno, variants, out, diag, start, start_bf, weighted, stats, *scratch):
    held, rows_held, panel_held, weights_held, sems, small = scratch
    first = fetch(
        [
            pltpu.make_async_copy(panel, panel_held, small.at[0]),
            pltpu.make_async_copy(weights, weights_held, small.at[1]),
        ]
    )

    def ready():
        for copy in first:
            copy.wait()
        mu = weights_held[...].reshape(1, weights_held.shape[0])
        whole = 1.0 / mu + ratio[0]
        right = panel_held[...]
        way = right / whole
        diag[0:1, :] = whole
        diag[1:2, :] = mu
        start[...] = way
        start_bf[...] = way.astype(BF16)
        exact = mu * way
        high = exact.astype(BF16)
        weighted[...] = jnp.concatenate([high, (exact - high.astype(F32)).astype(BF16)], axis=0)
        norm = jnp.sum(right * way, axis=1, keepdims=True)
        own = jnp.sum(way * (way / mu), axis=1, keepdims=True)
        lane = lax.broadcasted_iota(jnp.int32, stats.shape, 1)
        stats[...] = jnp.where(lane == 0, norm, jnp.where(lane == 1, own, 0.0))
        return start_bf[...], weighted[...], stats[...]

    scores_body(plan, digit, lax.axis_index("samp"), ready, geno, variants, out, held, rows_held, sems)


def scores_kernel(plan, digit, start_bf, weighted, stats, geno, variants, out, held, rows_held, sems):
    scores_body(
        plan,
        digit,
        lax.axis_index("samp"),
        lambda: (start_bf[...], weighted[...], stats[...]),
        geno,
        variants,
        out,
        held,
        rows_held,
        sems,
    )


def terms_kernel(plan, digit, ratio, scores, *refs):
    *before, geno, out, held, sems = refs
    width, total = plan.width, plan.total
    me = lax.axis_index("samp")
    samples = geno.shape[1]
    chunks = [me ^ (digit * plan.stride) ^ r for r in plan.rest]
    copies = fetch(geno_copies(plan, chunks, geno, held, sems))
    scale = ratio[0] / plan.markers
    terms = before[0][:, :samples] if before else jnp.zeros((out.shape[0], samples), F32)
    stats = before[0][:, samples:] if before else jnp.zeros((out.shape[0], LANES), F32)
    lane = lax.broadcasted_iota(jnp.int32, stats.shape, 1)
    for j, copy in enumerate(copies):
        raw = scores[:, j * width : (j + 1) * width]
        fresh = fresh_lanes(chunks[j], width, total, raw.shape[0])
        scaled = jnp.where(fresh, scale * raw, 0.0)
        square = jnp.sum(scaled * raw, axis=1, keepdims=True)
        stats = stats + jnp.where(lane == 2, square, jnp.where((lane < 2) & (chunks[j] == plan.count - 1), raw[:, :LANES], 0.0))
        copy.wait()
        terms = terms + jnp.dot(
            scaled.astype(BF16), held[j * width : (j + 1) * width, :], preferred_element_type=F32
        )
    out[:, :samples] = terms
    out[:, samples:] = stats


def update_kernel(diag, start, panel, own, other, solution, residual, norm, alpha_out):
    samples = start.shape[1]
    total = own[...] + other[...]
    start_norm = own[:, samples : samples + 1]
    curvature = own[:, samples + 1 : samples + 2] + total[:, samples + 2 : samples + 3]
    alpha = start_norm / curvature
    image = start[...] / diag[1:2, :] + total[:, :samples]
    left = panel[...] - alpha * image
    solution[...] = alpha * start[...]
    residual[...] = left
    norm[...] = jnp.broadcast_to(jnp.sum(left * (left / diag[0:1, :]), axis=1, keepdims=True), norm.shape)
    alpha_out[...] = jnp.broadcast_to(alpha, alpha_out.shape)


def direction_kernel(diag, start, own, residual, *refs):
    *norms, out = refs
    samples = start.shape[1]
    total = norms[0][:, :1]
    for ref in norms[1:]:
        total = total + ref[:, :1]
    start_norm = own[:, samples : samples + 1]
    out[...] = residual[...] / diag[0:1, :] + (total / start_norm) * start[...]


def genes_of(sizes, index):
    gene = jnp.zeros(index.shape, jnp.int32)
    end = jnp.int32(0)
    for g in range(sizes.shape[1]):
        end = end + sizes[0, g]
        gene = gene + (end <= index).astype(jnp.int32)
    return gene


def cross_kernel(plan, block, span, sizes, weights, variants, *refs):
    *outs, scaled = refs
    me = lax.axis_index("samp")
    count = variants.shape[0]
    mu = weights[...].reshape(1, weights.shape[0])
    cols = genes_of(sizes, lax.broadcasted_iota(jnp.int32, (1, count), 1))
    row = lax.broadcasted_iota(jnp.int32, (block, LANES), 0)
    for digit, out in enumerate(outs):
        places = []
        for j, r in enumerate(plan.rest):
            first = pl.multiple_of((me ^ (digit * plan.stride) ^ r) * block, block)
            mine = variants[pl.ds(first, block), :]
            scaled[j * block : (j + 1) * block, :] = (mine.astype(F32) * mu).astype(BF16)
            places.append(first + row)
        cross = lax.dot_general(scaled[...], variants[...], NT, preferred_element_type=F32)
        rows = genes_of(sizes, jnp.concatenate(places, axis=0))[:, :1]
        cross = jnp.where(rows == cols, cross, 0.0)
        folded = cross[:, :span]
        for low in range(span, count, span):
            folded = folded + cross[:, low : low + span]
        out[...] = folded


def gram_kernel(plan, samples, sizes, alpha, *refs):
    *parts, out, full = refs
    arrays, sums = parts[: plan.radix], parts[plan.radix :]
    me = lax.axis_index("samp")
    count = out.shape[2]
    block = out.shape[1]
    share = count // plan.radix
    for digit, ref in enumerate(arrays):
        quarter = (me // plan.stride % plan.radix) ^ digit
        full[:, pl.ds(pl.multiple_of(quarter * share, LANES), share)] = ref[:, -share:] * alpha[:, :1]
    cross = sums[0][...]
    for ref in sums[1:]:
        cross = cross + ref[...]
    first = me * block
    window = max(block, LANES)
    base = pl.multiple_of(first // window * window, window)
    wide = lax.dot_general(
        full[:, pl.ds(base, window)],
        full[...],
        (((0,), (0,)), ((), ())),
        precision=lax.Precision.HIGHEST,
        preferred_element_type=F32,
    )
    correction = wide[:block]
    for step in range(1, window // block):
        correction = jnp.where(first - base == step * block, wide[step * block : (step + 1) * block], correction)
    cols = genes_of(sizes, lax.broadcasted_iota(jnp.int32, (1, count), 1))
    rows = genes_of(sizes, first + lax.broadcasted_iota(jnp.int32, (block, LANES), 0))[:, :1]
    span = cross.shape[1]
    for low in range(0, count, span):
        piece = (cross - correction[:, low : low + span]) / samples
        out[0, :, low : low + span] = jnp.where(rows == cols[:, low : low + span], piece, 0.0)


@dataclasses.dataclass(frozen=True)
class Plan:
    count: int
    radix: int
    stride: int
    rest: tuple
    width: int
    total: int
    markers: int


def tied(array, *others):
    return lax.optimization_barrier((array, *others))[0]


def body(genotypes, variants, weights, variance_ratio, panel, gene_sizes):
    count = lax.axis_size("samp")
    marks = lax.axis_size("mark")
    stages = stages_of(count)
    (radix, stride), later = stages[0], stages[1:]
    firsts = [digit * stride for digit in range(radix)]
    rest = offsets_of(later)
    local, samples = genotypes.shape
    width = up(-(-local // count), LANES)
    if count * width - local < 2:
        width += LANES
    plan = Plan(count, radix, stride, tuple(rest), width, local, local * marks)
    num_variants = variants.shape[0]
    share = num_variants // radix
    rows = panel.shape[0]
    vmem = pl.BlockSpec(memory_space=VMEM)
    smem = pl.BlockSpec(memory_space=pltpu.SMEM)
    hbm = pl.BlockSpec(memory_space=pl.ANY)
    columns = len(rest) * width
    window = VMEM((columns, samples), BF16)
    sems = pltpu.SemaphoreType.DMA((len(rest) + 1,))
    rows_held = VMEM((share, samples), BF16)
    payload = VMEM((rows, columns + share), F32)

    lead = radix - 1
    sent = {}
    sent[lead], diag, start, start_bf, weighted, stats = pl.pallas_call(
        functools.partial(lead_kernel, plan, lead),
        out_shape=[
            payload,
            VMEM((8, samples), F32),
            VMEM((rows, samples), F32),
            VMEM((rows, samples), BF16),
            VMEM((2 * rows, samples), BF16),
            VMEM((rows, LANES), F32),
        ],
        in_specs=[smem] + [hbm] * 4,
        out_specs=[vmem] * 6,
        scratch_shapes=[
            window,
            rows_held,
            VMEM((rows, samples), F32),
            VMEM((samples,), F32),
            sems,
            pltpu.SemaphoreType.DMA((2,)),
        ],
        name="scores_lead",
    )(variance_ratio, weights, panel, genotypes, variants)
    diag, start = in_vmem(diag), in_vmem(start)
    after = sent[lead]
    for d in (*range(1, lead), 0):
        start_bf, after = lax.optimization_barrier((start_bf, after))
        sent[d] = pl.pallas_call(
            functools.partial(scores_kernel, plan, d),
            out_shape=payload,
            in_specs=[vmem] * 3 + [hbm] * 2,
            out_specs=vmem,
            scratch_shapes=[window, rows_held, sems],
            name="scores",
        )(in_vmem(start_bf), in_vmem(weighted), in_vmem(stats), genotypes, variants)
        after = sent[d]

    block = num_variants // count
    span = up(GENE_MAX, LANES)
    if num_variants % span or num_variants <= span:
        span = num_variants
    crosses = list(
        pl.pallas_call(
            functools.partial(cross_kernel, plan, block, span),
            out_shape=[jax.ShapeDtypeStruct((block * len(rest), span), F32)] * radix,
            in_specs=[smem] + [vmem] * 2,
            out_specs=[vmem] * radix,
            scratch_shapes=[VMEM((block * len(rest), samples), BF16)],
            name="cross",
        )(gene_sizes, weights, tied(variants, sent[0]))
    )

    got = sent[0]
    for d in range(1, radix):
        got = got + swap(sent[d], count, firsts[d])
    got, crosses[0] = lax.optimization_barrier((got, crosses[0]))
    near = [swap(tied(crosses[d], got), count, firsts[d]) for d in range(1, lead)]
    shared, got = got[:, -share:], got[:, :-share]
    for r, s in later:
        wide = got.shape[1] // r
        pieces = [jnp.concatenate([got[:, d * wide : (d + 1) * wide], shared], axis=1) for d in range(r)]
        total = pieces[0]
        for d in range(1, r):
            total = total + swap(pieces[d], count, d * s)
        got, shared = total[:, :wide], total[:, wide:]
    for r, s in reversed(later):
        got = jnp.concatenate([got] + [swap(got, count, d * s) for d in range(1, r)], axis=1)
    everything = jnp.concatenate([got, shared], axis=1)
    arrays = [in_vmem(everything)] + [in_vmem(swap(everything, count, firsts[d])) for d in range(1, radix)]

    own = ()
    for d in range(radix):
        whole = pl.pallas_call(
            functools.partial(terms_kernel, plan, d),
            out_shape=VMEM((rows, samples + LANES), F32),
            in_specs=[smem, vmem] + [vmem] * len(own) + [hbm],
            out_specs=vmem,
            scratch_shapes=[window, sems],
            name="terms",
        )(variance_ratio, arrays[d], *map(in_vmem, own), genotypes)
        own = (whole,)
    (held,) = own
    assert marks & (marks - 1) == 0
    other = None
    offset = 1
    while offset < marks:
        other = swap(held, marks, offset, "mark")
        offset *= 2
        if offset < marks:
            kept = held[:, samples : samples + 2]
            held = held + other
            held = jnp.concatenate([held[:, :samples], kept, held[:, samples + 2 :]], axis=1)
    held = in_vmem(held)
    flat = VMEM((rows, LANES), F32)
    full = jax.ShapeDtypeStruct((rows, samples), F32)
    solution, residual, norm, alpha = pl.pallas_call(
        update_kernel,
        out_shape=[VMEM((rows, samples), F32)] * 2 + [flat] * 2,
        in_specs=[vmem] * 5,
        out_specs=[vmem] * 4,
        name="update",
    )(diag, start, panel, held, in_vmem(other))
    norms = [norm]
    for r, s in stages:
        total = norms[0]
        for one in norms[1:]:
            total = total + one
        norms = [total] + [swap(total, count, d * s) for d in range(1, r)]
    direction = pl.pallas_call(
        direction_kernel,
        out_shape=full,
        in_specs=[vmem] * (4 + len(norms)),
        out_specs=vmem,
        name="direction",
    )(diag, start, held, in_vmem(residual), *map(in_vmem, norms))

    far = swap(crosses[lead], count, firsts[lead])
    sums = [crosses[0], *near, far]
    for r, s in later:
        total = sums[0]
        for one in sums[1:]:
            total = total + one
        tall = total.shape[0] // r
        sums = [total[:tall]] + [swap(total[d * tall : (d + 1) * tall], count, d * s) for d in range(1, r)]
    gram = pl.pallas_call(
        functools.partial(gram_kernel, plan, samples * count),
        out_shape=jax.ShapeDtypeStruct((1, block, num_variants), F32),
        in_specs=[smem] + [vmem] * (1 + radix + len(sums)),
        out_specs=vmem,
        scratch_shapes=[VMEM((rows, num_variants), F32)],
        name="gram",
    )(gene_sizes, in_vmem(alpha), *arrays, *map(in_vmem, sums))
    return solution, residual, direction, gram


def solution(mesh):
    return jax.shard_map(
        body,
        mesh=mesh,
        in_specs=(
            P("mark", "samp"),
            P("mark", "samp"),
            P("samp"),
            P(),
            P(None, "samp"),
            P("mark", None),
        ),
        out_specs=(P(None, "samp"), P(None, "samp"), P(None, "samp"), P("mark", "samp", None)),
        check_vma=False,
    )
```

```python
import dataclasses
import functools

import jax
import jax.numpy as jnp
from jax import lax
from jax.experimental import pallas as pl
from jax.experimental.pallas import tpu as pltpu
from jax.sharding import PartitionSpec as P


GENE_MAX = 400
LANES = 128
F32 = jnp.float32
BF16 = jnp.bfloat16
VMEM = pltpu.VMEM
NT = (((1,), (1,)), ((), ()))


def up(value, step):
    return -(-value // step) * step


def stages_of(count):
    found, stride = [], 1
    while stride < count:
        radix = 4 if count // stride % 4 == 0 else 2
        found.append((radix, stride))
        stride *= radix
    return found


def offsets_of(stages):
    found = [0]
    for radix, stride in stages:
        found = [base ^ (digit * stride) for base in found for digit in range(radix)]
    return found


def swap(array, count, offset, axis="samp"):
    return lax.ppermute(array, axis, [(i, i ^ offset) for i in range(count)])


def chunk_start(chunk, width, total):
    return pl.multiple_of(jnp.minimum(chunk * width, total - width), 16)


def fresh_lanes(chunk, width, total, rows):
    lane = lax.broadcasted_iota(jnp.int32, (rows, width), 1)
    return lane + jnp.minimum(chunk * width, total - width) >= chunk * width


def in_vmem(array):
    return pltpu.with_memory_space_constraint(array, pltpu.VMEM)


def fetch(copies):
    for copy in copies:
        copy.start()
    return copies


def geno_copies(plan, chunks, geno, held, sems, base=0):
    width, total = plan.width, plan.total
    return [
        pltpu.make_async_copy(
            geno.at[pl.ds(chunk_start(chunk, width, total), width), :],
            held.at[pl.ds(j * width, width), :],
            sems.at[base + j],
        )
        for j, chunk in enumerate(chunks)
    ]


def scores_begin(plan, digits, me, geno, variants, held, rows_held, sems):
    begun, per = [], len(plan.rest) + 1
    share = rows_held.shape[0] // len(digits)
    columns = held.shape[0] // len(digits)
    for at, digit in enumerate(digits):
        chunks = [me ^ (digit * plan.stride) ^ r for r in plan.rest]
        window = held.at[pl.ds(at * columns, columns), :]
        copies = geno_copies(plan, chunks, geno, window, sems, at * per)
        quarter = (me // plan.stride % plan.radix) ^ digit
        rows_copy = pltpu.make_async_copy(
            variants.at[pl.ds(pl.multiple_of(quarter * share, 16), share), :],
            rows_held.at[pl.ds(at * share, share), :],
            sems.at[at * per + len(chunks)],
        )
        begun.append((chunks, fetch([*copies, rows_copy])))
    return begun


def scores_finish(plan, begun, start_bf, weighted, stats, held, rows_held, outs):
    width, total = plan.width, plan.total
    share = rows_held.shape[0] // len(outs)
    for at, ((chunks, (*copies, rows_copy)), out) in enumerate(zip(begun, outs)):
        for j, copy in enumerate(copies):
            copy.wait()
            low = (at * len(chunks) + j) * width
            part = lax.dot_general(start_bf, held[low : low + width, :], NT, preferred_element_type=F32)
            part = jnp.where(fresh_lanes(chunks[j], width, total, part.shape[0]), part, 0.0)
            out[:, j * width : (j + 1) * width] = part
            lane = lax.broadcasted_iota(jnp.int32, stats.shape, 1)
            head = jnp.where((lane < 2) & (chunks[j] == plan.count - 1), stats, part[:, :LANES])
            out[:, j * width : j * width + LANES] = head
        rows_copy.wait()
        both = lax.dot_general(
            weighted, rows_held[at * share : (at + 1) * share, :], NT, preferred_element_type=F32
        )
        high = both.shape[0] // 2
        out[:, len(chunks) * width :] = both[:high] + both[high:]


def lead_kernel(plan, digit, ratio, weights, panel, geno, variants, out, diag, start, start_bf, weighted, stats, *scratch):
    held, rows_held, panel_held, weights_held, sems, small = scratch
    first = fetch(
        [
            pltpu.make_async_copy(panel, panel_held, small.at[0]),
            pltpu.make_async_copy(weights, weights_held, small.at[1]),
        ]
    )
    begun = scores_begin(plan, (digit,), lax.axis_index("samp"), geno, variants, held, rows_held, sems)
    for copy in first:
        copy.wait()
    mu = weights_held[...].reshape(1, weights_held.shape[0])
    whole = 1.0 / mu + ratio[0]
    right = panel_held[...]
    way = right / whole
    diag[0:1, :] = whole
    diag[1:2, :] = mu
    start[...] = way
    start_bf[...] = way.astype(BF16)
    exact = mu * way
    high = exact.astype(BF16)
    weighted[...] = jnp.concatenate([high, (exact - high.astype(F32)).astype(BF16)], axis=0)
    norm = jnp.sum(right * way, axis=1, keepdims=True)
    own = jnp.sum(way * (way / mu), axis=1, keepdims=True)
    lane = lax.broadcasted_iota(jnp.int32, stats.shape, 1)
    stats[...] = jnp.where(lane == 0, norm, jnp.where(lane == 1, own, 0.0))
    scores_finish(plan, begun, start_bf[...], weighted[...], stats[...], held, rows_held, (out,))


def scores_kernel(plan, digits, start_bf, weighted, stats, geno, variants, *refs):
    *outs, held, rows_held, sems = refs
    begun = scores_begin(plan, digits, lax.axis_index("samp"), geno, variants, held, rows_held, sems)
    scores_finish(plan, begun, start_bf[...], weighted[...], stats[...], held, rows_held, outs)


def terms_kernel(plan, digit, ratio, scores, *refs):
    *before, geno, out, held, sems = refs
    width, total = plan.width, plan.total
    me = lax.axis_index("samp")
    samples = geno.shape[1]
    chunks = [me ^ (digit * plan.stride) ^ r for r in plan.rest]
    copies = fetch(geno_copies(plan, chunks, geno, held, sems))
    scale = ratio[0] / plan.markers
    terms = before[0][:, :samples] if before else jnp.zeros((out.shape[0], samples), F32)
    stats = before[0][:, samples:] if before else jnp.zeros((out.shape[0], LANES), F32)
    lane = lax.broadcasted_iota(jnp.int32, stats.shape, 1)
    for j, copy in enumerate(copies):
        raw = scores[:, j * width : (j + 1) * width]
        fresh = fresh_lanes(chunks[j], width, total, raw.shape[0])
        scaled = jnp.where(fresh, scale * raw, 0.0)
        square = jnp.sum(scaled * raw, axis=1, keepdims=True)
        stats = stats + jnp.where(lane == 2, square, jnp.where((lane < 2) & (chunks[j] == plan.count - 1), raw[:, :LANES], 0.0))
        copy.wait()
        terms = terms + jnp.dot(
            scaled.astype(BF16), held[j * width : (j + 1) * width, :], preferred_element_type=F32
        )
    out[:, :samples] = terms
    out[:, samples:] = stats


def update_kernel(diag, start, panel, own, other, solution, residual, norm, alpha_out):
    samples = start.shape[1]
    total = own[...] + other[...]
    start_norm = own[:, samples : samples + 1]
    curvature = own[:, samples + 1 : samples + 2] + total[:, samples + 2 : samples + 3]
    alpha = start_norm / curvature
    image = start[...] / diag[1:2, :] + total[:, :samples]
    left = panel[...] - alpha * image
    solution[...] = alpha * start[...]
    residual[...] = left
    norm[...] = jnp.broadcast_to(jnp.sum(left * (left / diag[0:1, :]), axis=1, keepdims=True), norm.shape)
    alpha_out[...] = jnp.broadcast_to(alpha, alpha_out.shape)


def direction_kernel(diag, start, own, residual, *refs):
    *norms, out = refs
    samples = start.shape[1]
    total = norms[0][:, :1]
    for ref in norms[1:]:
        total = total + ref[:, :1]
    start_norm = own[:, samples : samples + 1]
    out[...] = residual[...] / diag[0:1, :] + (total / start_norm) * start[...]


def gene_bounds(sizes, index, count):
    low = jnp.zeros(index.shape, jnp.int32)
    high = jnp.full(index.shape, count, jnp.int32)
    end = jnp.int32(0)
    for g in range(sizes.shape[1]):
        end = end + sizes[0, g]
        low = jnp.where(end <= index, end, low)
        high = jnp.where((end > index) & (end < high), end, high)
    return low, high


def cross_kernel(plan, block, sizes, weights, variants, *refs):
    *outs, scaled = refs
    keep_x, keep_y, send_x, send_y = outs
    me = lax.axis_index("samp")
    count = variants.shape[0]
    half = GENE_MAX // 2
    quarter = block * len(plan.rest)
    mu = weights[...].reshape(1, weights.shape[0])
    lane = lax.broadcasted_iota(jnp.int32, (1, quarter), 1)
    column = lax.broadcasted_iota(jnp.int32, (count, quarter), 0)
    places = (
        ((keep_x, 0), (keep_y, 0)),
        ((send_x, 0), (keep_y, 1)),
        ((keep_x, 1), (send_y, 0)),
        ((send_x, 1), (send_y, 1)),
    )
    for digit in range(plan.radix):
        index = lane
        for j, r in enumerate(plan.rest):
            first = pl.multiple_of((me ^ (digit * plan.stride) ^ r) * block, block)
            mine = variants[pl.ds(first, block), :]
            scaled[j * block : (j + 1) * block, :] = (mine.astype(F32) * mu).astype(BF16)
            index = jnp.where(lane // block == j, first + lane - j * block, index)
        cross = lax.dot_general(variants[...], scaled[...], NT, preferred_element_type=F32)
        low, high = gene_bounds(sizes, index, count)
        cross = jnp.where((column >= low) & (column < high), cross, 0.0)
        for part, (out, at) in enumerate(places[digit]):
            folded = None
            for base in range(part * half, count, GENE_MAX):
                piece = cross[base : min(base + half, count)]
                if piece.shape[0] < half:
                    piece = jnp.concatenate([piece, jnp.zeros((half - piece.shape[0], quarter), F32)], axis=0)
                folded = piece if folded is None else folded + piece
            out[:, at * quarter : (at + 1) * quarter] = folded


def halves_kernel(keep_x, keep_y, got_x, got_y, own_x, own_y, pass_x, pass_y):
    quarter = own_x.shape[1]
    own_x[...] = keep_x[:, :quarter] + got_x[:, :quarter]
    own_y[...] = keep_y[:, :quarter] + got_y[:, :quarter]
    pass_x[...] = keep_x[:, quarter:] + got_x[:, quarter:]
    pass_y[...] = keep_y[:, quarter:] + got_y[:, quarter:]


def split_kernel(terms, *refs):
    ins, outs = refs[: -len(terms[1])], refs[-len(terms[1]) :]
    if terms[0]:
        low, high = ins[0][...] + ins[2][...], ins[1][...] + ins[3][...]
    else:
        total = ins[0][...]
        for ref in ins[1:]:
            total = total + ref[...]
        low, high = total[:, : total.shape[1] // 2], total[:, total.shape[1] // 2 :]
    wide = low.shape[1] // len(outs)
    for j, out in enumerate(outs):
        out[...] = jnp.concatenate(
            [low[:, j * wide : (j + 1) * wide], high[:, j * wide : (j + 1) * wide]], axis=1
        )


def gram_kernel(plan, samples, sizes, alpha, *refs):
    *parts, out, full = refs
    arrays, sums = parts[: plan.radix], parts[plan.radix :]
    me = lax.axis_index("samp")
    count = out.shape[2]
    block = out.shape[1]
    share = count // plan.radix
    for digit, ref in enumerate(arrays):
        quarter = (me // plan.stride % plan.radix) ^ digit
        full[:, pl.ds(pl.multiple_of(quarter * share, LANES), share)] = ref[:, -share:] * alpha[:, :1]
    cross = sums[0][...]
    for ref in sums[1:]:
        cross = cross + ref[...]
    cross = jnp.concatenate([cross[:, :block], cross[:, block:]], axis=0).T
    cross = jnp.concatenate([cross] * (-(-count // GENE_MAX)), axis=1)[:, :count]
    first = me * block
    window = max(block, LANES)
    base = pl.multiple_of(first // window * window, window)
    wide = lax.dot_general(
        full[:, pl.ds(base, window)],
        full[...],
        (((0,), (0,)), ((), ())),
        precision=lax.Precision.HIGHEST,
        preferred_element_type=F32,
    )
    correction = wide[:block]
    for step in range(1, window // block):
        correction = jnp.where(first - base == step * block, wide[step * block : (step + 1) * block], correction)
    low, high = gene_bounds(sizes, first + lax.broadcasted_iota(jnp.int32, (block, LANES), 0), count)
    column = lax.broadcasted_iota(jnp.int32, (block, count), 1)
    same = (column >= low[:, :1]) & (column < high[:, :1])
    out[0] = jnp.where(same, (cross - correction) / samples, 0.0)


@dataclasses.dataclass(frozen=True)
class Plan:
    count: int
    radix: int
    stride: int
    rest: tuple
    width: int
    total: int
    markers: int


def tied(array, *others):
    return lax.optimization_barrier((array, *others))[0]


def body(genotypes, variants, weights, variance_ratio, panel, gene_sizes):
    count = lax.axis_size("samp")
    marks = lax.axis_size("mark")
    stages = stages_of(count)
    (radix, stride), later = stages[0], stages[1:]
    firsts = [digit * stride for digit in range(radix)]
    rest = offsets_of(later)
    local, samples = genotypes.shape
    width = up(-(-local // count), LANES)
    if count * width - local < 2:
        width += LANES
    plan = Plan(count, radix, stride, tuple(rest), width, local, local * marks)
    num_variants = variants.shape[0]
    share = num_variants // radix
    rows = panel.shape[0]
    vmem = pl.BlockSpec(memory_space=VMEM)
    smem = pl.BlockSpec(memory_space=pltpu.SMEM)
    hbm = pl.BlockSpec(memory_space=pl.ANY)
    columns = len(rest) * width
    window = VMEM((columns, samples), BF16)
    sems = pltpu.SemaphoreType.DMA((len(rest) + 1,))
    payload = VMEM((rows, columns + share), F32)

    lead = radix - 1
    sent = {}
    sent[lead], diag, start, start_bf, weighted, stats = pl.pallas_call(
        functools.partial(lead_kernel, plan, lead),
        out_shape=[
            payload,
            VMEM((8, samples), F32),
            VMEM((rows, samples), F32),
            VMEM((rows, samples), BF16),
            VMEM((2 * rows, samples), BF16),
            VMEM((rows, LANES), F32),
        ],
        in_specs=[smem] + [hbm] * 4,
        out_specs=[vmem] * 6,
        scratch_shapes=[
            VMEM((columns, samples), BF16),
            VMEM((share, samples), BF16),
            VMEM((rows, samples), F32),
            VMEM((samples,), F32),
            sems,
            pltpu.SemaphoreType.DMA((2,)),
        ],
        name="scores_lead",
    )(variance_ratio, weights, panel, genotypes, variants)
    diag, start = in_vmem(diag), in_vmem(start)
    after = sent[lead]
    for digits in (tuple(range(1, lead)), (0,)):
        start_bf, after = lax.optimization_barrier((start_bf, after))
        found = pl.pallas_call(
            functools.partial(scores_kernel, plan, digits),
            out_shape=[payload] * len(digits),
            in_specs=[vmem] * 3 + [hbm] * 2,
            out_specs=[vmem] * len(digits),
            scratch_shapes=[
                VMEM((len(digits) * columns, samples), BF16),
                VMEM((len(digits) * share, samples), BF16),
                pltpu.SemaphoreType.DMA((len(digits) * (len(rest) + 1),)),
            ],
            name="scores",
        )(in_vmem(start_bf), in_vmem(weighted), in_vmem(stats), genotypes, variants)
        sent.update(zip(digits, found))
        after = found[0]

    assert radix == 4
    block = num_variants // count
    quarter = block * len(rest)
    half = GENE_MAX // 2
    keep_x, keep_y, send_x, send_y = pl.pallas_call(
        functools.partial(cross_kernel, plan, block),
        out_shape=[VMEM((half, 2 * quarter), F32)] * radix,
        in_specs=[smem] + [vmem] * 2,
        out_specs=[vmem] * radix,
        scratch_shapes=[VMEM((quarter, samples), BF16)],
        name="cross",
    )(gene_sizes, weights, tied(variants, sent[0]))

    got = sent[0]
    for d in range(1, radix):
        got = got + swap(sent[d], count, firsts[d])
    got, send_x, send_y = lax.optimization_barrier((got, send_x, send_y))
    got_x = swap(send_x, count, firsts[1])
    got_y = swap(send_y, count, firsts[2])
    piece = VMEM((half, quarter), F32)
    own_x, own_y, pass_x, pass_y = pl.pallas_call(
        halves_kernel, out_shape=[piece] * 4, in_specs=[vmem] * 4, out_specs=[vmem] * 4, name="halves"
    )(*map(in_vmem, (keep_x, keep_y, got_x, got_y)))
    sums = [own_x, own_y, swap(pass_x, count, firsts[2]), swap(pass_y, count, firsts[1])]
    paired, wide = True, quarter
    for r, s in later:
        wide //= r
        pieces = pl.pallas_call(
            functools.partial(split_kernel, (paired, range(r))),
            out_shape=[VMEM((half, 2 * wide), F32)] * r,
            in_specs=[vmem] * len(sums),
            out_specs=[vmem] * r,
            name="split",
        )(*map(in_vmem, sums))
        paired = False
        sums = [pieces[0]] + [swap(pieces[d], count, d * s) for d in range(1, r)]

    shared, got = got[:, -share:], got[:, :-share]
    for r, s in later:
        wide = got.shape[1] // r
        pieces = [jnp.concatenate([got[:, d * wide : (d + 1) * wide], shared], axis=1) for d in range(r)]
        total = pieces[0]
        for d in range(1, r):
            total = total + swap(pieces[d], count, d * s)
        got, shared = total[:, :wide], total[:, wide:]
    for r, s in reversed(later):
        got = jnp.concatenate([got] + [swap(got, count, d * s) for d in range(1, r)], axis=1)
    everything = jnp.concatenate([got, shared], axis=1)
    arrays = [in_vmem(everything)] + [in_vmem(swap(everything, count, firsts[d])) for d in range(1, radix)]

    own = ()
    for d in (0, 1, 3, 2):
        whole = pl.pallas_call(
            functools.partial(terms_kernel, plan, d),
            out_shape=VMEM((rows, samples + LANES), F32),
            in_specs=[smem, vmem] + [vmem] * len(own) + [hbm],
            out_specs=vmem,
            scratch_shapes=[window, sems],
            name="terms",
        )(variance_ratio, arrays[d], *map(in_vmem, own), genotypes)
        own = (whole,)
    (held,) = own
    assert marks & (marks - 1) == 0
    other = None
    offset = 1
    while offset < marks:
        other = swap(held, marks, offset, "mark")
        offset *= 2
        if offset < marks:
            kept = held[:, samples : samples + 2]
            held = held + other
            held = jnp.concatenate([held[:, :samples], kept, held[:, samples + 2 :]], axis=1)
    held = in_vmem(held)
    flat = VMEM((rows, LANES), F32)
    full = jax.ShapeDtypeStruct((rows, samples), F32)
    solution, residual, norm, alpha = pl.pallas_call(
        update_kernel,
        out_shape=[VMEM((rows, samples), F32)] * 2 + [flat] * 2,
        in_specs=[vmem] * 5,
        out_specs=[vmem] * 4,
        name="update",
    )(diag, start, panel, held, in_vmem(other))
    norms = [norm]
    for r, s in stages:
        total = norms[0]
        for one in norms[1:]:
            total = total + one
        norms = [total] + [swap(total, count, d * s) for d in range(1, r)]
    direction = pl.pallas_call(
        direction_kernel,
        out_shape=full,
        in_specs=[vmem] * (4 + len(norms)),
        out_specs=vmem,
        name="direction",
    )(diag, start, held, in_vmem(residual), *map(in_vmem, norms))

    gram = pl.pallas_call(
        functools.partial(gram_kernel, plan, samples * count),
        out_shape=jax.ShapeDtypeStruct((1, block, num_variants), F32),
        in_specs=[smem] + [vmem] * (1 + radix + len(sums)),
        out_specs=vmem,
        scratch_shapes=[VMEM((rows, num_variants), F32)],
        name="gram",
    )(gene_sizes, in_vmem(alpha), *arrays, *map(in_vmem, sums))
    return solution, residual, direction, gram


def solution(mesh):
    return jax.shard_map(
        body,
        mesh=mesh,
        in_specs=(
            P("mark", "samp"),
            P("mark", "samp"),
            P("samp"),
            P(),
            P(None, "samp"),
            P("mark", None),
        ),
        out_specs=(P(None, "samp"), P(None, "samp"), P(None, "samp"), P("mark", "samp", None)),
        check_vma=False,
    )
```

```python
import dataclasses
import functools

import jax
import jax.numpy as jnp
from jax import lax
from jax.experimental import pallas as pl
from jax.experimental.pallas import tpu as pltpu
from jax.sharding import PartitionSpec as P


GENE_MAX = 400
LANES = 128
F32 = jnp.float32
BF16 = jnp.bfloat16
VMEM = pltpu.VMEM
NT = (((1,), (1,)), ((), ()))


def up(value, step):
    return -(-value // step) * step


def stages_of(count):
    found, stride = [], 1
    while stride < count:
        radix = 4 if count // stride % 4 == 0 else 2
        found.append((radix, stride))
        stride *= radix
    return found


def offsets_of(stages):
    found = [0]
    for radix, stride in stages:
        found = [base ^ (digit * stride) for base in found for digit in range(radix)]
    return found


def swap(array, count, offset, axis="samp"):
    return lax.ppermute(array, axis, [(i, i ^ offset) for i in range(count)])


def chunk_start(chunk, width, total):
    return pl.multiple_of(jnp.minimum(chunk * width, total - width), 16)


def fresh_lanes(chunk, width, total, rows):
    lane = lax.broadcasted_iota(jnp.int32, (rows, width), 1)
    return lane + jnp.minimum(chunk * width, total - width) >= chunk * width


def in_vmem(array):
    return pltpu.with_memory_space_constraint(array, pltpu.VMEM)


def fetch(copies):
    for copy in copies:
        copy.start()
    return copies


def geno_copies(plan, chunks, geno, held, sems, base=0):
    width, total = plan.width, plan.total
    return [
        pltpu.make_async_copy(
            geno.at[pl.ds(chunk_start(chunk, width, total), width), :],
            held.at[pl.ds(j * width, width), :],
            sems.at[base + j],
        )
        for j, chunk in enumerate(chunks)
    ]


def scores_begin(plan, digits, me, geno, variants, held, rows_held, sems):
    begun, per = [], len(plan.rest) + 1
    share = rows_held.shape[0] // len(digits)
    columns = held.shape[0] // len(digits)
    for at, digit in enumerate(digits):
        chunks = [me ^ (digit * plan.stride) ^ r for r in plan.rest]
        window = held.at[pl.ds(at * columns, columns), :]
        copies = geno_copies(plan, chunks, geno, window, sems, at * per)
        quarter = (me // plan.stride % plan.radix) ^ digit
        rows_copy = pltpu.make_async_copy(
            variants.at[pl.ds(pl.multiple_of(quarter * share, 16), share), :],
            rows_held.at[pl.ds(at * share, share), :],
            sems.at[at * per + len(chunks)],
        )
        begun.append((chunks, fetch([*copies, rows_copy])))
    return begun


def scores_finish(plan, begun, start_bf, weighted, stats, held, rows_held, outs):
    width, total = plan.width, plan.total
    share = rows_held.shape[0] // len(outs)
    for at, ((chunks, (*copies, rows_copy)), out) in enumerate(zip(begun, outs)):
        for j, copy in enumerate(copies):
            copy.wait()
            low = (at * len(chunks) + j) * width
            part = lax.dot_general(start_bf, held[low : low + width, :], NT, preferred_element_type=F32)
            part = jnp.where(fresh_lanes(chunks[j], width, total, part.shape[0]), part, 0.0)
            out[:, j * width : (j + 1) * width] = part
            lane = lax.broadcasted_iota(jnp.int32, stats.shape, 1)
            head = jnp.where((lane < 2) & (chunks[j] == plan.count - 1), stats, part[:, :LANES])
            out[:, j * width : j * width + LANES] = head
        rows_copy.wait()
        both = lax.dot_general(
            weighted, rows_held[at * share : (at + 1) * share, :], NT, preferred_element_type=F32
        )
        high = both.shape[0] // 2
        out[:, len(chunks) * width :] = both[:high] + both[high:]


def lead_kernel(plan, digit, ratio, weights, panel, geno, variants, out, diag, start, start_bf, weighted, stats, *scratch):
    held, rows_held, panel_held, weights_held, sems, small = scratch
    first = fetch(
        [
            pltpu.make_async_copy(panel, panel_held, small.at[0]),
            pltpu.make_async_copy(weights, weights_held, small.at[1]),
        ]
    )
    begun = scores_begin(plan, (digit,), lax.axis_index("samp"), geno, variants, held, rows_held, sems)
    for copy in first:
        copy.wait()
    mu = weights_held[...].reshape(1, weights_held.shape[0])
    whole = 1.0 / mu + ratio[0]
    right = panel_held[...]
    way = right / whole
    diag[0:1, :] = whole
    diag[1:2, :] = mu
    start[...] = way
    start_bf[...] = way.astype(BF16)
    exact = mu * way
    high = exact.astype(BF16)
    weighted[...] = jnp.concatenate([high, (exact - high.astype(F32)).astype(BF16)], axis=0)
    norm = jnp.sum(right * way, axis=1, keepdims=True)
    own = jnp.sum(way * (way / mu), axis=1, keepdims=True)
    lane = lax.broadcasted_iota(jnp.int32, stats.shape, 1)
    stats[...] = jnp.where(lane == 0, norm, jnp.where(lane == 1, own, 0.0))
    scores_finish(plan, begun, start_bf[...], weighted[...], stats[...], held, rows_held, (out,))


def scores_kernel(plan, digits, start_bf, weighted, stats, geno, variants, *refs):
    *outs, held, rows_held, sems = refs
    begun = scores_begin(plan, digits, lax.axis_index("samp"), geno, variants, held, rows_held, sems)
    scores_finish(plan, begun, start_bf[...], weighted[...], stats[...], held, rows_held, outs)


def terms_kernel(plan, digit, ratio, scores, *refs):
    *before, geno, out, held, sems = refs
    width, total = plan.width, plan.total
    me = lax.axis_index("samp")
    samples = geno.shape[1]
    chunks = [me ^ (digit * plan.stride) ^ r for r in plan.rest]
    copies = fetch(geno_copies(plan, chunks, geno, held, sems))
    scale = ratio[0] / plan.markers
    terms = before[0][:, :samples] if before else jnp.zeros((out.shape[0], samples), F32)
    stats = before[0][:, samples:] if before else jnp.zeros((out.shape[0], LANES), F32)
    lane = lax.broadcasted_iota(jnp.int32, stats.shape, 1)
    for j, copy in enumerate(copies):
        raw = scores[:, j * width : (j + 1) * width]
        fresh = fresh_lanes(chunks[j], width, total, raw.shape[0])
        scaled = jnp.where(fresh, scale * raw, 0.0)
        square = jnp.sum(scaled * raw, axis=1, keepdims=True)
        stats = stats + jnp.where(lane == 2, square, jnp.where((lane < 2) & (chunks[j] == plan.count - 1), raw[:, :LANES], 0.0))
        copy.wait()
        terms = terms + jnp.dot(
            scaled.astype(BF16), held[j * width : (j + 1) * width, :], preferred_element_type=F32
        )
    out[:, :samples] = terms
    out[:, samples:] = stats


def update_kernel(diag, start, panel, own, other, solution, residual, norm, alpha_out):
    samples = start.shape[1]
    total = own[...] + other[...]
    start_norm = own[:, samples : samples + 1]
    curvature = own[:, samples + 1 : samples + 2] + total[:, samples + 2 : samples + 3]
    alpha = start_norm / curvature
    image = start[...] / diag[1:2, :] + total[:, :samples]
    left = panel[...] - alpha * image
    solution[...] = alpha * start[...]
    residual[...] = left
    norm[...] = jnp.broadcast_to(jnp.sum(left * (left / diag[0:1, :]), axis=1, keepdims=True), norm.shape)
    alpha_out[...] = jnp.broadcast_to(alpha, alpha_out.shape)


def direction_kernel(diag, start, own, residual, *refs):
    *norms, out = refs
    samples = start.shape[1]
    total = norms[0][:, :1]
    for ref in norms[1:]:
        total = total + ref[:, :1]
    start_norm = own[:, samples : samples + 1]
    out[...] = residual[...] / diag[0:1, :] + (total / start_norm) * start[...]


def gene_bounds(sizes, index, count):
    low = jnp.zeros(index.shape, jnp.int32)
    high = jnp.full(index.shape, count, jnp.int32)
    end = jnp.int32(0)
    for g in range(sizes.shape[1]):
        end = end + sizes[0, g]
        low = jnp.where(end <= index, end, low)
        high = jnp.where((end > index) & (end < high), end, high)
    return low, high


def cross_kernel(plan, block, sizes, weights, variants, *refs):
    *outs, scaled = refs
    own_x, own_y, pass_x, pass_y, send_x, send_y = outs
    me = lax.axis_index("samp")
    count = variants.shape[0]
    half = GENE_MAX // 2
    quarter = block * len(plan.rest)
    mu = weights[...].reshape(1, weights.shape[0])
    lane = lax.broadcasted_iota(jnp.int32, (1, quarter), 1)
    column = lax.broadcasted_iota(jnp.int32, (count, quarter), 0)
    places = (
        ((own_x, 0), (own_y, 0)),
        ((send_x, 0), (pass_y, 0)),
        ((pass_x, 0), (send_y, 0)),
        ((send_x, 1), (send_y, 1)),
    )
    for digit in range(plan.radix):
        index = lane
        for j, r in enumerate(plan.rest):
            first = pl.multiple_of((me ^ (digit * plan.stride) ^ r) * block, block)
            mine = variants[pl.ds(first, block), :]
            scaled[j * block : (j + 1) * block, :] = (mine.astype(F32) * mu).astype(BF16)
            index = jnp.where(lane // block == j, first + lane - j * block, index)
        cross = lax.dot_general(variants[...], scaled[...], NT, preferred_element_type=F32)
        low, high = gene_bounds(sizes, index, count)
        cross = jnp.where((column >= low) & (column < high), cross, 0.0)
        for part, (out, at) in enumerate(places[digit]):
            folded = None
            for base in range(part * half, count, GENE_MAX):
                piece = cross[base : min(base + half, count)]
                if piece.shape[0] < half:
                    piece = jnp.concatenate([piece, jnp.zeros((half - piece.shape[0], quarter), F32)], axis=0)
                folded = piece if folded is None else folded + piece
            out[:, at * quarter : (at + 1) * quarter] = folded


def halves_kernel(got_x, got_y, *refs):
    before, after = refs[:4], refs[4:]
    quarter = before[0].shape[1]
    for at, (old, new) in enumerate(zip(before, after)):
        got = (got_x, got_y)[at % 2]
        low = at // 2 * quarter
        new[...] = old[...] + got[:, low : low + quarter]


def split_kernel(paired, keep, *refs):
    *terms, kept, sent = refs
    if paired:
        low, high = keep[...] + terms[1][...], terms[0][...] + terms[2][...]
    else:
        total = keep[...]
        for ref in terms:
            total = total + ref[...]
        low, high = total[:, : total.shape[1] // 2], total[:, total.shape[1] // 2 :]
    wide = low.shape[1] // 4
    cut = [part[:, j * wide : (j + 1) * wide] for j in range(4) for part in (low, high)]
    kept[...] = jnp.concatenate(cut[0:2] + cut[4:6], axis=1)
    sent[...] = jnp.concatenate(cut[2:4] + cut[6:8], axis=1)


def merge_kernel(wide, *refs):
    terms, outs = refs[:-4], refs[-4:]
    tail = slice(4 * wide, terms[0].shape[1])
    for place in [slice(j * wide, (j + 1) * wide) for j in range(4)] + [tail]:
        total = terms[0][:, place]
        for ref in terms[1:]:
            total = total + ref[:, place]
        if place is tail:
            for out in outs:
                out[:, wide:] = total
        else:
            outs[place.start // wide][:, :wide] = total


def gram_kernel(plan, samples, sizes, alpha, *refs):
    *parts, out, full = refs
    arrays, sums = parts[: plan.radix], parts[plan.radix :]
    me = lax.axis_index("samp")
    count = out.shape[2]
    block = out.shape[1]
    share = count // plan.radix
    for digit, ref in enumerate(arrays):
        quarter = (me // plan.stride % plan.radix) ^ digit
        full[:, pl.ds(pl.multiple_of(quarter * share, LANES), share)] = ref[:, -share:] * alpha[:, :1]
    cross = sums[0][...]
    for ref in sums[1:]:
        cross = cross + ref[...]
    cross = jnp.concatenate([cross[:, :block], cross[:, block:]], axis=0).T
    cross = jnp.concatenate([cross] * (-(-count // GENE_MAX)), axis=1)[:, :count]
    first = me * block
    window = max(block, LANES)
    base = pl.multiple_of(first // window * window, window)
    wide = lax.dot_general(
        full[:, pl.ds(base, window)],
        full[...],
        (((0,), (0,)), ((), ())),
        precision=lax.Precision.HIGHEST,
        preferred_element_type=F32,
    )
    correction = wide[:block]
    for step in range(1, window // block):
        correction = jnp.where(first - base == step * block, wide[step * block : (step + 1) * block], correction)
    low, high = gene_bounds(sizes, first + lax.broadcasted_iota(jnp.int32, (block, LANES), 0), count)
    column = lax.broadcasted_iota(jnp.int32, (block, count), 1)
    same = (column >= low[:, :1]) & (column < high[:, :1])
    out[0] = jnp.where(same, (cross - correction) / samples, 0.0)


@dataclasses.dataclass(frozen=True)
class Plan:
    count: int
    radix: int
    stride: int
    rest: tuple
    width: int
    total: int
    markers: int


def tied(array, *others):
    return lax.optimization_barrier((array, *others))[0]


def body(genotypes, variants, weights, variance_ratio, panel, gene_sizes):
    count = lax.axis_size("samp")
    marks = lax.axis_size("mark")
    stages = stages_of(count)
    (radix, stride), later = stages[0], stages[1:]
    firsts = [digit * stride for digit in range(radix)]
    rest = offsets_of(later)
    local, samples = genotypes.shape
    width = up(-(-local // count), LANES)
    if count * width - local < 2:
        width += LANES
    plan = Plan(count, radix, stride, tuple(rest), width, local, local * marks)
    num_variants = variants.shape[0]
    share = num_variants // radix
    rows = panel.shape[0]
    vmem = pl.BlockSpec(memory_space=VMEM)
    smem = pl.BlockSpec(memory_space=pltpu.SMEM)
    hbm = pl.BlockSpec(memory_space=pl.ANY)
    columns = len(rest) * width
    window = VMEM((columns, samples), BF16)
    sems = pltpu.SemaphoreType.DMA((len(rest) + 1,))
    payload = VMEM((rows, columns + share), F32)

    lead = radix - 1
    sent = {}
    sent[lead], diag, start, start_bf, weighted, stats = pl.pallas_call(
        functools.partial(lead_kernel, plan, lead),
        out_shape=[
            payload,
            VMEM((8, samples), F32),
            VMEM((rows, samples), F32),
            VMEM((rows, samples), BF16),
            VMEM((2 * rows, samples), BF16),
            VMEM((rows, LANES), F32),
        ],
        in_specs=[smem] + [hbm] * 4,
        out_specs=[vmem] * 6,
        scratch_shapes=[
            VMEM((columns, samples), BF16),
            VMEM((share, samples), BF16),
            VMEM((rows, samples), F32),
            VMEM((samples,), F32),
            sems,
            pltpu.SemaphoreType.DMA((2,)),
        ],
        name="scores_lead",
    )(variance_ratio, weights, panel, genotypes, variants)
    diag, start = in_vmem(diag), in_vmem(start)
    after = sent[lead]
    for digits in (tuple(range(1, lead)), (0,)):
        start_bf, after = lax.optimization_barrier((start_bf, after))
        found = pl.pallas_call(
            functools.partial(scores_kernel, plan, digits),
            out_shape=[payload] * len(digits),
            in_specs=[vmem] * 3 + [hbm] * 2,
            out_specs=[vmem] * len(digits),
            scratch_shapes=[
                VMEM((len(digits) * columns, samples), BF16),
                VMEM((len(digits) * share, samples), BF16),
                pltpu.SemaphoreType.DMA((len(digits) * (len(rest) + 1),)),
            ],
            name="scores",
        )(in_vmem(start_bf), in_vmem(weighted), in_vmem(stats), genotypes, variants)
        sent.update(zip(digits, found))
        after = found[0]

    assert radix == 4
    block = num_variants // count
    quarter = block * len(rest)
    half = GENE_MAX // 2
    *parts, send_x, send_y = pl.pallas_call(
        functools.partial(cross_kernel, plan, block),
        out_shape=[VMEM((half, quarter), F32)] * 4 + [VMEM((half, 2 * quarter), F32)] * 2,
        in_specs=[smem] + [vmem] * 2,
        out_specs=[vmem] * 6,
        scratch_shapes=[VMEM((quarter, samples), BF16)],
        name="cross",
    )(gene_sizes, weights, tied(variants, sent[0]))

    terms = [sent[0]] + [swap(sent[d], count, firsts[d]) for d in range(1, radix)]
    wide = columns
    assert all(r == 4 for r, _ in later)
    for level, (r, s) in enumerate(later):
        wide //= r
        pieces = pl.pallas_call(
            functools.partial(merge_kernel, wide),
            out_shape=[VMEM((rows, wide + share), F32)] * r,
            in_specs=[vmem] * len(terms),
            out_specs=[vmem] * r,
            name="merge",
        )(*map(in_vmem, terms))
        if level == 0:
            piece, send_x, send_y = lax.optimization_barrier((pieces[0], send_x, send_y))
        else:
            piece = pieces[0]
        terms = [piece] + [swap(pieces[d], count, d * s) for d in range(1, r)]
    total = terms[0]
    for one in terms[1:]:
        total = total + one
    got, shared = total[:, :wide], total[:, wide:]
    got_x = swap(send_x, count, firsts[1])
    got_y = swap(send_y, count, firsts[2])
    own_x, own_y, pass_x, pass_y = pl.pallas_call(
        halves_kernel,
        out_shape=[VMEM((half, quarter), F32)] * 4,
        in_specs=[vmem] * 6,
        out_specs=[vmem] * 4,
        input_output_aliases={2 + i: i for i in range(4)},
        name="halves",
    )(*map(in_vmem, (got_x, got_y, *parts)))
    sums = [own_x, own_y, swap(pass_x, count, firsts[2]), swap(pass_y, count, firsts[1])]
    wide = quarter
    for level, (r, s) in enumerate(later):
        wide //= r
        kept, moved = pl.pallas_call(
            functools.partial(split_kernel, level == 0),
            out_shape=[VMEM((half, 4 * wide), F32)] * 2,
            in_specs=[vmem] * len(sums),
            out_specs=[vmem] * 2,
            name="split",
        )(*map(in_vmem, sums))
        both = kept + swap(moved, count, s)
        sums = [both[:, : 2 * wide], swap(both[:, 2 * wide :], count, 2 * s)]

    for r, s in reversed(later):
        got = jnp.concatenate([got] + [swap(got, count, d * s) for d in range(1, r)], axis=1)
    everything = jnp.concatenate([got, shared], axis=1)
    arrays = [in_vmem(everything)] + [in_vmem(swap(everything, count, firsts[d])) for d in range(1, radix)]

    own = ()
    for d in range(radix):
        whole = pl.pallas_call(
            functools.partial(terms_kernel, plan, d),
            out_shape=VMEM((rows, samples + LANES), F32),
            in_specs=[smem, vmem] + [vmem] * len(own) + [hbm],
            out_specs=vmem,
            scratch_shapes=[window, sems],
            name="terms",
        )(variance_ratio, arrays[d], *map(in_vmem, own), genotypes)
        own = (whole,)
    (held,) = own
    assert marks & (marks - 1) == 0
    other = None
    offset = 1
    while offset < marks:
        other = swap(held, marks, offset, "mark")
        offset *= 2
        if offset < marks:
            kept = held[:, samples : samples + 2]
            held = held + other
            held = jnp.concatenate([held[:, :samples], kept, held[:, samples + 2 :]], axis=1)
    held = in_vmem(held)
    flat = VMEM((rows, LANES), F32)
    full = jax.ShapeDtypeStruct((rows, samples), F32)
    solution, residual, norm, alpha = pl.pallas_call(
        update_kernel,
        out_shape=[VMEM((rows, samples), F32)] * 2 + [flat] * 2,
        in_specs=[vmem] * 5,
        out_specs=[vmem] * 4,
        name="update",
    )(diag, start, panel, held, in_vmem(other))
    norms = [norm]
    for r, s in stages:
        total = norms[0]
        for one in norms[1:]:
            total = total + one
        norms = [total] + [swap(total, count, d * s) for d in range(1, r)]
    direction = pl.pallas_call(
        direction_kernel,
        out_shape=full,
        in_specs=[vmem] * (4 + len(norms)),
        out_specs=vmem,
        name="direction",
    )(diag, start, held, in_vmem(residual), *map(in_vmem, norms))

    gram = pl.pallas_call(
        functools.partial(gram_kernel, plan, samples * count),
        out_shape=jax.ShapeDtypeStruct((1, block, num_variants), F32),
        in_specs=[smem] + [vmem] * (1 + radix + len(sums)),
        out_specs=vmem,
        scratch_shapes=[VMEM((rows, num_variants), F32)],
        name="gram",
    )(gene_sizes, in_vmem(alpha), *arrays, *map(in_vmem, sums))
    return solution, residual, direction, gram


def solution(mesh):
    return jax.shard_map(
        body,
        mesh=mesh,
        in_specs=(
            P("mark", "samp"),
            P("mark", "samp"),
            P("samp"),
            P(),
            P(None, "samp"),
            P("mark", None),
        ),
        out_specs=(P(None, "samp"), P(None, "samp"), P(None, "samp"), P("mark", "samp", None)),
        check_vma=False,
    )
```

```python
import dataclasses
import functools

import jax
import jax.numpy as jnp
from jax import lax
from jax.experimental import pallas as pl
from jax.experimental.pallas import tpu as pltpu
from jax.sharding import PartitionSpec as P


GENE_MAX = 400
LANES = 128
F32 = jnp.float32
BF16 = jnp.bfloat16
VMEM = pltpu.VMEM
NT = (((1,), (1,)), ((), ()))


def up(value, step):
    return -(-value // step) * step


def stages_of(count):
    found, stride = [], 1
    while stride < count:
        radix = 4 if count // stride % 4 == 0 else 2
        found.append((radix, stride))
        stride *= radix
    return found


def offsets_of(stages):
    found = [0]
    for radix, stride in stages:
        found = [base ^ (digit * stride) for base in found for digit in range(radix)]
    return found


def swap(array, count, offset, axis="samp"):
    return lax.ppermute(array, axis, [(i, i ^ offset) for i in range(count)])


def chunk_start(chunk, width, total):
    return pl.multiple_of(jnp.minimum(chunk * width, total - width), 16)


def fresh_lanes(chunk, width, total, rows):
    lane = lax.broadcasted_iota(jnp.int32, (rows, width), 1)
    return lane + jnp.minimum(chunk * width, total - width) >= chunk * width


def in_vmem(array):
    return pltpu.with_memory_space_constraint(array, pltpu.VMEM)


def fetch(copies):
    for copy in copies:
        copy.start()
    return copies


def geno_copies(plan, chunks, geno, held, sems, base=0):
    width, total = plan.width, plan.total
    return [
        pltpu.make_async_copy(
            geno.at[pl.ds(chunk_start(chunk, width, total), width), :],
            held.at[pl.ds(j * width, width), :],
            sems.at[base + j],
        )
        for j, chunk in enumerate(chunks)
    ]


def scores_begin(plan, digits, me, geno, held, sems):
    begun, per = [], len(plan.rest)
    columns = held.shape[0] // len(digits)
    for at, digit in enumerate(digits):
        chunks = [me ^ (digit * plan.stride) ^ r for r in plan.rest]
        window = held.at[pl.ds(at * columns, columns), :]
        begun.append((chunks, fetch(geno_copies(plan, chunks, geno, window, sems, at * per))))
    return begun


def scores_finish(plan, begun, start_bf, stats, held, outs):
    width, total = plan.width, plan.total
    for at, ((chunks, copies), out) in enumerate(zip(begun, outs)):
        for j, copy in enumerate(copies):
            copy.wait()
            low = (at * len(chunks) + j) * width
            part = lax.dot_general(start_bf, held[low : low + width, :], NT, preferred_element_type=F32)
            part = jnp.where(fresh_lanes(chunks[j], width, total, part.shape[0]), part, 0.0)
            out[:, j * width : (j + 1) * width] = part
            lane = lax.broadcasted_iota(jnp.int32, stats.shape, 1)
            head = jnp.where((lane < 2) & (chunks[j] == plan.count - 1), stats, part[:, :LANES])
            out[:, j * width : j * width + LANES] = head


def lead_kernel(plan, digit, ratio, weights, panel, geno, out, diag, right, start, start_bf, weighted, stats, *scratch):
    held, weights_held, ratio_held, sems, small = scratch
    first = fetch(
        [
            pltpu.make_async_copy(panel, right, small.at[0]),
            pltpu.make_async_copy(weights, weights_held, small.at[1]),
            pltpu.make_async_copy(ratio, ratio_held, small.at[2]),
        ]
    )
    begun = scores_begin(plan, (digit,), lax.axis_index("samp"), geno, held, sems)
    for copy in first:
        copy.wait()
    mu = weights_held[...].reshape(1, weights_held.shape[0])
    whole = 1.0 / mu + ratio_held[0]
    way = right[...] / whole
    diag[0:1, :] = whole
    diag[1:2, :] = mu
    diag[2:3, :] = jnp.full(mu.shape, ratio_held[0], F32)
    start[...] = way
    start_bf[...] = way.astype(BF16)
    exact = mu * way
    high = exact.astype(BF16)
    weighted[...] = jnp.concatenate([high, (exact - high.astype(F32)).astype(BF16)], axis=0)
    norm = jnp.sum(right[...] * way, axis=1, keepdims=True)
    own = jnp.sum(way * (way / mu), axis=1, keepdims=True)
    lane = lax.broadcasted_iota(jnp.int32, stats.shape, 1)
    stats[...] = jnp.where(lane == 0, norm, jnp.where(lane == 1, own, 0.0))
    scores_finish(plan, begun, start_bf[...], stats[...], held, (out,))


def scores_kernel(plan, digits, start_bf, stats, geno, *refs):
    *outs, held, sems = refs
    begun = scores_begin(plan, digits, lax.axis_index("samp"), geno, held, sems)
    scores_finish(plan, begun, start_bf[...], stats[...], held, outs)


def terms_kernel(plan, digit, diag, scores, *refs):
    *before, geno, out, held, sems = refs
    width, total = plan.width, plan.total
    me = lax.axis_index("samp")
    samples = geno.shape[1]
    chunks = [me ^ (digit * plan.stride) ^ r for r in plan.rest]
    copies = fetch(geno_copies(plan, chunks, geno, held, sems))
    scale = diag[2:3, 0:1] / plan.markers
    terms = before[0][:, :samples] if before else jnp.zeros((out.shape[0], samples), F32)
    stats = before[0][:, samples:] if before else jnp.zeros((out.shape[0], LANES), F32)
    lane = lax.broadcasted_iota(jnp.int32, stats.shape, 1)
    for j, copy in enumerate(copies):
        raw = scores[:, j * width : (j + 1) * width]
        fresh = fresh_lanes(chunks[j], width, total, raw.shape[0])
        scaled = jnp.where(fresh, scale * raw, 0.0)
        square = jnp.sum(scaled * raw, axis=1, keepdims=True)
        stats = stats + jnp.where(lane == 2, square, jnp.where((lane < 2) & (chunks[j] == plan.count - 1), raw[:, :LANES], 0.0))
        copy.wait()
        terms = terms + jnp.dot(
            scaled.astype(BF16), held[j * width : (j + 1) * width, :], preferred_element_type=F32
        )
    out[:, :samples] = terms
    out[:, samples:] = stats


def update_kernel(diag, start, right, own, other, solution, residual, norm, alpha_out):
    samples = start.shape[1]
    total = own[...] + other[...]
    start_norm = own[:, samples : samples + 1]
    curvature = own[:, samples + 1 : samples + 2] + total[:, samples + 2 : samples + 3]
    alpha = start_norm / curvature
    image = start[...] / diag[1:2, :] + total[:, :samples]
    left = right[...] - alpha * image
    solution[...] = alpha * start[...]
    residual[...] = left
    norm[...] = jnp.broadcast_to(jnp.sum(left * (left / diag[0:1, :]), axis=1, keepdims=True), norm.shape)
    alpha_out[...] = jnp.broadcast_to(alpha, alpha_out.shape)


def direction_kernel(diag, start, own, residual, *refs):
    *norms, out = refs
    samples = start.shape[1]
    total = norms[0][:, :1]
    for ref in norms[1:]:
        total = total + ref[:, :1]
    start_norm = own[:, samples : samples + 1]
    out[...] = residual[...] / diag[0:1, :] + (total / start_norm) * start[...]


def gene_bounds(sizes, index, count):
    low = jnp.zeros(index.shape, jnp.int32)
    high = jnp.full(index.shape, count, jnp.int32)
    end = jnp.int32(0)
    for g in range(sizes.shape[1]):
        end = end + sizes[0, g]
        low = jnp.where(end <= index, end, low)
        high = jnp.where((end > index) & (end < high), end, high)
    return low, high


def cross_kernel(plan, block, sizes, weights, variants, weighted, *refs):
    *outs, scaled = refs
    own_x, own_y, pass_x, pass_y, send_x, send_y = outs
    me = lax.axis_index("samp")
    count = variants.shape[0]
    half = GENE_MAX // 2
    quarter = block * len(plan.rest)
    both = lax.dot_general(weighted[...], variants[...], NT, preferred_element_type=F32)
    rows = both.shape[0] // 2
    beta = both[:rows] + both[rows:]
    for at, (sent, kept) in enumerate(((send_x, pass_x), (send_y, pass_y))):
        sent[half:, :] = beta[:, 2 * at * quarter : 2 * (at + 1) * quarter]
        for j in range(2):
            low = (2 * at + j) * quarter
            kept[half + j * rows : half + (j + 1) * rows, :] = beta[:, low : low + quarter]
    mu = weights[...].reshape(1, weights.shape[0])
    lane = lax.broadcasted_iota(jnp.int32, (1, quarter), 1)
    column = lax.broadcasted_iota(jnp.int32, (count, quarter), 0)
    places = (
        ((own_x, 0), (own_y, 0)),
        ((send_x, 0), (pass_y, 0)),
        ((pass_x, 0), (send_y, 0)),
        ((send_x, 1), (send_y, 1)),
    )
    for digit in range(plan.radix):
        index = lane
        for j, r in enumerate(plan.rest):
            first = pl.multiple_of((me ^ (digit * plan.stride) ^ r) * block, block)
            mine = variants[pl.ds(first, block), :]
            scaled[j * block : (j + 1) * block, :] = (mine.astype(F32) * mu).astype(BF16)
            index = jnp.where(lane // block == j, first + lane - j * block, index)
        cross = lax.dot_general(variants[...], scaled[...], NT, preferred_element_type=F32)
        low, high = gene_bounds(sizes, index, count)
        cross = jnp.where((column >= low) & (column < high), cross, 0.0)
        for part, (out, at) in enumerate(places[digit]):
            folded = None
            for base in range(part * half, count, GENE_MAX):
                piece = cross[base : min(base + half, count)]
                if piece.shape[0] < half:
                    piece = jnp.concatenate([piece, jnp.zeros((half - piece.shape[0], quarter), F32)], axis=0)
                folded = piece if folded is None else folded + piece
            out[:half, at * quarter : (at + 1) * quarter] = folded


def halves_kernel(got_x, got_y, *refs):
    before, after = refs[:4], refs[4:]
    half, quarter = before[0].shape
    rows = got_x.shape[0] - half
    for at, (old, new) in enumerate(zip(before, after)):
        got = (got_x, got_y)[at % 2]
        low = at // 2 * quarter
        new[:half, :] = old[:half, :] + got[:half, low : low + quarter]
        if at >= 2:
            for j in range(2):
                to = slice(half + j * rows, half + (j + 1) * rows)
                new[to, :] = old[to, :] + got[half:, j * quarter : (j + 1) * quarter]


def split_kernel(own_x, own_y, pass_x, pass_y, got_x, got_y, kept, sent):
    half, quarter = own_x.shape
    low, high = own_x[...] + got_x[:half, :], own_y[...] + got_y[:half, :]
    wide = quarter // 4
    cut = [part[:, j * wide : (j + 1) * wide] for j in range(4) for part in (low, high)]
    kept[:half, :] = jnp.concatenate(cut[0:2] + cut[4:6], axis=1)
    sent[:half, :] = jnp.concatenate(cut[2:4] + cut[6:8], axis=1)
    tall = pass_x.shape[0] - half
    for at, (mine, got) in enumerate(((pass_x, got_x), (pass_y, got_y))):
        beta = mine[half:, :] + got[half:, :]
        for out in (kept, sent):
            out[half + at * tall : half + (at + 1) * tall, :] = beta


def pair_kernel(half, kept, got, stay, sent):
    wide = kept.shape[1] // 2
    tall = kept.shape[0] - half
    total = kept[...] + got[...]
    stay[:half, :] = total[:half, :wide]
    sent[:half, :] = total[:half, wide:]
    for out in (stay, sent):
        for j in range(2):
            out[half + j * tall : half + (j + 1) * tall, :] = total[half:, j * wide : (j + 1) * wide]


def gram_kernel(samples, sizes, alpha, *refs):
    *sums, solved, left, out, solved_out, left_out, full, sems = refs
    copies = fetch(
        [
            pltpu.make_async_copy(solved, solved_out, sems.at[0]),
            pltpu.make_async_copy(left, left_out, sems.at[1]),
        ]
    )
    me = lax.axis_index("samp")
    count = out.shape[2]
    block = out.shape[1]
    half = GENE_MAX // 2
    rows = full.shape[0]
    total = sums[0][...]
    for ref in sums[1:]:
        total = total + ref[...]
    parts = count // LANES
    for j in range(parts):
        low = half + (j % 2 * (parts // 2) + j // 2) * rows
        full[:, j * LANES : (j + 1) * LANES] = total[low : low + rows, :] * alpha[:, :1]
    cross = jnp.concatenate([total[:half, :block], total[:half, block : 2 * block]], axis=0).T
    cross = jnp.concatenate([cross] * (-(-count // GENE_MAX)), axis=1)[:, :count]
    first = me * block
    window = max(block, LANES)
    base = pl.multiple_of(first // window * window, window)
    wide = lax.dot_general(
        full[:, pl.ds(base, window)],
        full[...],
        (((0,), (0,)), ((), ())),
        precision=lax.Precision.HIGHEST,
        preferred_element_type=F32,
    )
    correction = wide[:block]
    for step in range(1, window // block):
        correction = jnp.where(first - base == step * block, wide[step * block : (step + 1) * block], correction)
    low, high = gene_bounds(sizes, first + lax.broadcasted_iota(jnp.int32, (block, LANES), 0), count)
    column = lax.broadcasted_iota(jnp.int32, (block, count), 1)
    same = (column >= low[:, :1]) & (column < high[:, :1])
    out[0] = jnp.where(same, (cross - correction) / samples, 0.0)
    for copy in copies:
        copy.wait()


def cut_by(products, scores, count, stride):
    wide = products.shape[1] // 8
    low, high = products[:, : 4 * wide], products[:, 4 * wide :]
    cut = [jnp.concatenate([p[:, j * wide : (j + 1) * wide] for p in (low, high)], axis=1) for j in range(4)]
    kept = jnp.concatenate([cut[0], cut[2]], axis=1)
    kept = kept + swap(jnp.concatenate([cut[1], cut[3]], axis=1), count, stride)
    scores = scores + swap(scores, count, stride)
    products = kept[:, : 2 * wide] + swap(kept[:, 2 * wide :], count, 2 * stride)
    return products, scores + swap(scores, count, 2 * stride)


def merge_kernel(*refs):
    terms, outs = refs[:-4], refs[-4:]
    wide = outs[0].shape[1]
    for j, out in enumerate(outs):
        total = terms[0][:, j * wide : (j + 1) * wide]
        for ref in terms[1:]:
            total = total + ref[:, j * wide : (j + 1) * wide]
        out[...] = total


@dataclasses.dataclass(frozen=True)
class Plan:
    count: int
    radix: int
    stride: int
    rest: tuple
    width: int
    total: int
    markers: int


def tied(array, *others):
    return lax.optimization_barrier((array, *others))[0]


def body(genotypes, variants, weights, variance_ratio, panel, gene_sizes):
    count = lax.axis_size("samp")
    marks = lax.axis_size("mark")
    stages = stages_of(count)
    (radix, stride), later = stages[0], stages[1:]
    firsts = [digit * stride for digit in range(radix)]
    rest = offsets_of(later)
    local, samples = genotypes.shape
    width = up(-(-local // count), LANES)
    if count * width - local < 2:
        width += LANES
    plan = Plan(count, radix, stride, tuple(rest), width, local, local * marks)
    num_variants = variants.shape[0]
    rows = panel.shape[0]
    vmem = pl.BlockSpec(memory_space=VMEM)
    smem = pl.BlockSpec(memory_space=pltpu.SMEM)
    hbm = pl.BlockSpec(memory_space=pl.ANY)
    columns = len(rest) * width
    payload = VMEM((rows, columns), F32)

    lead = radix - 1
    sent = {}
    sent[lead], diag, right, start, start_bf, weighted, stats = pl.pallas_call(
        functools.partial(lead_kernel, plan, lead),
        out_shape=[
            payload,
            VMEM((8, samples), F32),
            VMEM((rows, samples), F32),
            VMEM((rows, samples), F32),
            VMEM((rows, samples), BF16),
            VMEM((2 * rows, samples), BF16),
            VMEM((rows, LANES), F32),
        ],
        in_specs=[hbm] * 4,
        out_specs=[vmem] * 7,
        scratch_shapes=[
            VMEM((columns, samples), BF16),
            VMEM((samples,), F32),
            pltpu.SMEM((1,), F32),
            pltpu.SemaphoreType.DMA((len(rest),)),
            pltpu.SemaphoreType.DMA((3,)),
        ],
        name="scores_lead",
    )(variance_ratio, weights, panel, genotypes)
    diag, right, start = in_vmem(diag), in_vmem(right), in_vmem(start)
    after = sent[lead]
    for digits in (tuple(range(1, lead)), (0,)):
        start_bf, after = lax.optimization_barrier((start_bf, after))
        found = pl.pallas_call(
            functools.partial(scores_kernel, plan, digits),
            out_shape=[payload] * len(digits),
            in_specs=[vmem] * 2 + [hbm],
            out_specs=[vmem] * len(digits),
            scratch_shapes=[
                VMEM((len(digits) * columns, samples), BF16),
                pltpu.SemaphoreType.DMA((len(digits) * len(rest),)),
            ],
            name="scores",
        )(in_vmem(start_bf), in_vmem(stats), genotypes)
        sent.update(zip(digits, found))
        after = found[0]

    assert radix == 4 and all(r == 4 for r, _ in later)
    block = num_variants // count
    quarter = block * len(rest)
    assert 4 * quarter == num_variants
    half = GENE_MAX // 2
    own_shape = VMEM((half, quarter), F32)
    pass_shape = VMEM((half + 2 * rows, quarter), F32)
    send_shape = VMEM((half + rows, 2 * quarter), F32)
    *parts, send_x, send_y = pl.pallas_call(
        functools.partial(cross_kernel, plan, block),
        out_shape=[own_shape] * 2 + [pass_shape] * 2 + [send_shape] * 2,
        in_specs=[smem] + [vmem] * 3,
        out_specs=[vmem] * 6,
        scratch_shapes=[VMEM((quarter, samples), BF16)],
        name="cross",
    )(gene_sizes, weights, tied(variants, sent[0]), in_vmem(weighted))

    terms = [sent[0]] + [swap(sent[d], count, firsts[d]) for d in range(1, radix)]
    wide = columns
    for level, (r, s) in enumerate(later):
        wide //= r
        pieces = pl.pallas_call(
            merge_kernel,
            out_shape=[VMEM((rows, wide), F32)] * r,
            in_specs=[vmem] * len(terms),
            out_specs=[vmem] * r,
            name="merge",
        )(*map(in_vmem, terms))
        piece = pieces[0]
        if level == 0:
            piece, send_x, send_y = lax.optimization_barrier((piece, send_x, send_y))
        terms = [piece] + [swap(pieces[d], count, d * s) for d in range(1, r)]
    got = terms[0]
    for one in terms[1:]:
        got = got + one
    for r, s in reversed(later):
        got = jnp.concatenate([got] + [swap(got, count, d * s) for d in range(1, r)], axis=1)
    arrays = [in_vmem(got)] + [in_vmem(swap(got, count, firsts[d])) for d in range(1, radix)]

    got_x = swap(send_x, count, firsts[1])
    got_y = swap(send_y, count, firsts[2])
    own_x, own_y, pass_x, pass_y = pl.pallas_call(
        halves_kernel,
        out_shape=[own_shape] * 2 + [pass_shape] * 2,
        in_specs=[vmem] * 6,
        out_specs=[vmem] * 4,
        input_output_aliases={2 + i: i for i in range(4)},
        name="halves",
    )(*map(in_vmem, (got_x, got_y, *parts)))
    got_x, got_y = swap(pass_x, count, firsts[2]), swap(pass_y, count, firsts[1])
    (r, s), deeper = later[0], later[1:]
    wide = quarter // 2
    tall = half + 4 * rows
    kept, moved = pl.pallas_call(
        split_kernel,
        out_shape=[VMEM((tall, quarter), F32)] * 2,
        in_specs=[vmem] * 6,
        out_specs=[vmem] * 2,
        name="split",
    )(*map(in_vmem, (own_x, own_y, pass_x, pass_y, got_x, got_y)))
    got_x = swap(moved, count, s)
    kept, moved = pl.pallas_call(
        functools.partial(pair_kernel, half),
        out_shape=[VMEM((tall + 4 * rows, wide), F32)] * 2,
        in_specs=[vmem] * 2,
        out_specs=[vmem] * 2,
        name="pair",
    )(in_vmem(kept), in_vmem(got_x))
    sums = [kept, swap(moved, count, 2 * s)]
    if deeper:
        products, scores = sums[0] + sums[1], None
        products, scores = products[:half], products[half:]
        for r, s in deeper:
            products, scores = cut_by(products, scores, count, s)
        products = jnp.pad(products, ((0, 0), (0, wide - products.shape[1])))
        sums = [jnp.concatenate([products, scores], axis=0)]

    own = ()
    for d in range(radix):
        whole = pl.pallas_call(
            functools.partial(terms_kernel, plan, d),
            out_shape=VMEM((rows, samples + LANES), F32),
            in_specs=[vmem] * (2 + len(own)) + [hbm],
            out_specs=vmem,
            scratch_shapes=[VMEM((columns, samples), BF16), pltpu.SemaphoreType.DMA((len(rest),))],
            name="terms",
        )(diag, arrays[d], *map(in_vmem, own), genotypes)
        own = (whole,)
    (held,) = own
    assert marks & (marks - 1) == 0
    other = None
    offset = 1
    while offset < marks:
        other = swap(held, marks, offset, "mark")
        offset *= 2
        if offset < marks:
            kept = held[:, samples : samples + 2]
            held = held + other
            held = jnp.concatenate([held[:, :samples], kept, held[:, samples + 2 :]], axis=1)
    held = in_vmem(held)
    flat = VMEM((rows, LANES), F32)
    full = jax.ShapeDtypeStruct((rows, samples), F32)
    solution, residual, norm, alpha = pl.pallas_call(
        update_kernel,
        out_shape=[VMEM((rows, samples), F32)] * 2 + [flat] * 2,
        in_specs=[vmem] * 5,
        out_specs=[vmem] * 4,
        name="update",
    )(diag, start, right, held, in_vmem(other))
    norms = [norm]
    for r, s in stages:
        total = norms[0]
        for one in norms[1:]:
            total = total + one
        norms = [total] + [swap(total, count, d * s) for d in range(1, r)]
    direction = pl.pallas_call(
        direction_kernel,
        out_shape=full,
        in_specs=[vmem] * (4 + len(norms)),
        out_specs=vmem,
        name="direction",
    )(diag, start, held, in_vmem(residual), *map(in_vmem, norms))

    gram, solution, residual = pl.pallas_call(
        functools.partial(gram_kernel, samples * count),
        out_shape=[jax.ShapeDtypeStruct((1, block, num_variants), F32), full, full],
        in_specs=[smem] + [vmem] * (3 + len(sums)),
        out_specs=[vmem, hbm, hbm],
        scratch_shapes=[VMEM((rows, num_variants), F32), pltpu.SemaphoreType.DMA((2,))],
        name="gram",
    )(gene_sizes, *map(in_vmem, (alpha, *sums, solution, residual)))
    return solution, residual, direction, gram


def solution(mesh):
    return jax.shard_map(
        body,
        mesh=mesh,
        in_specs=(
            P("mark", "samp"),
            P("mark", "samp"),
            P("samp"),
            P(),
            P(None, "samp"),
            P("mark", None),
        ),
        out_specs=(P(None, "samp"), P(None, "samp"), P(None, "samp"), P("mark", "samp", None)),
        check_vma=False,
    )
```

```python
import dataclasses
import functools

import jax
import jax.numpy as jnp
from jax import lax
from jax.experimental import pallas as pl
from jax.experimental.pallas import tpu as pltpu
from jax.sharding import PartitionSpec as P


GENE_MAX = 400
LANES = 128
F32 = jnp.float32
BF16 = jnp.bfloat16
VMEM = pltpu.VMEM
NT = (((1,), (1,)), ((), ()))


def up(value, step):
    return -(-value // step) * step


def stages_of(count):
    found, stride = [], 1
    while stride < count:
        radix = 4 if count // stride % 4 == 0 else 2
        found.append((radix, stride))
        stride *= radix
    return found


def offsets_of(stages):
    found = [0]
    for radix, stride in stages:
        found = [base ^ (digit * stride) for base in found for digit in range(radix)]
    return found


def swap(array, count, offset, axis="samp"):
    return lax.ppermute(array, axis, [(i, i ^ offset) for i in range(count)])


def chunk_start(chunk, width, total):
    return pl.multiple_of(jnp.minimum(chunk * width, total - width), 16)


def fresh_lanes(chunk, width, total, rows):
    lane = lax.broadcasted_iota(jnp.int32, (rows, width), 1)
    return lane + jnp.minimum(chunk * width, total - width) >= chunk * width


def in_vmem(array):
    return pltpu.with_memory_space_constraint(array, pltpu.VMEM)


def fetch(copies):
    for copy in copies:
        copy.start()
    return copies


def geno_copies(plan, chunks, geno, held, sems, base=0):
    width, total = plan.width, plan.total
    return [
        pltpu.make_async_copy(
            geno.at[pl.ds(chunk_start(chunk, width, total), width), :],
            held.at[pl.ds(j * width, width), :],
            sems.at[base + j],
        )
        for j, chunk in enumerate(chunks)
    ]


def scores_begin(plan, digits, me, geno, held, sems):
    begun, per = [], len(plan.rest)
    columns = held.shape[0] // len(digits)
    for at, digit in enumerate(digits):
        chunks = [me ^ (digit * plan.stride) ^ r for r in plan.rest]
        window = held.at[pl.ds(at * columns, columns), :]
        begun.append((chunks, fetch(geno_copies(plan, chunks, geno, window, sems, at * per))))
    return begun


def scores_finish(plan, begun, start_bf, stats, held, outs):
    width, total = plan.width, plan.total
    for at, ((chunks, copies), out) in enumerate(zip(begun, outs)):
        for j, copy in enumerate(copies):
            copy.wait()
            low = (at * len(chunks) + j) * width
            part = lax.dot_general(start_bf, held[low : low + width, :], NT, preferred_element_type=F32)
            part = jnp.where(fresh_lanes(chunks[j], width, total, part.shape[0]), part, 0.0)
            out[:, j * width : (j + 1) * width] = part
            lane = lax.broadcasted_iota(jnp.int32, stats.shape, 1)
            head = jnp.where((lane < 2) & (chunks[j] == plan.count - 1), stats, part[:, :LANES])
            out[:, j * width : j * width + LANES] = head


def lead_kernel(plan, digit, ratio, weights, panel, geno, out, diag, right, start, start_bf, weighted, stats, *scratch):
    held, weights_held, ratio_held, sems, small = scratch
    first = fetch(
        [
            pltpu.make_async_copy(panel, right, small.at[0]),
            pltpu.make_async_copy(weights, weights_held, small.at[1]),
            pltpu.make_async_copy(ratio, ratio_held, small.at[2]),
        ]
    )
    begun = scores_begin(plan, (digit,), lax.axis_index("samp"), geno, held, sems)
    for copy in first:
        copy.wait()
    mu = weights_held[...].reshape(1, weights_held.shape[0])
    whole = 1.0 / mu + ratio_held[0]
    way = right[...] / whole
    diag[0:1, :] = whole
    diag[1:2, :] = mu
    diag[2:3, :] = jnp.full(mu.shape, ratio_held[0], F32)
    start[...] = way
    start_bf[...] = way.astype(BF16)
    exact = mu * way
    high = exact.astype(BF16)
    weighted[...] = jnp.concatenate([high, (exact - high.astype(F32)).astype(BF16)], axis=0)
    norm = jnp.sum(right[...] * way, axis=1, keepdims=True)
    own = jnp.sum(way * (way / mu), axis=1, keepdims=True)
    lane = lax.broadcasted_iota(jnp.int32, stats.shape, 1)
    stats[...] = jnp.where(lane == 0, norm, jnp.where(lane == 1, own, 0.0))
    scores_finish(plan, begun, start_bf[...], stats[...], held, (out,))


def scores_kernel(plan, digits, start_bf, stats, geno, *refs):
    *outs, held, sems = refs
    begun = scores_begin(plan, digits, lax.axis_index("samp"), geno, held, sems)
    scores_finish(plan, begun, start_bf[...], stats[...], held, outs)


def terms_kernel(plan, digit, diag, scores, *refs):
    *before, geno, out, held, sems = refs
    width, total = plan.width, plan.total
    me = lax.axis_index("samp")
    samples = geno.shape[1]
    chunks = [me ^ (digit * plan.stride) ^ r for r in plan.rest]
    copies = fetch(geno_copies(plan, chunks, geno, held, sems))
    scale = diag[2:3, 0:1] / plan.markers
    terms = before[0][:, :samples] if before else jnp.zeros((out.shape[0], samples), F32)
    stats = before[0][:, samples:] if before else jnp.zeros((out.shape[0], LANES), F32)
    lane = lax.broadcasted_iota(jnp.int32, stats.shape, 1)
    for j, copy in enumerate(copies):
        raw = scores[:, j * width : (j + 1) * width]
        fresh = fresh_lanes(chunks[j], width, total, raw.shape[0])
        scaled = jnp.where(fresh, scale * raw, 0.0)
        square = jnp.sum(scaled * raw, axis=1, keepdims=True)
        stats = stats + jnp.where(lane == 2, square, jnp.where((lane < 2) & (chunks[j] == plan.count - 1), raw[:, :LANES], 0.0))
        copy.wait()
        terms = terms + jnp.dot(
            scaled.astype(BF16), held[j * width : (j + 1) * width, :], preferred_element_type=F32
        )
    out[:, :samples] = terms
    out[:, samples:] = stats


def update_kernel(diag, start, right, own, other, solution, residual, norm, alpha_out):
    samples = start.shape[1]
    total = own[...] + other[...]
    start_norm = own[:, samples : samples + 1]
    curvature = own[:, samples + 1 : samples + 2] + total[:, samples + 2 : samples + 3]
    alpha = start_norm / curvature
    image = start[...] / diag[1:2, :] + total[:, :samples]
    left = right[...] - alpha * image
    solution[...] = alpha * start[...]
    residual[...] = left
    norm[...] = jnp.broadcast_to(jnp.sum(left * (left / diag[0:1, :]), axis=1, keepdims=True), norm.shape)
    alpha_out[...] = jnp.broadcast_to(alpha, alpha_out.shape)


def gene_bounds(sizes, index, count):
    low = jnp.zeros(index.shape, jnp.int32)
    high = jnp.full(index.shape, count, jnp.int32)
    end = jnp.int32(0)
    for g in range(sizes.shape[1]):
        end = end + sizes[0, g]
        low = jnp.where(end <= index, end, low)
        high = jnp.where((end > index) & (end < high), end, high)
    return low, high


def cross_kernel(plan, block, digit, sizes, start_bf, stats, diag, weighted, geno, all_variants, *refs):
    *outs, held, variants, scaled, sems, small = refs
    me = lax.axis_index("samp")
    (copy,) = fetch([pltpu.make_async_copy(all_variants, variants, small.at[0])])
    begun = scores_begin(plan, (digit,), me, geno, held, sems)
    copy.wait()
    cross_products(plan, block, me, sizes, diag[1:2, :], variants, weighted, scaled, outs[1:])
    scores_finish(plan, begun, start_bf[...], stats[...], held, outs[:1])


def cross_products(plan, block, me, sizes, mu, variants, weighted, scaled, outs):
    own_x, own_y, pass_x, pass_y, send_x, send_y = outs
    count = variants.shape[0]
    half = GENE_MAX // 2
    quarter = block * len(plan.rest)
    both = lax.dot_general(weighted[...], variants[...], NT, preferred_element_type=F32)
    rows = both.shape[0] // 2
    beta = both[:rows] + both[rows:]
    for at, (sent, kept) in enumerate(((send_x, pass_x), (send_y, pass_y))):
        sent[half:, :] = beta[:, 2 * at * quarter : 2 * (at + 1) * quarter]
        for j in range(2):
            low = (2 * at + j) * quarter
            kept[half + j * rows : half + (j + 1) * rows, :] = beta[:, low : low + quarter]
    lane = lax.broadcasted_iota(jnp.int32, (1, quarter), 1)
    column = lax.broadcasted_iota(jnp.int32, (count, quarter), 0)
    places = (
        ((own_x, 0), (own_y, 0)),
        ((send_x, 0), (pass_y, 0)),
        ((pass_x, 0), (send_y, 0)),
        ((send_x, 1), (send_y, 1)),
    )
    for digit in range(plan.radix):
        index = lane
        for j, r in enumerate(plan.rest):
            first = pl.multiple_of((me ^ (digit * plan.stride) ^ r) * block, block)
            mine = variants[pl.ds(first, block), :]
            scaled[j * block : (j + 1) * block, :] = (mine.astype(F32) * mu).astype(BF16)
            index = jnp.where(lane // block == j, first + lane - j * block, index)
        cross = lax.dot_general(variants[...], scaled[...], NT, preferred_element_type=F32)
        low, high = gene_bounds(sizes, index, count)
        cross = jnp.where((column >= low) & (column < high), cross, 0.0)
        for part, (out, at) in enumerate(places[digit]):
            folded = None
            for base in range(part * half, count, GENE_MAX):
                piece = cross[base : min(base + half, count)]
                if piece.shape[0] < half:
                    piece = jnp.concatenate([piece, jnp.zeros((half - piece.shape[0], quarter), F32)], axis=0)
                folded = piece if folded is None else folded + piece
            out[:half, at * quarter : (at + 1) * quarter] = folded


def halves_kernel(got_x, got_y, *refs):
    before, after = refs[:4], refs[4:]
    half, quarter = before[0].shape
    rows = got_x.shape[0] - half
    for at, (old, new) in enumerate(zip(before, after)):
        got = (got_x, got_y)[at % 2]
        low = at // 2 * quarter
        new[:half, :] = old[:half, :] + got[:half, low : low + quarter]
        if at >= 2:
            for j in range(2):
                to = slice(half + j * rows, half + (j + 1) * rows)
                new[to, :] = old[to, :] + got[half:, j * quarter : (j + 1) * quarter]


def split_kernel(own_x, own_y, pass_x, pass_y, got_x, got_y, kept, sent):
    half, quarter = own_x.shape
    low, high = own_x[...] + got_x[:half, :], own_y[...] + got_y[:half, :]
    wide = quarter // 4
    cut = [part[:, j * wide : (j + 1) * wide] for j in range(4) for part in (low, high)]
    kept[:half, :] = jnp.concatenate(cut[0:2] + cut[4:6], axis=1)
    sent[:half, :] = jnp.concatenate(cut[2:4] + cut[6:8], axis=1)
    tall = pass_x.shape[0] - half
    for at, (mine, got) in enumerate(((pass_x, got_x), (pass_y, got_y))):
        beta = mine[half:, :] + got[half:, :]
        for out in (kept, sent):
            out[half + at * tall : half + (at + 1) * tall, :] = beta


def pair_kernel(half, kept, got, stay, sent):
    wide = kept.shape[1] // 2
    tall = kept.shape[0] - half
    total = kept[...] + got[...]
    stay[:half, :] = total[:half, :wide]
    sent[:half, :] = total[:half, wide:]
    for out in (stay, sent):
        for j in range(2):
            out[half + j * tall : half + (j + 1) * tall, :] = total[half:, j * wide : (j + 1) * wide]


def last_kernel(samples, levels, sizes, diag, start, held, alpha, solved, left, *refs):
    *ins, solved_out, left_out, way_out, gram_out, way, out, full, sems = refs
    norms, sums = ins[:levels], ins[levels:]
    copies = fetch(
        [
            pltpu.make_async_copy(solved, solved_out, sems.at[0]),
            pltpu.make_async_copy(left, left_out, sems.at[1]),
        ]
    )
    norm = norms[0][:, :1]
    for ref in norms[1:]:
        norm = norm + ref[:, :1]
    wide = start.shape[1]
    start_norm = held[:, wide : wide + 1]
    way[...] = left[...] / diag[0:1, :] + (norm / start_norm) * start[...]
    copies += fetch([pltpu.make_async_copy(way, way_out, sems.at[2])])
    me = lax.axis_index("samp")
    count = out.shape[2]
    block = out.shape[1]
    half = GENE_MAX // 2
    rows = full.shape[0]
    total = sums[0][...]
    for ref in sums[1:]:
        total = total + ref[...]
    parts = count // LANES
    for j in range(parts):
        low = half + (j % 2 * (parts // 2) + j // 2) * rows
        full[:, j * LANES : (j + 1) * LANES] = total[low : low + rows, :] * alpha[:, :1]
    cross = jnp.concatenate([total[:half, :block], total[:half, block : 2 * block]], axis=0).T
    cross = jnp.concatenate([cross] * (-(-count // GENE_MAX)), axis=1)[:, :count]
    first = me * block
    window = max(block, LANES)
    base = pl.multiple_of(first // window * window, window)
    wide = lax.dot_general(
        full[:, pl.ds(base, window)],
        full[...],
        (((0,), (0,)), ((), ())),
        precision=lax.Precision.HIGHEST,
        preferred_element_type=F32,
    )
    correction = wide[:block]
    for step in range(1, window // block):
        correction = jnp.where(first - base == step * block, wide[step * block : (step + 1) * block], correction)
    low, high = gene_bounds(sizes, first + lax.broadcasted_iota(jnp.int32, (block, LANES), 0), count)
    column = lax.broadcasted_iota(jnp.int32, (block, count), 1)
    same = (column >= low[:, :1]) & (column < high[:, :1])
    out[0] = jnp.where(same, (cross - correction) / samples, 0.0)
    copies += fetch([pltpu.make_async_copy(out, gram_out, sems.at[3])])
    for copy in copies:
        copy.wait()


def cut_by(products, scores, count, stride):
    wide = products.shape[1] // 8
    low, high = products[:, : 4 * wide], products[:, 4 * wide :]
    cut = [jnp.concatenate([p[:, j * wide : (j + 1) * wide] for p in (low, high)], axis=1) for j in range(4)]
    kept = jnp.concatenate([cut[0], cut[2]], axis=1)
    kept = kept + swap(jnp.concatenate([cut[1], cut[3]], axis=1), count, stride)
    scores = scores + swap(scores, count, stride)
    products = kept[:, : 2 * wide] + swap(kept[:, 2 * wide :], count, 2 * stride)
    return products, scores + swap(scores, count, 2 * stride)


def merge_kernel(*refs):
    terms, outs = refs[:-4], refs[-4:]
    wide = outs[0].shape[1]
    for j, out in enumerate(outs):
        total = terms[0][:, j * wide : (j + 1) * wide]
        for ref in terms[1:]:
            total = total + ref[:, j * wide : (j + 1) * wide]
        out[...] = total


@dataclasses.dataclass(frozen=True)
class Plan:
    count: int
    radix: int
    stride: int
    rest: tuple
    width: int
    total: int
    markers: int


def body(genotypes, variants, weights, variance_ratio, panel, gene_sizes):
    count = lax.axis_size("samp")
    marks = lax.axis_size("mark")
    stages = stages_of(count)
    (radix, stride), later = stages[0], stages[1:]
    firsts = [digit * stride for digit in range(radix)]
    rest = offsets_of(later)
    local, samples = genotypes.shape
    width = up(-(-local // count), LANES)
    if count * width - local < 2:
        width += LANES
    plan = Plan(count, radix, stride, tuple(rest), width, local, local * marks)
    num_variants = variants.shape[0]
    rows = panel.shape[0]
    vmem = pl.BlockSpec(memory_space=VMEM)
    smem = pl.BlockSpec(memory_space=pltpu.SMEM)
    hbm = pl.BlockSpec(memory_space=pltpu.MemorySpace.HBM)
    columns = len(rest) * width
    payload = VMEM((rows, columns), F32)

    lead = radix - 1
    sent = {}
    sent[lead], diag, right, start, start_bf, weighted, stats = pl.pallas_call(
        functools.partial(lead_kernel, plan, lead),
        out_shape=[
            payload,
            VMEM((8, samples), F32),
            VMEM((rows, samples), F32),
            VMEM((rows, samples), F32),
            VMEM((rows, samples), BF16),
            VMEM((2 * rows, samples), BF16),
            VMEM((rows, LANES), F32),
        ],
        in_specs=[hbm] * 4,
        out_specs=[vmem] * 7,
        scratch_shapes=[
            VMEM((columns, samples), BF16),
            VMEM((samples,), F32),
            pltpu.SMEM((1,), F32),
            pltpu.SemaphoreType.DMA((len(rest),)),
            pltpu.SemaphoreType.DMA((3,)),
        ],
        name="scores_lead",
    )(variance_ratio, weights, panel, genotypes)
    diag, right, start = in_vmem(diag), in_vmem(right), in_vmem(start)
    after = sent[lead]
    start_bf, after = lax.optimization_barrier((start_bf, after))
    digits = tuple(range(1, lead))
    found = pl.pallas_call(
        functools.partial(scores_kernel, plan, digits),
        out_shape=[payload] * len(digits),
        in_specs=[vmem] * 2 + [hbm],
        out_specs=[vmem] * len(digits),
        scratch_shapes=[
            VMEM((len(digits) * columns, samples), BF16),
            pltpu.SemaphoreType.DMA((len(digits) * len(rest),)),
        ],
        name="scores",
    )(in_vmem(start_bf), in_vmem(stats), genotypes)
    sent.update(zip(digits, found))
    start_bf, after = lax.optimization_barrier((start_bf, found[0]))

    assert radix == 4 and all(r == 4 for r, _ in later)
    block = num_variants // count
    quarter = block * len(rest)
    assert 4 * quarter == num_variants
    half = GENE_MAX // 2
    own_shape = VMEM((half, quarter), F32)
    pass_shape = VMEM((half + 2 * rows, quarter), F32)
    send_shape = VMEM((half + rows, 2 * quarter), F32)
    sent[0], *parts, send_x, send_y = pl.pallas_call(
        functools.partial(cross_kernel, plan, block, 0),
        out_shape=[payload] + [own_shape] * 2 + [pass_shape] * 2 + [send_shape] * 2,
        in_specs=[smem] + [vmem] * 4 + [hbm] * 2,
        out_specs=[vmem] * 7,
        scratch_shapes=[
            VMEM((columns, samples), BF16),
            VMEM((num_variants, samples), BF16),
            VMEM((quarter, samples), BF16),
            pltpu.SemaphoreType.DMA((len(rest),)),
            pltpu.SemaphoreType.DMA((1,)),
        ],
        name="scores_cross",
    )(gene_sizes, in_vmem(start_bf), in_vmem(stats), diag, in_vmem(weighted), genotypes, variants)

    terms = [sent[0]] + [swap(sent[d], count, firsts[d]) for d in range(1, radix)]
    wide = columns
    for level, (r, s) in enumerate(later):
        wide //= r
        pieces = pl.pallas_call(
            merge_kernel,
            out_shape=[VMEM((rows, wide), F32)] * r,
            in_specs=[vmem] * len(terms),
            out_specs=[vmem] * r,
            name="merge",
        )(*map(in_vmem, terms))
        piece = pieces[0]
        if level == 0:
            piece, send_x, send_y = lax.optimization_barrier((piece, send_x, send_y))
        terms = [piece] + [swap(pieces[d], count, d * s) for d in range(1, r)]
    got = terms[0]
    for one in terms[1:]:
        got = got + one
    for r, s in reversed(later):
        got = jnp.concatenate([got] + [swap(got, count, d * s) for d in range(1, r)], axis=1)
    arrays = [in_vmem(got)] + [in_vmem(swap(got, count, firsts[d])) for d in range(1, radix)]

    got_x = swap(send_x, count, firsts[1])
    got_y = swap(send_y, count, firsts[2])
    own_x, own_y, pass_x, pass_y = pl.pallas_call(
        halves_kernel,
        out_shape=[own_shape] * 2 + [pass_shape] * 2,
        in_specs=[vmem] * 6,
        out_specs=[vmem] * 4,
        input_output_aliases={2 + i: i for i in range(4)},
        name="halves",
    )(*map(in_vmem, (got_x, got_y, *parts)))
    got_x, got_y = swap(pass_x, count, firsts[2]), swap(pass_y, count, firsts[1])
    (r, s), deeper = later[0], later[1:]
    wide = quarter // 2
    tall = half + 4 * rows
    kept, moved = pl.pallas_call(
        split_kernel,
        out_shape=[VMEM((tall, quarter), F32)] * 2,
        in_specs=[vmem] * 6,
        out_specs=[vmem] * 2,
        name="split",
    )(*map(in_vmem, (own_x, own_y, pass_x, pass_y, got_x, got_y)))
    got_x = swap(moved, count, s)
    kept, moved = pl.pallas_call(
        functools.partial(pair_kernel, half),
        out_shape=[VMEM((tall + 4 * rows, wide), F32)] * 2,
        in_specs=[vmem] * 2,
        out_specs=[vmem] * 2,
        name="pair",
    )(in_vmem(kept), in_vmem(got_x))
    sums = [kept, swap(moved, count, 2 * s)]
    if deeper:
        products, scores = sums[0] + sums[1], None
        products, scores = products[:half], products[half:]
        for r, s in deeper:
            products, scores = cut_by(products, scores, count, s)
        products = jnp.pad(products, ((0, 0), (0, wide - products.shape[1])))
        sums = [jnp.concatenate([products, scores], axis=0)]

    own = ()
    for d in range(radix):
        whole = pl.pallas_call(
            functools.partial(terms_kernel, plan, d),
            out_shape=VMEM((rows, samples + LANES), F32),
            in_specs=[vmem] * (2 + len(own)) + [hbm],
            out_specs=vmem,
            scratch_shapes=[VMEM((columns, samples), BF16), pltpu.SemaphoreType.DMA((len(rest),))],
            name="terms",
        )(diag, arrays[d], *map(in_vmem, own), genotypes)
        own = (whole,)
    (held,) = own
    assert marks & (marks - 1) == 0
    other = None
    offset = 1
    while offset < marks:
        other = swap(held, marks, offset, "mark")
        offset *= 2
        if offset < marks:
            kept = held[:, samples : samples + 2]
            held = held + other
            held = jnp.concatenate([held[:, :samples], kept, held[:, samples + 2 :]], axis=1)
    held = in_vmem(held)
    flat = VMEM((rows, LANES), F32)
    full = jax.ShapeDtypeStruct((rows, samples), F32)
    solution, residual, norm, alpha = pl.pallas_call(
        update_kernel,
        out_shape=[VMEM((rows, samples), F32)] * 2 + [flat] * 2,
        in_specs=[vmem] * 5,
        out_specs=[vmem] * 4,
        name="update",
    )(diag, start, right, held, in_vmem(other))
    norms = [norm]
    for r, s in stages:
        total = norms[0]
        for one in norms[1:]:
            total = total + one
        norms = [total] + [swap(total, count, d * s) for d in range(1, r)]
    gram_shape = (1, block, num_variants)
    solution, residual, direction, gram = pl.pallas_call(
        functools.partial(last_kernel, samples * count, len(norms)),
        out_shape=[full] * 3 + [jax.ShapeDtypeStruct(gram_shape, F32)],
        in_specs=[smem] + [vmem] * (6 + len(norms) + len(sums)),
        out_specs=[hbm] * 4,
        scratch_shapes=[
            VMEM((rows, samples), F32),
            VMEM(gram_shape, F32),
            VMEM((rows, num_variants), F32),
            pltpu.SemaphoreType.DMA((4,)),
        ],
        name="last",
    )(gene_sizes, diag, start, held, *map(in_vmem, (alpha, solution, residual, *norms, *sums)))
    return solution, residual, direction, gram


def solution(mesh):
    return jax.shard_map(
        body,
        mesh=mesh,
        in_specs=(
            P("mark", "samp"),
            P("mark", "samp"),
            P("samp"),
            P(),
            P(None, "samp"),
            P("mark", None),
        ),
        out_specs=(P(None, "samp"), P(None, "samp"), P(None, "samp"), P("mark", "samp", None)),
        check_vma=False,
    )
```

```python
import dataclasses
import functools

import jax
import jax.numpy as jnp
from jax import lax
from jax.experimental import pallas as pl
from jax.experimental.pallas import tpu as pltpu
from jax.sharding import PartitionSpec as P


GENE_MAX = 400
LANES = 128
F32 = jnp.float32
BF16 = jnp.bfloat16
VMEM = pltpu.VMEM
NT = (((1,), (1,)), ((), ()))


def up(value, step):
    return -(-value // step) * step


def stages_of(count):
    found, stride = [], 1
    while stride < count:
        radix = 4 if count // stride % 4 == 0 else 2
        found.append((radix, stride))
        stride *= radix
    return found


def offsets_of(stages):
    found = [0]
    for radix, stride in stages:
        found = [base ^ (digit * stride) for base in found for digit in range(radix)]
    return found


def swap(array, count, offset, axis="samp"):
    return lax.ppermute(array, axis, [(i, i ^ offset) for i in range(count)])


def chunk_start(chunk, width, total):
    return pl.multiple_of(jnp.minimum(chunk * width, total - width), 16)


def fresh_lanes(chunk, width, total, rows):
    lane = lax.broadcasted_iota(jnp.int32, (rows, width), 1)
    return lane + jnp.minimum(chunk * width, total - width) >= chunk * width


def kernel(*args, grant=16 << 20, **kwargs):
    return pl.pallas_call(*args, compiler_params=pltpu.CompilerParams(vmem_limit_bytes=grant), **kwargs)


def in_vmem(array):
    return pltpu.with_memory_space_constraint(array, pltpu.VMEM)


def fetch(copies):
    for copy in copies:
        copy.start()
    return copies


def geno_copies(plan, chunks, geno, held, sems, base=0):
    width, total = plan.width, plan.total
    return [
        pltpu.make_async_copy(
            geno.at[pl.ds(chunk_start(chunk, width, total), width), :],
            held.at[pl.ds(j * width, width), :],
            sems.at[base + j],
        )
        for j, chunk in enumerate(chunks)
    ]


def scores_begin(plan, digits, me, geno, helds, sems):
    begun, per = [], len(plan.rest)
    for at, (digit, held) in enumerate(zip(digits, helds)):
        chunks = [me ^ (digit * plan.stride) ^ r for r in plan.rest]
        begun.append((chunks, held, fetch(geno_copies(plan, chunks, geno, held, sems, at * per))))
    return begun


def scores_finish(plan, begun, start_bf, stats, outs):
    width, total = plan.width, plan.total
    for (chunks, held, copies), out in zip(begun, outs):
        for j, copy in enumerate(copies):
            copy.wait()
            low = j * width
            part = lax.dot_general(start_bf, held[low : low + width, :], NT, preferred_element_type=F32)
            part = jnp.where(fresh_lanes(chunks[j], width, total, part.shape[0]), part, 0.0)
            out[:, j * width : (j + 1) * width] = part
            lane = lax.broadcasted_iota(jnp.int32, stats.shape, 1)
            head = jnp.where((lane < 2) & (chunks[j] == plan.count - 1), stats, part[:, :LANES])
            out[:, j * width : j * width + LANES] = head


def lead_kernel(plan, digit, ratio, weights, panel, geno, out, held, diag, right, start, start_bf, weighted, stats, *scratch):
    weights_held, ratio_held, sems, small = scratch
    first = fetch(
        [
            pltpu.make_async_copy(panel, right, small.at[0]),
            pltpu.make_async_copy(weights, weights_held, small.at[1]),
            pltpu.make_async_copy(ratio, ratio_held, small.at[2]),
        ]
    )
    begun = scores_begin(plan, (digit,), lax.axis_index("samp"), geno, (held,), sems)
    for copy in first:
        copy.wait()
    mu = weights_held[...].reshape(1, weights_held.shape[0])
    whole = 1.0 / mu + ratio_held[0]
    way = right[...] / whole
    diag[0:1, :] = whole
    diag[1:2, :] = mu
    diag[2:3, :] = jnp.full(mu.shape, ratio_held[0], F32)
    start[...] = way
    start_bf[...] = way.astype(BF16)
    exact = mu * way
    high = exact.astype(BF16)
    weighted[...] = jnp.concatenate([high, (exact - high.astype(F32)).astype(BF16)], axis=0)
    norm = jnp.sum(right[...] * way, axis=1, keepdims=True)
    own = jnp.sum(way * (way / mu), axis=1, keepdims=True)
    lane = lax.broadcasted_iota(jnp.int32, stats.shape, 1)
    stats[...] = jnp.where(lane == 0, norm, jnp.where(lane == 1, own, 0.0))
    scores_finish(plan, begun, start_bf[...], stats[...], (out,))


def scores_kernel(plan, digits, start_bf, stats, geno, *refs):
    *outs, sems = refs
    outs, helds = outs[: len(digits)], outs[len(digits) :]
    begun = scores_begin(plan, digits, lax.axis_index("samp"), geno, helds, sems)
    scores_finish(plan, begun, start_bf[...], stats[...], outs)


def terms_kernel(plan, digit, diag, scores, held, *refs):
    *before, out = refs
    width, total = plan.width, plan.total
    me = lax.axis_index("samp")
    samples = held.shape[1]
    chunks = [me ^ (digit * plan.stride) ^ r for r in plan.rest]
    scale = diag[2:3, 0:1] / plan.markers
    terms = before[0][:, :samples] if before else jnp.zeros((out.shape[0], samples), F32)
    stats = before[0][:, samples:] if before else jnp.zeros((out.shape[0], LANES), F32)
    lane = lax.broadcasted_iota(jnp.int32, stats.shape, 1)
    for j in range(len(chunks)):
        raw = scores[:, j * width : (j + 1) * width]
        fresh = fresh_lanes(chunks[j], width, total, raw.shape[0])
        scaled = jnp.where(fresh, scale * raw, 0.0)
        square = jnp.sum(scaled * raw, axis=1, keepdims=True)
        stats = stats + jnp.where(lane == 2, square, jnp.where((lane < 2) & (chunks[j] == plan.count - 1), raw[:, :LANES], 0.0))
        terms = terms + jnp.dot(
            scaled.astype(BF16), held[j * width : (j + 1) * width, :], preferred_element_type=F32
        )
    out[:, :samples] = terms
    out[:, samples:] = stats


def update_kernel(diag, start, right, own, other, solution, residual, norm, alpha_out):
    samples = start.shape[1]
    total = own[...] + other[...]
    start_norm = own[:, samples : samples + 1]
    curvature = own[:, samples + 1 : samples + 2] + total[:, samples + 2 : samples + 3]
    alpha = start_norm / curvature
    image = start[...] / diag[1:2, :] + total[:, :samples]
    left = right[...] - alpha * image
    solution[...] = alpha * start[...]
    residual[...] = left
    norm[...] = jnp.broadcast_to(jnp.sum(left * (left / diag[0:1, :]), axis=1, keepdims=True), norm.shape)
    alpha_out[...] = jnp.broadcast_to(alpha, alpha_out.shape)


def gene_bounds(sizes, index, count):
    low = jnp.zeros(index.shape, jnp.int32)
    high = jnp.full(index.shape, count, jnp.int32)
    end = jnp.int32(0)
    for g in range(sizes.shape[1]):
        end = end + sizes[0, g]
        low = jnp.where(end <= index, end, low)
        high = jnp.where((end > index) & (end < high), end, high)
    return low, high


def cross_kernel(plan, block, digit, sizes, start_bf, stats, diag, weighted, geno, all_variants, *refs):
    out, held, *outs, variants, scaled, sems, small = refs
    me = lax.axis_index("samp")
    (copy,) = fetch([pltpu.make_async_copy(all_variants, variants, small.at[0])])
    begun = scores_begin(plan, (digit,), me, geno, (held,), sems)
    copy.wait()
    cross_products(plan, block, me, sizes, diag[1:2, :], variants, weighted, scaled, outs)
    scores_finish(plan, begun, start_bf[...], stats[...], (out,))


def cross_products(plan, block, me, sizes, mu, variants, weighted, scaled, outs):
    own_x, own_y, pass_x, pass_y, send_x, send_y = outs
    count = variants.shape[0]
    half = GENE_MAX // 2
    quarter = block * len(plan.rest)
    both = lax.dot_general(weighted[...], variants[...], NT, preferred_element_type=F32)
    rows = both.shape[0] // 2
    beta = both[:rows] + both[rows:]
    for at, (sent, kept) in enumerate(((send_x, pass_x), (send_y, pass_y))):
        sent[half:, :] = beta[:, 2 * at * quarter : 2 * (at + 1) * quarter]
        for j in range(2):
            low = (2 * at + j) * quarter
            kept[half + j * rows : half + (j + 1) * rows, :] = beta[:, low : low + quarter]
    lane = lax.broadcasted_iota(jnp.int32, (1, quarter), 1)
    column = lax.broadcasted_iota(jnp.int32, (count, quarter), 0)
    places = (
        ((own_x, 0), (own_y, 0)),
        ((send_x, 0), (pass_y, 0)),
        ((pass_x, 0), (send_y, 0)),
        ((send_x, 1), (send_y, 1)),
    )
    for digit in range(plan.radix):
        index = lane
        for j, r in enumerate(plan.rest):
            first = pl.multiple_of((me ^ (digit * plan.stride) ^ r) * block, block)
            mine = variants[pl.ds(first, block), :]
            scaled[j * block : (j + 1) * block, :] = (mine.astype(F32) * mu).astype(BF16)
            index = jnp.where(lane // block == j, first + lane - j * block, index)
        cross = lax.dot_general(variants[...], scaled[...], NT, preferred_element_type=F32)
        low, high = gene_bounds(sizes, index, count)
        cross = jnp.where((column >= low) & (column < high), cross, 0.0)
        for part, (out, at) in enumerate(places[digit]):
            folded = None
            for base in range(part * half, count, GENE_MAX):
                piece = cross[base : min(base + half, count)]
                if piece.shape[0] < half:
                    piece = jnp.concatenate([piece, jnp.zeros((half - piece.shape[0], quarter), F32)], axis=0)
                folded = piece if folded is None else folded + piece
            out[:half, at * quarter : (at + 1) * quarter] = folded


def halves_kernel(got_x, got_y, *refs):
    before, after = refs[:4], refs[4:]
    half, quarter = before[0].shape
    rows = got_x.shape[0] - half
    for at, (old, new) in enumerate(zip(before, after)):
        got = (got_x, got_y)[at % 2]
        low = at // 2 * quarter
        new[:half, :] = old[:half, :] + got[:half, low : low + quarter]
        if at >= 2:
            for j in range(2):
                to = slice(half + j * rows, half + (j + 1) * rows)
                new[to, :] = old[to, :] + got[half:, j * quarter : (j + 1) * quarter]


def split_kernel(own_x, own_y, pass_x, pass_y, got_x, got_y, kept, sent):
    half, quarter = own_x.shape
    low, high = own_x[...] + got_x[:half, :], own_y[...] + got_y[:half, :]
    wide = quarter // 4
    cut = [part[:, j * wide : (j + 1) * wide] for j in range(4) for part in (low, high)]
    kept[:half, :] = jnp.concatenate(cut[0:2] + cut[4:6], axis=1)
    sent[:half, :] = jnp.concatenate(cut[2:4] + cut[6:8], axis=1)
    tall = pass_x.shape[0] - half
    for at, (mine, got) in enumerate(((pass_x, got_x), (pass_y, got_y))):
        beta = mine[half:, :] + got[half:, :]
        for out in (kept, sent):
            out[half + at * tall : half + (at + 1) * tall, :] = beta


def pair_kernel(half, kept, got, stay, sent):
    wide = kept.shape[1] // 2
    tall = kept.shape[0] - half
    total = kept[...] + got[...]
    stay[:half, :] = total[:half, :wide]
    sent[:half, :] = total[:half, wide:]
    for out in (stay, sent):
        for j in range(2):
            out[half + j * tall : half + (j + 1) * tall, :] = total[half:, j * wide : (j + 1) * wide]


def last_kernel(samples, levels, sizes, diag, start, held, alpha, solved, left, *refs):
    *ins, solved_out, left_out, way_out, gram_out, way, out, full, sems = refs
    norms, sums = ins[:levels], ins[levels:]
    copies = fetch(
        [
            pltpu.make_async_copy(solved, solved_out, sems.at[0]),
            pltpu.make_async_copy(left, left_out, sems.at[1]),
        ]
    )
    norm = norms[0][:, :1]
    for ref in norms[1:]:
        norm = norm + ref[:, :1]
    wide = start.shape[1]
    start_norm = held[:, wide : wide + 1]
    way[...] = left[...] / diag[0:1, :] + (norm / start_norm) * start[...]
    copies += fetch([pltpu.make_async_copy(way, way_out, sems.at[2])])
    me = lax.axis_index("samp")
    count = out.shape[2]
    block = out.shape[1]
    half = GENE_MAX // 2
    rows = full.shape[0]
    total = sums[0][...]
    for ref in sums[1:]:
        total = total + ref[...]
    parts = count // LANES
    for j in range(parts):
        low = half + (j % 2 * (parts // 2) + j // 2) * rows
        full[:, j * LANES : (j + 1) * LANES] = total[low : low + rows, :] * alpha[:, :1]
    cross = jnp.concatenate([total[:half, :block], total[:half, block : 2 * block]], axis=0).T
    cross = jnp.concatenate([cross] * (-(-count // GENE_MAX)), axis=1)[:, :count]
    first = me * block
    window = max(block, LANES)
    base = pl.multiple_of(first // window * window, window)
    wide = lax.dot_general(
        full[:, pl.ds(base, window)],
        full[...],
        (((0,), (0,)), ((), ())),
        precision=lax.Precision.HIGHEST,
        preferred_element_type=F32,
    )
    correction = wide[:block]
    for step in range(1, window // block):
        correction = jnp.where(first - base == step * block, wide[step * block : (step + 1) * block], correction)
    low, high = gene_bounds(sizes, first + lax.broadcasted_iota(jnp.int32, (block, LANES), 0), count)
    column = lax.broadcasted_iota(jnp.int32, (block, count), 1)
    same = (column >= low[:, :1]) & (column < high[:, :1])
    out[0] = jnp.where(same, (cross - correction) / samples, 0.0)
    copies += fetch([pltpu.make_async_copy(out, gram_out, sems.at[3])])
    for copy in copies:
        copy.wait()


def cut_by(products, scores, count, stride):
    wide = products.shape[1] // 8
    low, high = products[:, : 4 * wide], products[:, 4 * wide :]
    cut = [jnp.concatenate([p[:, j * wide : (j + 1) * wide] for p in (low, high)], axis=1) for j in range(4)]
    kept = jnp.concatenate([cut[0], cut[2]], axis=1)
    kept = kept + swap(jnp.concatenate([cut[1], cut[3]], axis=1), count, stride)
    scores = scores + swap(scores, count, stride)
    products = kept[:, : 2 * wide] + swap(kept[:, 2 * wide :], count, 2 * stride)
    return products, scores + swap(scores, count, 2 * stride)


def merge_kernel(*refs):
    terms, outs = refs[:-4], refs[-4:]
    wide = outs[0].shape[1]
    for j, out in enumerate(outs):
        total = terms[0][:, j * wide : (j + 1) * wide]
        for ref in terms[1:]:
            total = total + ref[:, j * wide : (j + 1) * wide]
        out[...] = total


@dataclasses.dataclass(frozen=True)
class Plan:
    count: int
    radix: int
    stride: int
    rest: tuple
    width: int
    total: int
    markers: int


def body(genotypes, variants, weights, variance_ratio, panel, gene_sizes):
    count = lax.axis_size("samp")
    marks = lax.axis_size("mark")
    stages = stages_of(count)
    (radix, stride), later = stages[0], stages[1:]
    firsts = [digit * stride for digit in range(radix)]
    rest = offsets_of(later)
    local, samples = genotypes.shape
    width = up(-(-local // count), LANES)
    if count * width - local < 2:
        width += LANES
    plan = Plan(count, radix, stride, tuple(rest), width, local, local * marks)
    num_variants = variants.shape[0]
    rows = panel.shape[0]
    vmem = pl.BlockSpec(memory_space=VMEM)
    smem = pl.BlockSpec(memory_space=pltpu.SMEM)
    hbm = pl.BlockSpec(memory_space=pltpu.MemorySpace.HBM)
    columns = len(rest) * width
    payload = VMEM((rows, columns), F32)
    window = VMEM((columns, samples), BF16)

    lead = radix - 1
    sent, genos = {}, {}
    sent[lead], genos[lead], diag, right, start, start_bf, weighted, stats = kernel(
        functools.partial(lead_kernel, plan, lead),
        out_shape=[
            payload,
            window,
            VMEM((8, samples), F32),
            VMEM((rows, samples), F32),
            VMEM((rows, samples), F32),
            VMEM((rows, samples), BF16),
            VMEM((2 * rows, samples), BF16),
            VMEM((rows, LANES), F32),
        ],
        in_specs=[hbm] * 4,
        out_specs=[vmem] * 8,
        scratch_shapes=[
            VMEM((samples,), F32),
            pltpu.SMEM((1,), F32),
            pltpu.SemaphoreType.DMA((len(rest),)),
            pltpu.SemaphoreType.DMA((3,)),
        ],
        name="scores_lead",
    )(variance_ratio, weights, panel, genotypes)
    diag, right, start = in_vmem(diag), in_vmem(right), in_vmem(start)
    after = sent[lead]
    start_bf, after = lax.optimization_barrier((start_bf, after))
    digits = tuple(range(1, lead))
    found = kernel(
        functools.partial(scores_kernel, plan, digits),
        out_shape=[payload] * len(digits) + [window] * len(digits),
        in_specs=[vmem] * 2 + [hbm],
        out_specs=[vmem] * (2 * len(digits)),
        scratch_shapes=[
            pltpu.SemaphoreType.DMA((len(digits) * len(rest),)),
        ],
        name="scores",
    )(in_vmem(start_bf), in_vmem(stats), genotypes)
    sent.update(zip(digits, found))
    genos.update(zip(digits, found[len(digits) :]))
    start_bf, after = lax.optimization_barrier((start_bf, found[0]))

    assert radix == 4 and all(r == 4 for r, _ in later)
    block = num_variants // count
    quarter = block * len(rest)
    assert 4 * quarter == num_variants
    half = GENE_MAX // 2
    own_shape = VMEM((half, quarter), F32)
    pass_shape = VMEM((half + 2 * rows, quarter), F32)
    send_shape = VMEM((half + rows, 2 * quarter), F32)
    sent[0], genos[0], *parts, send_x, send_y = kernel(
        functools.partial(cross_kernel, plan, block, 0),
        out_shape=[payload, window] + [own_shape] * 2 + [pass_shape] * 2 + [send_shape] * 2,
        in_specs=[smem] + [vmem] * 4 + [hbm] * 2,
        out_specs=[vmem] * 8,
        scratch_shapes=[
            VMEM((num_variants, samples), BF16),
            VMEM((quarter, samples), BF16),
            pltpu.SemaphoreType.DMA((len(rest),)),
            pltpu.SemaphoreType.DMA((1,)),
        ],
        name="scores_cross",
    )(gene_sizes, in_vmem(start_bf), in_vmem(stats), diag, in_vmem(weighted), genotypes, variants)

    terms = [sent[0]] + [swap(sent[d], count, firsts[d]) for d in range(1, radix)]
    wide = columns
    for level, (r, s) in enumerate(later):
        wide //= r
        pieces = kernel(
            merge_kernel,
            out_shape=[VMEM((rows, wide), F32)] * r,
            in_specs=[vmem] * len(terms),
            out_specs=[vmem] * r,
            name="merge",
        )(*map(in_vmem, terms))
        piece = pieces[0]
        if level == 0:
            piece, send_x, send_y = lax.optimization_barrier((piece, send_x, send_y))
        terms = [piece] + [swap(pieces[d], count, d * s) for d in range(1, r)]
    got = terms[0]
    for one in terms[1:]:
        got = got + one
    for r, s in reversed(later):
        got = jnp.concatenate([got] + [swap(got, count, d * s) for d in range(1, r)], axis=1)
    arrays = [in_vmem(got)] + [in_vmem(swap(got, count, firsts[d])) for d in range(1, radix)]

    got_x = swap(send_x, count, firsts[1])
    got_y = swap(send_y, count, firsts[2])
    own_x, own_y, pass_x, pass_y = kernel(
        halves_kernel,
        out_shape=[own_shape] * 2 + [pass_shape] * 2,
        in_specs=[vmem] * 6,
        out_specs=[vmem] * 4,
        input_output_aliases={2 + i: i for i in range(4)},
        name="halves",
    )(*map(in_vmem, (got_x, got_y, *parts)))
    got_x, got_y = swap(pass_x, count, firsts[2]), swap(pass_y, count, firsts[1])
    (r, s), deeper = later[0], later[1:]
    wide = quarter // 2
    tall = half + 4 * rows
    kept, moved = kernel(
        split_kernel,
        out_shape=[VMEM((tall, quarter), F32)] * 2,
        in_specs=[vmem] * 6,
        out_specs=[vmem] * 2,
        name="split",
    )(*map(in_vmem, (own_x, own_y, pass_x, pass_y, got_x, got_y)))
    got_x = swap(moved, count, s)
    kept, moved = kernel(
        functools.partial(pair_kernel, half),
        out_shape=[VMEM((tall + 4 * rows, wide), F32)] * 2,
        in_specs=[vmem] * 2,
        out_specs=[vmem] * 2,
        name="pair",
    )(in_vmem(kept), in_vmem(got_x))
    sums = [kept, swap(moved, count, 2 * s)]
    if deeper:
        products, scores = sums[0] + sums[1], None
        products, scores = products[:half], products[half:]
        for r, s in deeper:
            products, scores = cut_by(products, scores, count, s)
        products = jnp.pad(products, ((0, 0), (0, wide - products.shape[1])))
        sums = [jnp.concatenate([products, scores], axis=0)]

    own = ()
    for d in range(radix):
        whole = kernel(
            functools.partial(terms_kernel, plan, d),
            out_shape=VMEM((rows, samples + LANES), F32),
            in_specs=[vmem] * (3 + len(own)),
            out_specs=vmem,
            name="terms",
        )(diag, arrays[d], in_vmem(genos[d]), *map(in_vmem, own))
        own = (whole,)
    (held,) = own
    assert marks & (marks - 1) == 0
    other = None
    offset = 1
    while offset < marks:
        other = swap(held, marks, offset, "mark")
        offset *= 2
        if offset < marks:
            kept = held[:, samples : samples + 2]
            held = held + other
            held = jnp.concatenate([held[:, :samples], kept, held[:, samples + 2 :]], axis=1)
    held = in_vmem(held)
    flat = VMEM((rows, LANES), F32)
    full = jax.ShapeDtypeStruct((rows, samples), F32)
    solution, residual, norm, alpha = kernel(
        update_kernel,
        out_shape=[VMEM((rows, samples), F32)] * 2 + [flat] * 2,
        in_specs=[vmem] * 5,
        out_specs=[vmem] * 4,
        name="update",
    )(diag, start, right, held, in_vmem(other))
    norms = [norm]
    for r, s in stages:
        total = norms[0]
        for one in norms[1:]:
            total = total + one
        norms = [total] + [swap(total, count, d * s) for d in range(1, r)]
    gram_shape = (1, block, num_variants)
    solution, residual, direction, gram = kernel(
        functools.partial(last_kernel, samples * count, len(norms)),
        out_shape=[full] * 3 + [jax.ShapeDtypeStruct(gram_shape, F32)],
        in_specs=[smem] + [vmem] * (6 + len(norms) + len(sums)),
        out_specs=[hbm] * 4,
        scratch_shapes=[
            VMEM((rows, samples), F32),
            VMEM(gram_shape, F32),
            VMEM((rows, num_variants), F32),
            pltpu.SemaphoreType.DMA((4,)),
        ],
        name="last",
    )(gene_sizes, diag, start, held, *map(in_vmem, (alpha, solution, residual, *norms, *sums)))
    return solution, residual, direction, gram


def solution(mesh):
    return jax.shard_map(
        body,
        mesh=mesh,
        in_specs=(
            P("mark", "samp"),
            P("mark", "samp"),
            P("samp"),
            P(),
            P(None, "samp"),
            P("mark", None),
        ),
        out_specs=(P(None, "samp"), P(None, "samp"), P(None, "samp"), P("mark", "samp", None)),
        check_vma=False,
    )
```

```python
import dataclasses
import functools

import jax
import jax.numpy as jnp
from jax import lax
from jax.experimental import pallas as pl
from jax.experimental.pallas import tpu as pltpu
from jax.sharding import PartitionSpec as P


GENE_MAX = 400
LANES = 128
F32 = jnp.float32
BF16 = jnp.bfloat16
VMEM = pltpu.VMEM
NT = (((1,), (1,)), ((), ()))


def up(value, step):
    return -(-value // step) * step


def stages_of(count):
    found, stride = [], 1
    while stride < count:
        radix = 4 if count // stride % 4 == 0 else 2
        found.append((radix, stride))
        stride *= radix
    return found


def offsets_of(stages):
    found = [0]
    for radix, stride in stages:
        found = [base ^ (digit * stride) for base in found for digit in range(radix)]
    return found


def swap(array, count, offset, axis="samp"):
    return lax.ppermute(array, axis, [(i, i ^ offset) for i in range(count)])


def chunk_start(chunk, width, total):
    return pl.multiple_of(jnp.minimum(chunk * width, total - width), 16)


def fresh_lanes(chunk, width, total, rows):
    lane = lax.broadcasted_iota(jnp.int32, (rows, width), 1)
    return lane + jnp.minimum(chunk * width, total - width) >= chunk * width


def kernel(*args, grant=16 << 20, **kwargs):
    return pl.pallas_call(*args, compiler_params=pltpu.CompilerParams(vmem_limit_bytes=grant), **kwargs)


def in_vmem(array):
    return pltpu.with_memory_space_constraint(array, pltpu.VMEM)


def in_hbm(array):
    return pltpu.with_memory_space_constraint(array, pltpu.MemorySpace.HBM)


def fetch(copies):
    for copy in copies:
        copy.start()
    return copies


def geno_copies(plan, chunks, geno, held, sems, base=0):
    width, total = plan.width, plan.total
    return [
        pltpu.make_async_copy(
            geno.at[pl.ds(chunk_start(chunk, width, total), width), :],
            held.at[pl.ds(j * width, width), :],
            sems.at[base + j],
        )
        for j, chunk in enumerate(chunks)
    ]


def scores_begin(plan, digits, me, geno, helds, sems):
    begun, per = [], len(plan.rest)
    for at, (digit, held) in enumerate(zip(digits, helds)):
        chunks = [me ^ (digit * plan.stride) ^ r for r in plan.rest]
        begun.append((chunks, held, fetch(geno_copies(plan, chunks, geno, held, sems, at * per))))
    return begun


def scores_finish(plan, begun, start_bf, stats, outs):
    width, total = plan.width, plan.total
    for (chunks, held, copies), out in zip(begun, outs):
        for j, copy in enumerate(copies):
            copy.wait()
            low = j * width
            part = lax.dot_general(start_bf, held[low : low + width, :], NT, preferred_element_type=F32)
            part = jnp.where(fresh_lanes(chunks[j], width, total, part.shape[0]), part, 0.0)
            out[:, j * width : (j + 1) * width] = part
            lane = lax.broadcasted_iota(jnp.int32, stats.shape, 1)
            head = jnp.where((lane < 2) & (chunks[j] == plan.count - 1), stats, part[:, :LANES])
            out[:, j * width : j * width + LANES] = head


def lead_kernel(plan, digit, ratio, weights, panel, geno, out, held, diag, right, start, start_bf, weighted, stats, *scratch):
    weights_held, ratio_held, sems, small = scratch
    first = fetch(
        [
            pltpu.make_async_copy(panel, right, small.at[0]),
            pltpu.make_async_copy(weights, weights_held, small.at[1]),
            pltpu.make_async_copy(ratio, ratio_held, small.at[2]),
        ]
    )
    begun = scores_begin(plan, (digit,), lax.axis_index("samp"), geno, (held,), sems)
    for copy in first:
        copy.wait()
    mu = weights_held[...].reshape(1, weights_held.shape[0])
    whole = 1.0 / mu + ratio_held[0]
    way = right[...] / whole
    diag[0:1, :] = whole
    diag[1:2, :] = mu
    diag[2:3, :] = jnp.full(mu.shape, ratio_held[0], F32)
    start[...] = way
    start_bf[...] = way.astype(BF16)
    exact = mu * way
    high = exact.astype(BF16)
    weighted[...] = jnp.concatenate([high, (exact - high.astype(F32)).astype(BF16)], axis=0)
    norm = jnp.sum(right[...] * way, axis=1, keepdims=True)
    own = jnp.sum(way * (way / mu), axis=1, keepdims=True)
    lane = lax.broadcasted_iota(jnp.int32, stats.shape, 1)
    stats[...] = jnp.where(lane == 0, norm, jnp.where(lane == 1, own, 0.0))
    scores_finish(plan, begun, start_bf[...], stats[...], (out,))


def scores_kernel(plan, digits, start_bf, stats, geno, *refs):
    *outs, sems = refs
    outs, helds = outs[: len(digits)], outs[len(digits) :]
    begun = scores_begin(plan, digits, lax.axis_index("samp"), geno, helds, sems)
    scores_finish(plan, begun, start_bf[...], stats[...], outs)


def terms_kernel(plan, digit, diag, scores, held, *refs):
    *before, out = refs
    width, total = plan.width, plan.total
    me = lax.axis_index("samp")
    samples = held.shape[1]
    chunks = [me ^ (digit * plan.stride) ^ r for r in plan.rest]
    scale = diag[2:3, 0:1] / plan.markers
    terms = before[0][:, :samples] if before else jnp.zeros((out.shape[0], samples), F32)
    stats = before[0][:, samples:] if before else jnp.zeros((out.shape[0], LANES), F32)
    lane = lax.broadcasted_iota(jnp.int32, stats.shape, 1)
    for j in range(len(chunks)):
        raw = scores[:, j * width : (j + 1) * width]
        fresh = fresh_lanes(chunks[j], width, total, raw.shape[0])
        scaled = jnp.where(fresh, scale * raw, 0.0)
        square = jnp.sum(scaled * raw, axis=1, keepdims=True)
        stats = stats + jnp.where(lane == 2, square, jnp.where((lane < 2) & (chunks[j] == plan.count - 1), raw[:, :LANES], 0.0))
        terms = terms + jnp.dot(
            scaled.astype(BF16), held[j * width : (j + 1) * width, :], preferred_element_type=F32
        )
    out[:, :samples] = terms
    out[:, samples:] = stats


def update_kernel(diag, start, right, own, other, solution, residual, norm, alpha_out):
    samples = start.shape[1]
    total = own[...] + other[...]
    start_norm = own[:, samples : samples + 1]
    curvature = own[:, samples + 1 : samples + 2] + total[:, samples + 2 : samples + 3]
    alpha = start_norm / curvature
    image = start[...] / diag[1:2, :] + total[:, :samples]
    left = right[...] - alpha * image
    solution[...] = alpha * start[...]
    residual[...] = left
    norm[...] = jnp.broadcast_to(jnp.sum(left * (left / diag[0:1, :]), axis=1, keepdims=True), norm.shape)
    alpha_out[...] = jnp.broadcast_to(alpha, alpha_out.shape)


def gene_bounds(sizes, index, count):
    low = jnp.zeros(index.shape, jnp.int32)
    high = jnp.full(index.shape, count, jnp.int32)
    end = jnp.int32(0)
    for g in range(sizes.shape[1]):
        end = end + sizes[0, g]
        low = jnp.where(end <= index, end, low)
        high = jnp.where((end > index) & (end < high), end, high)
    return low, high


def cross_kernel(plan, block, digit, sizes, start_bf, stats, diag, weighted, geno, variants, *refs):
    out, held, *outs, scaled, sems = refs
    me = lax.axis_index("samp")
    begun = scores_begin(plan, (digit,), me, geno, (held,), sems)
    cross_products(plan, block, me, sizes, diag[1:2, :], variants, weighted, scaled, outs)
    scores_finish(plan, begun, start_bf[...], stats[...], (out,))


def cross_products(plan, block, me, sizes, mu, variants, weighted, scaled, outs):
    own_x, own_y, pass_x, pass_y, send_x, send_y = outs
    count = variants.shape[0]
    half = GENE_MAX // 2
    quarter = block * len(plan.rest)
    both = lax.dot_general(weighted[...], variants[...], NT, preferred_element_type=F32)
    rows = both.shape[0] // 2
    beta = both[:rows] + both[rows:]
    for at, (sent, kept) in enumerate(((send_x, pass_x), (send_y, pass_y))):
        sent[half:, :] = beta[:, 2 * at * quarter : 2 * (at + 1) * quarter]
        for j in range(2):
            low = (2 * at + j) * quarter
            kept[half + j * rows : half + (j + 1) * rows, :] = beta[:, low : low + quarter]
    lane = lax.broadcasted_iota(jnp.int32, (1, quarter), 1)
    column = lax.broadcasted_iota(jnp.int32, (count, quarter), 0)
    places = (
        ((own_x, 0), (own_y, 0)),
        ((send_x, 0), (pass_y, 0)),
        ((pass_x, 0), (send_y, 0)),
        ((send_x, 1), (send_y, 1)),
    )
    for digit in range(plan.radix):
        index = lane
        for j, r in enumerate(plan.rest):
            first = pl.multiple_of((me ^ (digit * plan.stride) ^ r) * block, block)
            mine = variants[pl.ds(first, block), :]
            scaled[j * block : (j + 1) * block, :] = (mine.astype(F32) * mu).astype(BF16)
            index = jnp.where(lane // block == j, first + lane - j * block, index)
        cross = lax.dot_general(variants[...], scaled[...], NT, preferred_element_type=F32)
        low, high = gene_bounds(sizes, index, count)
        cross = jnp.where((column >= low) & (column < high), cross, 0.0)
        for part, (out, at) in enumerate(places[digit]):
            folded = None
            for base in range(part * half, count, GENE_MAX):
                piece = cross[base : min(base + half, count)]
                if piece.shape[0] < half:
                    piece = jnp.concatenate([piece, jnp.zeros((half - piece.shape[0], quarter), F32)], axis=0)
                folded = piece if folded is None else folded + piece
            out[:half, at * quarter : (at + 1) * quarter] = folded


def halves_kernel(got_x, got_y, *refs):
    before, after = refs[:4], refs[4:]
    half, quarter = before[0].shape
    rows = got_x.shape[0] - half
    for at, (old, new) in enumerate(zip(before, after)):
        got = (got_x, got_y)[at % 2]
        low = at // 2 * quarter
        new[:half, :] = old[:half, :] + got[:half, low : low + quarter]
        if at >= 2:
            for j in range(2):
                to = slice(half + j * rows, half + (j + 1) * rows)
                new[to, :] = old[to, :] + got[half:, j * quarter : (j + 1) * quarter]


def split_kernel(own_x, own_y, pass_x, pass_y, got_x, got_y, kept, sent):
    half, quarter = own_x.shape
    low, high = own_x[...] + got_x[:half, :], own_y[...] + got_y[:half, :]
    wide = quarter // 4
    cut = [part[:, j * wide : (j + 1) * wide] for j in range(4) for part in (low, high)]
    kept[:half, :] = jnp.concatenate(cut[0:2] + cut[4:6], axis=1)
    sent[:half, :] = jnp.concatenate(cut[2:4] + cut[6:8], axis=1)
    tall = pass_x.shape[0] - half
    for at, (mine, got) in enumerate(((pass_x, got_x), (pass_y, got_y))):
        beta = mine[half:, :] + got[half:, :]
        for out in (kept, sent):
            out[half + at * tall : half + (at + 1) * tall, :] = beta


def pair_kernel(half, kept, got, stay, sent):
    wide = kept.shape[1] // 2
    tall = kept.shape[0] - half
    total = kept[...] + got[...]
    stay[:half, :] = total[:half, :wide]
    sent[:half, :] = total[:half, wide:]
    for out in (stay, sent):
        for j in range(2):
            out[half + j * tall : half + (j + 1) * tall, :] = total[half:, j * wide : (j + 1) * wide]


def last_kernel(samples, levels, sizes, diag, start, held, alpha, solved, left, *refs):
    *ins, solved_out, left_out, way_out, gram_out, way, out, full, sems = refs
    norms, sums = ins[:levels], ins[levels:]
    copies = fetch(
        [
            pltpu.make_async_copy(solved, solved_out, sems.at[0]),
            pltpu.make_async_copy(left, left_out, sems.at[1]),
        ]
    )
    norm = norms[0][:, :1]
    for ref in norms[1:]:
        norm = norm + ref[:, :1]
    wide = start.shape[1]
    start_norm = held[:, wide : wide + 1]
    way[...] = left[...] / diag[0:1, :] + (norm / start_norm) * start[...]
    copies += fetch([pltpu.make_async_copy(way, way_out, sems.at[2])])
    me = lax.axis_index("samp")
    count = out.shape[2]
    block = out.shape[1]
    half = GENE_MAX // 2
    rows = full.shape[0]
    total = sums[0][...]
    for ref in sums[1:]:
        total = total + ref[...]
    parts = count // LANES
    for j in range(parts):
        low = half + (j % 2 * (parts // 2) + j // 2) * rows
        full[:, j * LANES : (j + 1) * LANES] = total[low : low + rows, :] * alpha[:, :1]
    cross = jnp.concatenate([total[:half, :block], total[:half, block : 2 * block]], axis=0).T
    cross = jnp.concatenate([cross] * (-(-count // GENE_MAX)), axis=1)[:, :count]
    first = me * block
    window = max(block, LANES)
    base = pl.multiple_of(first // window * window, window)
    wide = lax.dot_general(
        full[:, pl.ds(base, window)],
        full[...],
        (((0,), (0,)), ((), ())),
        precision=lax.Precision.HIGHEST,
        preferred_element_type=F32,
    )
    correction = wide[:block]
    for step in range(1, window // block):
        correction = jnp.where(first - base == step * block, wide[step * block : (step + 1) * block], correction)
    low, high = gene_bounds(sizes, first + lax.broadcasted_iota(jnp.int32, (block, LANES), 0), count)
    column = lax.broadcasted_iota(jnp.int32, (block, count), 1)
    same = (column >= low[:, :1]) & (column < high[:, :1])
    out[0] = jnp.where(same, (cross - correction) / samples, 0.0)
    copies += fetch([pltpu.make_async_copy(out, gram_out, sems.at[3])])
    for copy in copies:
        copy.wait()


def cut_by(products, scores, count, stride):
    wide = products.shape[1] // 8
    low, high = products[:, : 4 * wide], products[:, 4 * wide :]
    cut = [jnp.concatenate([p[:, j * wide : (j + 1) * wide] for p in (low, high)], axis=1) for j in range(4)]
    kept = jnp.concatenate([cut[0], cut[2]], axis=1)
    kept = kept + swap(jnp.concatenate([cut[1], cut[3]], axis=1), count, stride)
    scores = scores + swap(scores, count, stride)
    products = kept[:, : 2 * wide] + swap(kept[:, 2 * wide :], count, 2 * stride)
    return products, scores + swap(scores, count, 2 * stride)


def merge_kernel(*refs):
    terms, outs = refs[:-4], refs[-4:]
    wide = outs[0].shape[1]
    for j, out in enumerate(outs):
        total = terms[0][:, j * wide : (j + 1) * wide]
        for ref in terms[1:]:
            total = total + ref[:, j * wide : (j + 1) * wide]
        out[...] = total


@dataclasses.dataclass(frozen=True)
class Plan:
    count: int
    radix: int
    stride: int
    rest: tuple
    width: int
    total: int
    markers: int


def body(genotypes, variants, weights, variance_ratio, panel, gene_sizes):
    count = lax.axis_size("samp")
    marks = lax.axis_size("mark")
    stages = stages_of(count)
    (radix, stride), later = stages[0], stages[1:]
    firsts = [digit * stride for digit in range(radix)]
    rest = offsets_of(later)
    local, samples = genotypes.shape
    width = up(-(-local // count), LANES)
    if count * width - local < 2:
        width += LANES
    plan = Plan(count, radix, stride, tuple(rest), width, local, local * marks)
    num_variants = variants.shape[0]
    rows = panel.shape[0]
    vmem = pl.BlockSpec(memory_space=VMEM)
    smem = pl.BlockSpec(memory_space=pltpu.SMEM)
    hbm = pl.BlockSpec(memory_space=pltpu.MemorySpace.HBM)
    genotypes, panel, weights = map(in_hbm, (genotypes, panel, weights))
    columns = len(rest) * width
    payload = VMEM((rows, columns), F32)
    window = VMEM((columns, samples), BF16)

    lead = radix - 1
    sent, genos = {}, {}
    sent[lead], genos[lead], diag, right, start, start_bf, weighted, stats = kernel(
        functools.partial(lead_kernel, plan, lead),
        out_shape=[
            payload,
            window,
            VMEM((8, samples), F32),
            VMEM((rows, samples), F32),
            VMEM((rows, samples), F32),
            VMEM((rows, samples), BF16),
            VMEM((2 * rows, samples), BF16),
            VMEM((rows, LANES), F32),
        ],
        in_specs=[hbm] * 4,
        out_specs=[vmem] * 8,
        scratch_shapes=[
            VMEM((samples,), F32),
            pltpu.SMEM((1,), F32),
            pltpu.SemaphoreType.DMA((len(rest),)),
            pltpu.SemaphoreType.DMA((3,)),
        ],
        name="scores_lead",
    )(variance_ratio, weights, panel, genotypes)
    diag, right, start = in_vmem(diag), in_vmem(right), in_vmem(start)
    after = sent[lead]
    start_bf, after = lax.optimization_barrier((start_bf, after))
    digits = tuple(range(1, lead))
    found = kernel(
        functools.partial(scores_kernel, plan, digits),
        out_shape=[payload] * len(digits) + [window] * len(digits),
        in_specs=[vmem] * 2 + [hbm],
        out_specs=[vmem] * (2 * len(digits)),
        scratch_shapes=[
            pltpu.SemaphoreType.DMA((len(digits) * len(rest),)),
        ],
        name="scores",
    )(in_vmem(start_bf), in_vmem(stats), genotypes)
    sent.update(zip(digits, found))
    genos.update(zip(digits, found[len(digits) :]))
    start_bf, after = lax.optimization_barrier((start_bf, found[0]))

    assert radix == 4 and all(r == 4 for r, _ in later)
    block = num_variants // count
    quarter = block * len(rest)
    assert 4 * quarter == num_variants
    half = GENE_MAX // 2
    own_shape = VMEM((half, quarter), F32)
    pass_shape = VMEM((half + 2 * rows, quarter), F32)
    send_shape = VMEM((half + rows, 2 * quarter), F32)
    sent[0], genos[0], *parts, send_x, send_y = kernel(
        functools.partial(cross_kernel, plan, block, 0),
        out_shape=[payload, window] + [own_shape] * 2 + [pass_shape] * 2 + [send_shape] * 2,
        in_specs=[smem] + [vmem] * 4 + [hbm, vmem],
        out_specs=[vmem] * 8,
        scratch_shapes=[
            VMEM((quarter, samples), BF16),
            pltpu.SemaphoreType.DMA((len(rest),)),
        ],
        name="scores_cross",
    )(gene_sizes, in_vmem(start_bf), in_vmem(stats), diag, in_vmem(weighted), genotypes, in_vmem(variants))

    terms = [sent[0]] + [swap(sent[d], count, firsts[d]) for d in range(1, radix)]
    wide = columns
    for level, (r, s) in enumerate(later):
        wide //= r
        pieces = kernel(
            merge_kernel,
            out_shape=[VMEM((rows, wide), F32)] * r,
            in_specs=[vmem] * len(terms),
            out_specs=[vmem] * r,
            name="merge",
        )(*map(in_vmem, terms))
        piece = pieces[0]
        if level == 0:
            piece, send_x, send_y = lax.optimization_barrier((piece, send_x, send_y))
        terms = [piece] + [swap(pieces[d], count, d * s) for d in range(1, r)]
    got = terms[0]
    for one in terms[1:]:
        got = got + one
    for r, s in reversed(later):
        got = jnp.concatenate([got] + [swap(got, count, d * s) for d in range(1, r)], axis=1)
    arrays = [in_vmem(got)] + [in_vmem(swap(got, count, firsts[d])) for d in range(1, radix)]

    got_x = swap(send_x, count, firsts[1])
    got_y = swap(send_y, count, firsts[2])
    own_x, own_y, pass_x, pass_y = kernel(
        halves_kernel,
        out_shape=[own_shape] * 2 + [pass_shape] * 2,
        in_specs=[vmem] * 6,
        out_specs=[vmem] * 4,
        input_output_aliases={2 + i: i for i in range(4)},
        name="halves",
    )(*map(in_vmem, (got_x, got_y, *parts)))
    got_x, got_y = swap(pass_x, count, firsts[2]), swap(pass_y, count, firsts[1])
    (r, s), deeper = later[0], later[1:]
    wide = quarter // 2
    tall = half + 4 * rows
    kept, moved = kernel(
        split_kernel,
        out_shape=[VMEM((tall, quarter), F32)] * 2,
        in_specs=[vmem] * 6,
        out_specs=[vmem] * 2,
        name="split",
    )(*map(in_vmem, (own_x, own_y, pass_x, pass_y, got_x, got_y)))
    got_x = swap(moved, count, s)
    kept, moved = kernel(
        functools.partial(pair_kernel, half),
        out_shape=[VMEM((tall + 4 * rows, wide), F32)] * 2,
        in_specs=[vmem] * 2,
        out_specs=[vmem] * 2,
        name="pair",
    )(in_vmem(kept), in_vmem(got_x))
    sums = [kept, swap(moved, count, 2 * s)]
    if deeper:
        products, scores = sums[0] + sums[1], None
        products, scores = products[:half], products[half:]
        for r, s in deeper:
            products, scores = cut_by(products, scores, count, s)
        products = jnp.pad(products, ((0, 0), (0, wide - products.shape[1])))
        sums = [jnp.concatenate([products, scores], axis=0)]

    own = ()
    for d in range(radix):
        whole = kernel(
            functools.partial(terms_kernel, plan, d),
            out_shape=VMEM((rows, samples + LANES), F32),
            in_specs=[vmem] * (3 + len(own)),
            out_specs=vmem,
            name="terms",
        )(diag, arrays[d], in_vmem(genos[d]), *map(in_vmem, own))
        own = (whole,)
    (held,) = own
    assert marks & (marks - 1) == 0
    other = None
    offset = 1
    while offset < marks:
        other = swap(held, marks, offset, "mark")
        offset *= 2
        if offset < marks:
            kept = held[:, samples : samples + 2]
            held = held + other
            held = jnp.concatenate([held[:, :samples], kept, held[:, samples + 2 :]], axis=1)
    held = in_vmem(held)
    flat = VMEM((rows, LANES), F32)
    full = jax.ShapeDtypeStruct((rows, samples), F32)
    solution, residual, norm, alpha = kernel(
        update_kernel,
        out_shape=[VMEM((rows, samples), F32)] * 2 + [flat] * 2,
        in_specs=[vmem] * 5,
        out_specs=[vmem] * 4,
        name="update",
    )(diag, start, right, held, in_vmem(other))
    norms = [norm]
    for r, s in stages:
        total = norms[0]
        for one in norms[1:]:
            total = total + one
        norms = [total] + [swap(total, count, d * s) for d in range(1, r)]
    gram_shape = (1, block, num_variants)
    solution, residual, direction, gram = kernel(
        functools.partial(last_kernel, samples * count, len(norms)),
        out_shape=[full] * 3 + [jax.ShapeDtypeStruct(gram_shape, F32)],
        in_specs=[smem] + [vmem] * (6 + len(norms) + len(sums)),
        out_specs=[hbm] * 4,
        scratch_shapes=[
            VMEM((rows, samples), F32),
            VMEM(gram_shape, F32),
            VMEM((rows, num_variants), F32),
            pltpu.SemaphoreType.DMA((4,)),
        ],
        name="last",
    )(gene_sizes, diag, start, held, *map(in_vmem, (alpha, solution, residual, *norms, *sums)))
    return solution, residual, direction, gram


def solution(mesh):
    return jax.shard_map(
        body,
        mesh=mesh,
        in_specs=(
            P("mark", "samp"),
            P("mark", "samp"),
            P("samp"),
            P(),
            P(None, "samp"),
            P("mark", None),
        ),
        out_specs=(P(None, "samp"), P(None, "samp"), P(None, "samp"), P("mark", "samp", None)),
        check_vma=False,
    )
```

```python
import dataclasses
import functools

import jax
import jax.numpy as jnp
from jax import lax
from jax.experimental import pallas as pl
from jax.experimental.pallas import tpu as pltpu
from jax.sharding import PartitionSpec as P


GENE_MAX = 400
LANES = 128
F32 = jnp.float32
BF16 = jnp.bfloat16
VMEM = pltpu.VMEM
NT = (((1,), (1,)), ((), ()))


def up(value, step):
    return -(-value // step) * step


def stages_of(count):
    found, stride = [], 1
    while stride < count:
        radix = 4 if count // stride % 4 == 0 else 2
        found.append((radix, stride))
        stride *= radix
    return found


def offsets_of(stages):
    found = [0]
    for radix, stride in stages:
        found = [base ^ (digit * stride) for base in found for digit in range(radix)]
    return found


def swap(array, count, offset, axis="samp"):
    return lax.ppermute(array, axis, [(i, i ^ offset) for i in range(count)])


def chunk_start(chunk, width, total):
    return pl.multiple_of(jnp.minimum(chunk * width, total - width), 16)


def fresh_lanes(chunk, width, total, rows):
    lane = lax.broadcasted_iota(jnp.int32, (rows, width), 1)
    return lane + jnp.minimum(chunk * width, total - width) >= chunk * width


def kernel(*args, grant=16 << 20, **kwargs):
    return pl.pallas_call(*args, compiler_params=pltpu.CompilerParams(vmem_limit_bytes=grant), **kwargs)


def in_vmem(array):
    return pltpu.with_memory_space_constraint(array, pltpu.VMEM)


def in_hbm(array):
    return pltpu.with_memory_space_constraint(array, pltpu.MemorySpace.HBM)


def fetch(copies):
    for copy in copies:
        copy.start()
    return copies


def geno_copies(plan, chunks, geno, held, sems, base=0):
    width, total = plan.width, plan.total
    return [
        pltpu.make_async_copy(
            geno.at[pl.ds(chunk_start(chunk, width, total), width), :],
            held.at[pl.ds(j * width, width), :],
            sems.at[base + j],
        )
        for j, chunk in enumerate(chunks)
    ]


def scores_begin(plan, digits, me, geno, helds, sems):
    begun, per = [], len(plan.rest)
    for at, (digit, held) in enumerate(zip(digits, helds)):
        chunks = [me ^ (digit * plan.stride) ^ r for r in plan.rest]
        begun.append((chunks, held, fetch(geno_copies(plan, chunks, geno, held, sems, at * per))))
    return begun


def scores_finish(plan, begun, start_bf, stats, outs):
    width, total = plan.width, plan.total
    for (chunks, held, copies), out in zip(begun, outs):
        for j, copy in enumerate(copies):
            copy.wait()
            low = j * width
            part = lax.dot_general(start_bf, held[low : low + width, :], NT, preferred_element_type=F32)
            part = jnp.where(fresh_lanes(chunks[j], width, total, part.shape[0]), part, 0.0)
            out[:, j * width : (j + 1) * width] = part
            lane = lax.broadcasted_iota(jnp.int32, stats.shape, 1)
            head = jnp.where((lane < 2) & (chunks[j] == plan.count - 1), stats, part[:, :LANES])
            out[:, j * width : j * width + LANES] = head


def lead_kernel(plan, digit, ratio, weights, panel, geno, out, held, diag, right, start, start_bf, weighted, stats, *scratch):
    weights_held, ratio_held, sems, small = scratch
    first = fetch(
        [
            pltpu.make_async_copy(panel, right, small.at[0]),
            pltpu.make_async_copy(weights, weights_held, small.at[1]),
            pltpu.make_async_copy(ratio, ratio_held, small.at[2]),
        ]
    )
    begun = scores_begin(plan, (digit,), lax.axis_index("samp"), geno, (held,), sems)
    for copy in first:
        copy.wait()
    mu = weights_held[...].reshape(1, weights_held.shape[0])
    whole = 1.0 / mu + ratio_held[0]
    way = right[...] / whole
    diag[0:1, :] = whole
    diag[1:2, :] = mu
    diag[2:3, :] = jnp.full(mu.shape, ratio_held[0], F32)
    start[...] = way
    start_bf[...] = way.astype(BF16)
    exact = mu * way
    high = exact.astype(BF16)
    weighted[...] = jnp.concatenate([high, (exact - high.astype(F32)).astype(BF16)], axis=0)
    norm = jnp.sum(right[...] * way, axis=1, keepdims=True)
    own = jnp.sum(way * (way / mu), axis=1, keepdims=True)
    lane = lax.broadcasted_iota(jnp.int32, stats.shape, 1)
    stats[...] = jnp.where(lane == 0, norm, jnp.where(lane == 1, own, 0.0))
    scores_finish(plan, begun, start_bf[...], stats[...], (out,))


def scores_kernel(plan, digits, start_bf, stats, geno, *refs):
    *outs, sems = refs
    outs, helds = outs[: len(digits)], outs[len(digits) :]
    begun = scores_begin(plan, digits, lax.axis_index("samp"), geno, helds, sems)
    scores_finish(plan, begun, start_bf[...], stats[...], outs)


def terms_kernel(plan, digit, diag, scores, held, *refs):
    *before, out = refs
    width, total = plan.width, plan.total
    me = lax.axis_index("samp")
    samples = held.shape[1]
    chunks = [me ^ (digit * plan.stride) ^ r for r in plan.rest]
    scale = diag[2:3, 0:1] / plan.markers
    terms = before[0][:, :samples] if before else jnp.zeros((out.shape[0], samples), F32)
    stats = before[0][:, samples:] if before else jnp.zeros((out.shape[0], LANES), F32)
    lane = lax.broadcasted_iota(jnp.int32, stats.shape, 1)
    for j in range(len(chunks)):
        raw = scores[:, j * width : (j + 1) * width]
        fresh = fresh_lanes(chunks[j], width, total, raw.shape[0])
        scaled = jnp.where(fresh, scale * raw, 0.0)
        square = jnp.sum(scaled * raw, axis=1, keepdims=True)
        stats = stats + jnp.where(lane == 2, square, jnp.where((lane < 2) & (chunks[j] == plan.count - 1), raw[:, :LANES], 0.0))
        terms = terms + jnp.dot(
            scaled.astype(BF16), held[j * width : (j + 1) * width, :], preferred_element_type=F32
        )
    out[:, :samples] = terms
    out[:, samples:] = stats


def update_kernel(diag, start, right, own, other, solution, residual, norm, alpha_out):
    samples = start.shape[1]
    total = own[...] + other[...]
    start_norm = own[:, samples : samples + 1]
    curvature = own[:, samples + 1 : samples + 2] + total[:, samples + 2 : samples + 3]
    alpha = start_norm / curvature
    image = start[...] / diag[1:2, :] + total[:, :samples]
    left = right[...] - alpha * image
    solution[...] = alpha * start[...]
    residual[...] = left
    norm[...] = jnp.broadcast_to(jnp.sum(left * (left / diag[0:1, :]), axis=1, keepdims=True), norm.shape)
    alpha_out[...] = jnp.broadcast_to(alpha, alpha_out.shape)


def gene_bounds(sizes, index, count):
    low = jnp.zeros(index.shape, jnp.int32)
    high = jnp.full(index.shape, count, jnp.int32)
    end = jnp.int32(0)
    for g in range(sizes.shape[1]):
        end = end + sizes[0, g]
        low = jnp.where(end <= index, end, low)
        high = jnp.where((end > index) & (end < high), end, high)
    return low, high


def cross_kernel(plan, block, digit, sizes, start_bf, stats, diag, weighted, geno, variants, *refs):
    out, held, *outs, scaled, sems = refs
    me = lax.axis_index("samp")
    begun = scores_begin(plan, (digit,), me, geno, (held,), sems)
    cross_products(plan, block, me, sizes, diag[1:2, :], variants, weighted, scaled, outs)
    scores_finish(plan, begun, start_bf[...], stats[...], (out,))


def cross_products(plan, block, me, sizes, mu, variants, weighted, scaled, outs):
    own_x, own_y, pass_x, pass_y, send_x, send_y = outs
    count = variants.shape[0]
    half = GENE_MAX // 2
    quarter = block * len(plan.rest)
    both = lax.dot_general(weighted[...], variants[...], NT, preferred_element_type=F32)
    rows = both.shape[0] // 2
    beta = both[:rows] + both[rows:]
    for at, (sent, kept) in enumerate(((send_x, pass_x), (send_y, pass_y))):
        sent[half:, :] = beta[:, 2 * at * quarter : 2 * (at + 1) * quarter]
        for j in range(2):
            low = (2 * at + j) * quarter
            kept[half + j * rows : half + (j + 1) * rows, :] = beta[:, low : low + quarter]
    lane = lax.broadcasted_iota(jnp.int32, (1, quarter), 1)
    column = lax.broadcasted_iota(jnp.int32, (count, quarter), 0)
    places = (
        ((own_x, 0), (own_y, 0)),
        ((send_x, 0), (pass_y, 0)),
        ((pass_x, 0), (send_y, 0)),
        ((send_x, 1), (send_y, 1)),
    )
    for digit in range(plan.radix):
        index = lane
        for j, r in enumerate(plan.rest):
            first = pl.multiple_of((me ^ (digit * plan.stride) ^ r) * block, block)
            mine = variants[pl.ds(first, block), :]
            scaled[j * block : (j + 1) * block, :] = (mine.astype(F32) * mu).astype(BF16)
            index = jnp.where(lane // block == j, first + lane - j * block, index)
        cross = lax.dot_general(variants[...], scaled[...], NT, preferred_element_type=F32)
        low, high = gene_bounds(sizes, index, count)
        cross = jnp.where((column >= low) & (column < high), cross, 0.0)
        for part, (out, at) in enumerate(places[digit]):
            folded = None
            for base in range(part * half, count, GENE_MAX):
                piece = cross[base : min(base + half, count)]
                if piece.shape[0] < half:
                    piece = jnp.concatenate([piece, jnp.zeros((half - piece.shape[0], quarter), F32)], axis=0)
                folded = piece if folded is None else folded + piece
            out[:half, at * quarter : (at + 1) * quarter] = folded


def halves_kernel(got_x, got_y, *refs):
    before, after = refs[:4], refs[4:]
    half, quarter = before[0].shape
    rows = got_x.shape[0] - half
    for at, (old, new) in enumerate(zip(before, after)):
        got = (got_x, got_y)[at % 2]
        low = at // 2 * quarter
        new[:half, :] = old[:half, :] + got[:half, low : low + quarter]
        if at >= 2:
            for j in range(2):
                to = slice(half + j * rows, half + (j + 1) * rows)
                new[to, :] = old[to, :] + got[half:, j * quarter : (j + 1) * quarter]


def split_kernel(own_x, own_y, pass_x, pass_y, got_x, got_y, kept, sent):
    half, quarter = own_x.shape
    low, high = own_x[...] + got_x[:half, :], own_y[...] + got_y[:half, :]
    wide = quarter // 4
    cut = [part[:, j * wide : (j + 1) * wide] for j in range(4) for part in (low, high)]
    kept[:half, :] = jnp.concatenate(cut[0:2] + cut[4:6], axis=1)
    sent[:half, :] = jnp.concatenate(cut[2:4] + cut[6:8], axis=1)
    tall = pass_x.shape[0] - half
    for at, (mine, got) in enumerate(((pass_x, got_x), (pass_y, got_y))):
        beta = mine[half:, :] + got[half:, :]
        for out in (kept, sent):
            out[half + at * tall : half + (at + 1) * tall, :] = beta


def pair_kernel(half, kept, got, stay, sent):
    wide = kept.shape[1] // 2
    tall = kept.shape[0] - half
    total = kept[...] + got[...]
    stay[:half, :] = total[:half, :wide]
    sent[:half, :] = total[:half, wide:]
    for out in (stay, sent):
        for j in range(2):
            out[half + j * tall : half + (j + 1) * tall, :] = total[half:, j * wide : (j + 1) * wide]


def last_kernel(samples, levels, sizes, diag, start, held, alpha, solved, left, *refs):
    *ins, solved_out, left_out, way_out, gram_out, way, out, full, sems = refs
    norms, sums = ins[:levels], ins[levels:]
    copies = fetch(
        [
            pltpu.make_async_copy(solved, solved_out, sems.at[0]),
            pltpu.make_async_copy(left, left_out, sems.at[1]),
        ]
    )
    norm = norms[0][:, :1]
    for ref in norms[1:]:
        norm = norm + ref[:, :1]
    wide = start.shape[1]
    start_norm = held[:, wide : wide + 1]
    way[...] = left[...] / diag[0:1, :] + (norm / start_norm) * start[...]
    copies += fetch([pltpu.make_async_copy(way, way_out, sems.at[2])])
    me = lax.axis_index("samp")
    count = out.shape[2]
    block = out.shape[1]
    half = GENE_MAX // 2
    rows = full.shape[0]
    total = sums[0][...]
    for ref in sums[1:]:
        total = total + ref[...]
    parts = count // LANES
    for j in range(parts):
        low = half + (j % 2 * (parts // 2) + j // 2) * rows
        full[:, j * LANES : (j + 1) * LANES] = total[low : low + rows, :] * alpha[:, :1]
    cross = jnp.concatenate([total[:half, :block], total[:half, block : 2 * block]], axis=0).T
    cross = jnp.concatenate([cross] * (-(-count // GENE_MAX)), axis=1)[:, :count]
    first = me * block
    window = max(block, LANES)
    base = pl.multiple_of(first // window * window, window)
    wide = lax.dot_general(
        full[:, pl.ds(base, window)],
        full[...],
        (((0,), (0,)), ((), ())),
        precision=lax.Precision.HIGHEST,
        preferred_element_type=F32,
    )
    correction = wide[:block]
    for step in range(1, window // block):
        correction = jnp.where(first - base == step * block, wide[step * block : (step + 1) * block], correction)
    low, high = gene_bounds(sizes, first + lax.broadcasted_iota(jnp.int32, (block, LANES), 0), count)
    column = lax.broadcasted_iota(jnp.int32, (block, count), 1)
    same = (column >= low[:, :1]) & (column < high[:, :1])
    out[0] = jnp.where(same, (cross - correction) / samples, 0.0)
    copies += fetch([pltpu.make_async_copy(out, gram_out, sems.at[3])])
    for copy in copies:
        copy.wait()


def cut_by(products, scores, count, stride):
    wide = products.shape[1] // 8
    low, high = products[:, : 4 * wide], products[:, 4 * wide :]
    cut = [jnp.concatenate([p[:, j * wide : (j + 1) * wide] for p in (low, high)], axis=1) for j in range(4)]
    kept = jnp.concatenate([cut[0], cut[2]], axis=1)
    kept = kept + swap(jnp.concatenate([cut[1], cut[3]], axis=1), count, stride)
    scores = scores + swap(scores, count, stride)
    products = kept[:, : 2 * wide] + swap(kept[:, 2 * wide :], count, 2 * stride)
    return products, scores + swap(scores, count, 2 * stride)


def merge_kernel(*refs):
    terms, outs = refs[:-4], refs[-4:]
    wide = outs[0].shape[1]
    for j, out in enumerate(outs):
        total = terms[0][:, j * wide : (j + 1) * wide]
        for ref in terms[1:]:
            total = total + ref[:, j * wide : (j + 1) * wide]
        out[...] = total


@dataclasses.dataclass(frozen=True)
class Plan:
    count: int
    radix: int
    stride: int
    rest: tuple
    width: int
    total: int
    markers: int


def body(genotypes, variants, weights, variance_ratio, panel, gene_sizes):
    count = lax.axis_size("samp")
    marks = lax.axis_size("mark")
    stages = stages_of(count)
    (radix, stride), later = stages[0], stages[1:]
    firsts = [digit * stride for digit in range(radix)]
    rest = offsets_of(later)
    local, samples = genotypes.shape
    width = up(-(-local // count), LANES)
    if count * width - local < 2:
        width += LANES
    plan = Plan(count, radix, stride, tuple(rest), width, local, local * marks)
    num_variants = variants.shape[0]
    rows = panel.shape[0]
    vmem = pl.BlockSpec(memory_space=VMEM)
    smem = pl.BlockSpec(memory_space=pltpu.SMEM)
    hbm = pl.BlockSpec(memory_space=pltpu.MemorySpace.HBM)
    genotypes, panel, weights = map(in_hbm, (genotypes, panel, weights))
    columns = len(rest) * width
    payload = VMEM((rows, columns), F32)
    window = VMEM((columns, samples), BF16)

    lead = radix - 1
    sent, genos = {}, {}
    sent[lead], genos[lead], diag, right, start, start_bf, weighted, stats = kernel(
        functools.partial(lead_kernel, plan, lead),
        out_shape=[
            payload,
            window,
            VMEM((8, samples), F32),
            VMEM((rows, samples), F32),
            VMEM((rows, samples), F32),
            VMEM((rows, samples), BF16),
            VMEM((2 * rows, samples), BF16),
            VMEM((rows, LANES), F32),
        ],
        in_specs=[hbm] * 4,
        out_specs=[vmem] * 8,
        scratch_shapes=[
            VMEM((samples,), F32),
            pltpu.SMEM((1,), F32),
            pltpu.SemaphoreType.DMA((len(rest),)),
            pltpu.SemaphoreType.DMA((3,)),
        ],
        name="scores_lead",
    )(variance_ratio, weights, panel, genotypes)
    diag, right, start = in_vmem(diag), in_vmem(right), in_vmem(start)
    after = sent[lead]
    start_bf, after = lax.optimization_barrier((start_bf, after))
    digits = tuple(range(1, lead))
    found = kernel(
        functools.partial(scores_kernel, plan, digits),
        out_shape=[payload] * len(digits) + [window] * len(digits),
        in_specs=[vmem] * 2 + [hbm],
        out_specs=[vmem] * (2 * len(digits)),
        scratch_shapes=[
            pltpu.SemaphoreType.DMA((len(digits) * len(rest),)),
        ],
        name="scores",
    )(in_vmem(start_bf), in_vmem(stats), genotypes)
    sent.update(zip(digits, found))
    genos.update(zip(digits, found[len(digits) :]))
    start_bf, after = lax.optimization_barrier((start_bf, found[0]))

    assert radix == 4 and all(r == 4 for r, _ in later)
    block = num_variants // count
    quarter = block * len(rest)
    assert 4 * quarter == num_variants
    half = GENE_MAX // 2
    own_shape = VMEM((half, quarter), F32)
    pass_shape = VMEM((half + 2 * rows, quarter), F32)
    send_shape = VMEM((half + rows, 2 * quarter), F32)
    sent[0], genos[0], *parts, send_x, send_y = kernel(
        functools.partial(cross_kernel, plan, block, 0),
        out_shape=[payload, window] + [own_shape] * 2 + [pass_shape] * 2 + [send_shape] * 2,
        in_specs=[smem] + [vmem] * 4 + [hbm, vmem],
        out_specs=[vmem] * 8,
        scratch_shapes=[
            VMEM((quarter, samples), BF16),
            pltpu.SemaphoreType.DMA((len(rest),)),
        ],
        name="scores_cross",
    )(gene_sizes, in_vmem(start_bf), in_vmem(stats), diag, in_vmem(weighted), genotypes, in_vmem(variants))

    terms = [sent[0]] + [swap(sent[d], count, firsts[d]) for d in range(1, radix)]
    wide = columns
    for r, s in later:
        wide //= r
        pieces = kernel(
            merge_kernel,
            out_shape=[VMEM((rows, wide), F32)] * r,
            in_specs=[vmem] * len(terms),
            out_specs=[vmem] * r,
            name="merge",
        )(*map(in_vmem, terms))
        terms = [pieces[0]] + [swap(pieces[d], count, d * s) for d in range(1, r)]
    got = terms[0]
    for one in terms[1:]:
        got = got + one
    for r, s in reversed(later):
        got = jnp.concatenate([got] + [swap(got, count, d * s) for d in range(1, r)], axis=1)
    arrays = [in_vmem(got)] + [in_vmem(swap(got, count, firsts[d])) for d in range(1, radix)]

    got_x = swap(send_x, count, firsts[1])
    got_y = swap(send_y, count, firsts[2])
    own_x, own_y, pass_x, pass_y = kernel(
        halves_kernel,
        out_shape=[own_shape] * 2 + [pass_shape] * 2,
        in_specs=[vmem] * 6,
        out_specs=[vmem] * 4,
        input_output_aliases={2 + i: i for i in range(4)},
        name="halves",
    )(*map(in_vmem, (got_x, got_y, *parts)))
    got_x, got_y = swap(pass_x, count, firsts[2]), swap(pass_y, count, firsts[1])
    (r, s), deeper = later[0], later[1:]
    wide = quarter // 2
    tall = half + 4 * rows
    kept, moved = kernel(
        split_kernel,
        out_shape=[VMEM((tall, quarter), F32)] * 2,
        in_specs=[vmem] * 6,
        out_specs=[vmem] * 2,
        name="split",
    )(*map(in_vmem, (own_x, own_y, pass_x, pass_y, got_x, got_y)))
    got_x = swap(moved, count, s)
    kept, moved = kernel(
        functools.partial(pair_kernel, half),
        out_shape=[VMEM((tall + 4 * rows, wide), F32)] * 2,
        in_specs=[vmem] * 2,
        out_specs=[vmem] * 2,
        name="pair",
    )(in_vmem(kept), in_vmem(got_x))
    sums = [kept, swap(moved, count, 2 * s)]
    if deeper:
        products, scores = sums[0] + sums[1], None
        products, scores = products[:half], products[half:]
        for r, s in deeper:
            products, scores = cut_by(products, scores, count, s)
        products = jnp.pad(products, ((0, 0), (0, wide - products.shape[1])))
        sums = [jnp.concatenate([products, scores], axis=0)]

    own = ()
    for d in range(radix):
        whole = kernel(
            functools.partial(terms_kernel, plan, d),
            out_shape=VMEM((rows, samples + LANES), F32),
            in_specs=[vmem] * (3 + len(own)),
            out_specs=vmem,
            name="terms",
        )(diag, arrays[d], in_vmem(genos[d]), *map(in_vmem, own))
        own = (whole,)
    (held,) = own
    assert marks & (marks - 1) == 0
    other = None
    offset = 1
    while offset < marks:
        other = swap(held, marks, offset, "mark")
        offset *= 2
        if offset < marks:
            kept = held[:, samples : samples + 2]
            held = held + other
            held = jnp.concatenate([held[:, :samples], kept, held[:, samples + 2 :]], axis=1)
    held = in_vmem(held)
    flat = VMEM((rows, LANES), F32)
    full = jax.ShapeDtypeStruct((rows, samples), F32)
    solution, residual, norm, alpha = kernel(
        update_kernel,
        out_shape=[VMEM((rows, samples), F32)] * 2 + [flat] * 2,
        in_specs=[vmem] * 5,
        out_specs=[vmem] * 4,
        name="update",
    )(diag, start, right, held, in_vmem(other))
    norms = [norm]
    for r, s in stages:
        total = norms[0]
        for one in norms[1:]:
            total = total + one
        norms = [total] + [swap(total, count, d * s) for d in range(1, r)]
    gram_shape = (1, block, num_variants)
    solution, residual, direction, gram = kernel(
        functools.partial(last_kernel, samples * count, len(norms)),
        out_shape=[full] * 3 + [jax.ShapeDtypeStruct(gram_shape, F32)],
        in_specs=[smem] + [vmem] * (6 + len(norms) + len(sums)),
        out_specs=[hbm] * 4,
        scratch_shapes=[
            VMEM((rows, samples), F32),
            VMEM(gram_shape, F32),
            VMEM((rows, num_variants), F32),
            pltpu.SemaphoreType.DMA((4,)),
        ],
        name="last",
    )(gene_sizes, diag, start, held, *map(in_vmem, (alpha, solution, residual, *norms, *sums)))
    return solution, residual, direction, gram


def solution(mesh):
    return jax.shard_map(
        body,
        mesh=mesh,
        in_specs=(
            P("mark", "samp"),
            P("mark", "samp"),
            P("samp"),
            P(),
            P(None, "samp"),
            P("mark", None),
        ),
        out_specs=(P(None, "samp"), P(None, "samp"), P(None, "samp"), P("mark", "samp", None)),
        check_vma=False,
    )
```

```python
import dataclasses
import functools

import jax
import jax.numpy as jnp
from jax import lax
from jax.experimental import pallas as pl
from jax.experimental.pallas import tpu as pltpu
from jax.sharding import PartitionSpec as P


GENE_MAX = 400
LANES = 128
F32 = jnp.float32
BF16 = jnp.bfloat16
VMEM = pltpu.VMEM
NT = (((1,), (1,)), ((), ()))


def up(value, step):
    return -(-value // step) * step


def stages_of(count):
    found, stride = [], 1
    while stride < count:
        radix = 4 if count // stride % 4 == 0 else 2
        found.append((radix, stride))
        stride *= radix
    return found


def offsets_of(stages):
    found = [0]
    for radix, stride in stages:
        found = [base ^ (digit * stride) for base in found for digit in range(radix)]
    return found


def swap(array, count, offset, axis="samp"):
    return lax.ppermute(array, axis, [(i, i ^ offset) for i in range(count)])


def chunk_start(chunk, width, total):
    return pl.multiple_of(jnp.minimum(chunk * width, total - width), 16)


def fresh_lanes(chunk, width, total, rows):
    lane = lax.broadcasted_iota(jnp.int32, (rows, width), 1)
    return lane + jnp.minimum(chunk * width, total - width) >= chunk * width


def kernel(*args, grant=16 << 20, **kwargs):
    return pl.pallas_call(*args, compiler_params=pltpu.CompilerParams(vmem_limit_bytes=grant), **kwargs)


def in_vmem(array):
    return pltpu.with_memory_space_constraint(array, pltpu.VMEM)


def in_hbm(array):
    return pltpu.with_memory_space_constraint(array, pltpu.MemorySpace.HBM)


def fetch(copies):
    for copy in copies:
        copy.start()
    return copies


def geno_copies(plan, chunks, geno, held, sems, base=0):
    width, total = plan.width, plan.total
    return [
        pltpu.make_async_copy(
            geno.at[pl.ds(chunk_start(chunk, width, total), width), :],
            held.at[pl.ds(j * width, width), :],
            sems.at[base + j],
        )
        for j, chunk in enumerate(chunks)
    ]


def scores_begin(plan, digits, me, geno, helds, sems):
    begun, per = [], len(plan.rest)
    for at, (digit, held) in enumerate(zip(digits, helds)):
        chunks = [me ^ (digit * plan.stride) ^ r for r in plan.rest]
        begun.append((chunks, held, fetch(geno_copies(plan, chunks, geno, held, sems, at * per))))
    return begun


def scores_finish(plan, begun, start_bf, stats, outs, group=1):
    width, total = plan.width, plan.total
    for (chunks, held, copies), out in zip(begun, outs):
        for base in range(0, len(copies), group):
            near = range(base, min(base + group, len(copies)))
            for j in near:
                copies[j].wait()
            low, high = near[0] * width, (near[-1] + 1) * width
            parts = lax.dot_general(start_bf, held[low:high, :], NT, preferred_element_type=F32)
            for j in near:
                part = parts[:, j * width - low : (j + 1) * width - low]
                part = jnp.where(fresh_lanes(chunks[j], width, total, part.shape[0]), part, 0.0)
                out[:, j * width : (j + 1) * width] = part
                lane = lax.broadcasted_iota(jnp.int32, stats.shape, 1)
                head = jnp.where((lane < 2) & (chunks[j] == plan.count - 1), stats, part[:, :LANES])
                out[:, j * width : j * width + LANES] = head


def lead_kernel(plan, digit, ratio, weights, panel, geno, out, held, diag, right, start, start_bf, weighted, stats, *scratch):
    weights_held, ratio_held, sems, small = scratch
    first = fetch(
        [
            pltpu.make_async_copy(panel, right, small.at[0]),
            pltpu.make_async_copy(weights, weights_held, small.at[1]),
            pltpu.make_async_copy(ratio, ratio_held, small.at[2]),
        ]
    )
    begun = scores_begin(plan, (digit,), lax.axis_index("samp"), geno, (held,), sems)
    for copy in first:
        copy.wait()
    mu = weights_held[...].reshape(1, weights_held.shape[0])
    whole = 1.0 / mu + ratio_held[0]
    way = right[...] / whole
    diag[0:1, :] = whole
    diag[1:2, :] = mu
    diag[2:3, :] = jnp.full(mu.shape, ratio_held[0], F32)
    start[...] = way
    start_bf[...] = way.astype(BF16)
    exact = mu * way
    high = exact.astype(BF16)
    weighted[...] = jnp.concatenate([high, (exact - high.astype(F32)).astype(BF16)], axis=0)
    norm = jnp.sum(right[...] * way, axis=1, keepdims=True)
    own = jnp.sum(way * (way / mu), axis=1, keepdims=True)
    lane = lax.broadcasted_iota(jnp.int32, stats.shape, 1)
    stats[...] = jnp.where(lane == 0, norm, jnp.where(lane == 1, own, 0.0))
    scores_finish(plan, begun, start_bf[...], stats[...], (out,))


def scores_kernel(plan, digits, start_bf, stats, geno, *refs):
    *outs, sems = refs
    outs, helds = outs[: len(digits)], outs[len(digits) :]
    begun = scores_begin(plan, digits, lax.axis_index("samp"), geno, helds, sems)
    scores_finish(plan, begun, start_bf[...], stats[...], outs, 2)


def terms_kernel(plan, digit, diag, scores, held, *refs):
    *before, out = refs
    width, total = plan.width, plan.total
    me = lax.axis_index("samp")
    samples = held.shape[1]
    chunks = [me ^ (digit * plan.stride) ^ r for r in plan.rest]
    scale = diag[2:3, 0:1] / plan.markers
    terms = before[0][:, :samples] if before else jnp.zeros((out.shape[0], samples), F32)
    stats = before[0][:, samples:] if before else jnp.zeros((out.shape[0], LANES), F32)
    lane = lax.broadcasted_iota(jnp.int32, stats.shape, 1)
    for j in range(len(chunks)):
        raw = scores[:, j * width : (j + 1) * width]
        fresh = fresh_lanes(chunks[j], width, total, raw.shape[0])
        scaled = jnp.where(fresh, scale * raw, 0.0)
        square = jnp.sum(scaled * raw, axis=1, keepdims=True)
        stats = stats + jnp.where(lane == 2, square, jnp.where((lane < 2) & (chunks[j] == plan.count - 1), raw[:, :LANES], 0.0))
        terms = terms + jnp.dot(
            scaled.astype(BF16), held[j * width : (j + 1) * width, :], preferred_element_type=F32
        )
    out[:, :samples] = terms
    out[:, samples:] = stats


def update_kernel(diag, start, right, own, other, solution, residual, norm, alpha_out):
    samples = start.shape[1]
    total = own[...] + other[...]
    start_norm = own[:, samples : samples + 1]
    curvature = own[:, samples + 1 : samples + 2] + total[:, samples + 2 : samples + 3]
    alpha = start_norm / curvature
    image = start[...] / diag[1:2, :] + total[:, :samples]
    left = right[...] - alpha * image
    solution[...] = alpha * start[...]
    residual[...] = left
    norm[...] = jnp.broadcast_to(jnp.sum(left * (left / diag[0:1, :]), axis=1, keepdims=True), norm.shape)
    alpha_out[...] = jnp.broadcast_to(alpha, alpha_out.shape)


def gene_bounds(sizes, index, count):
    low = jnp.zeros(index.shape, jnp.int32)
    high = jnp.full(index.shape, count, jnp.int32)
    end = jnp.int32(0)
    for g in range(sizes.shape[1]):
        end = end + sizes[0, g]
        low = jnp.where(end <= index, end, low)
        high = jnp.where((end > index) & (end < high), end, high)
    return low, high


def cross_kernel(plan, block, digit, sizes, start_bf, stats, diag, weighted, geno, variants, *refs):
    out, held, *outs, scaled, sems = refs
    me = lax.axis_index("samp")
    begun = scores_begin(plan, (digit,), me, geno, (held,), sems)
    cross_products(plan, block, me, sizes, diag[1:2, :], variants, weighted, scaled, outs)
    scores_finish(plan, begun, start_bf[...], stats[...], (out,), 4)


def cross_products(plan, block, me, sizes, mu, variants, weighted, scaled, outs):
    own_x, own_y, pass_x, pass_y, send_x, send_y = outs
    count = variants.shape[0]
    half = GENE_MAX // 2
    quarter = block * len(plan.rest)
    both = lax.dot_general(weighted[...], variants[...], NT, preferred_element_type=F32)
    rows = both.shape[0] // 2
    beta = both[:rows] + both[rows:]
    for at, (sent, kept) in enumerate(((send_x, pass_x), (send_y, pass_y))):
        sent[half:, :] = beta[:, 2 * at * quarter : 2 * (at + 1) * quarter]
        for j in range(2):
            low = (2 * at + j) * quarter
            kept[half + j * rows : half + (j + 1) * rows, :] = beta[:, low : low + quarter]
    lane = lax.broadcasted_iota(jnp.int32, (1, quarter), 1)
    column = lax.broadcasted_iota(jnp.int32, (count, quarter), 0)
    places = (
        ((own_x, 0), (own_y, 0)),
        ((send_x, 0), (pass_y, 0)),
        ((pass_x, 0), (send_y, 0)),
        ((send_x, 1), (send_y, 1)),
    )
    for digit in range(plan.radix):
        index = lane
        for j, r in enumerate(plan.rest):
            first = pl.multiple_of((me ^ (digit * plan.stride) ^ r) * block, block)
            mine = variants[pl.ds(first, block), :]
            scaled[j * block : (j + 1) * block, :] = (mine.astype(F32) * mu).astype(BF16)
            index = jnp.where(lane // block == j, first + lane - j * block, index)
        cross = lax.dot_general(variants[...], scaled[...], NT, preferred_element_type=F32)
        low, high = gene_bounds(sizes, index, count)
        cross = jnp.where((column >= low) & (column < high), cross, 0.0)
        for part, (out, at) in enumerate(places[digit]):
            folded = None
            for base in range(part * half, count, GENE_MAX):
                piece = cross[base : min(base + half, count)]
                if piece.shape[0] < half:
                    piece = jnp.concatenate([piece, jnp.zeros((half - piece.shape[0], quarter), F32)], axis=0)
                folded = piece if folded is None else folded + piece
            out[:half, at * quarter : (at + 1) * quarter] = folded


def halves_kernel(got_x, got_y, *refs):
    before, after = refs[:4], refs[4:]
    half, quarter = before[0].shape
    rows = got_x.shape[0] - half
    for at, (old, new) in enumerate(zip(before, after)):
        got = (got_x, got_y)[at % 2]
        low = at // 2 * quarter
        new[:half, :] = old[:half, :] + got[:half, low : low + quarter]
        if at >= 2:
            for j in range(2):
                to = slice(half + j * rows, half + (j + 1) * rows)
                new[to, :] = old[to, :] + got[half:, j * quarter : (j + 1) * quarter]


def split_kernel(own_x, own_y, pass_x, pass_y, got_x, got_y, kept, sent):
    half, quarter = own_x.shape
    low, high = own_x[...] + got_x[:half, :], own_y[...] + got_y[:half, :]
    wide = quarter // 4
    cut = [part[:, j * wide : (j + 1) * wide] for j in range(4) for part in (low, high)]
    kept[:half, :] = jnp.concatenate(cut[0:2] + cut[4:6], axis=1)
    sent[:half, :] = jnp.concatenate(cut[2:4] + cut[6:8], axis=1)
    tall = pass_x.shape[0] - half
    for at, (mine, got) in enumerate(((pass_x, got_x), (pass_y, got_y))):
        beta = mine[half:, :] + got[half:, :]
        for out in (kept, sent):
            out[half + at * tall : half + (at + 1) * tall, :] = beta


def pair_kernel(half, kept, got, stay, sent):
    wide = kept.shape[1] // 2
    tall = kept.shape[0] - half
    total = kept[...] + got[...]
    stay[:half, :] = total[:half, :wide]
    sent[:half, :] = total[:half, wide:]
    for out in (stay, sent):
        for j in range(2):
            out[half + j * tall : half + (j + 1) * tall, :] = total[half:, j * wide : (j + 1) * wide]


def direction_kernel(diag, start, held, left, *refs):
    *norms, out = refs
    norm = norms[0][:, :1]
    for ref in norms[1:]:
        norm = norm + ref[:, :1]
    wide = start.shape[1]
    start_norm = held[:, wide : wide + 1]
    out[...] = left[...] / diag[0:1, :] + (norm / start_norm) * start[...]


def gram_kernel(samples, sizes, alpha, solved, left, *refs):
    *sums, solved_out, left_out, gram_out, out, full, sems = refs
    copies = fetch(
        [
            pltpu.make_async_copy(solved, solved_out, sems.at[0]),
            pltpu.make_async_copy(left, left_out, sems.at[1]),
        ]
    )
    me = lax.axis_index("samp")
    count = out.shape[2]
    block = out.shape[1]
    half = GENE_MAX // 2
    rows = full.shape[0]
    total = sums[0][...]
    for ref in sums[1:]:
        total = total + ref[...]
    parts = count // LANES
    for j in range(parts):
        low = half + (j % 2 * (parts // 2) + j // 2) * rows
        full[:, j * LANES : (j + 1) * LANES] = total[low : low + rows, :] * alpha[:, :1]
    cross = jnp.concatenate([total[:half, :block], total[:half, block : 2 * block]], axis=0).T
    cross = jnp.concatenate([cross] * (-(-count // GENE_MAX)), axis=1)[:, :count]
    first = me * block
    window = max(block, LANES)
    base = pl.multiple_of(first // window * window, window)
    wide = lax.dot_general(
        full[:, pl.ds(base, window)],
        full[...],
        (((0,), (0,)), ((), ())),
        precision=lax.Precision.HIGHEST,
        preferred_element_type=F32,
    )
    correction = wide[:block]
    for step in range(1, window // block):
        correction = jnp.where(first - base == step * block, wide[step * block : (step + 1) * block], correction)
    low, high = gene_bounds(sizes, first + lax.broadcasted_iota(jnp.int32, (block, LANES), 0), count)
    column = lax.broadcasted_iota(jnp.int32, (block, count), 1)
    same = (column >= low[:, :1]) & (column < high[:, :1])
    out[0] = jnp.where(same, (cross - correction) / samples, 0.0)
    copies += fetch([pltpu.make_async_copy(out, gram_out, sems.at[2])])
    for copy in copies:
        copy.wait()


def cut_by(products, scores, count, stride):
    wide = products.shape[1] // 8
    low, high = products[:, : 4 * wide], products[:, 4 * wide :]
    cut = [jnp.concatenate([p[:, j * wide : (j + 1) * wide] for p in (low, high)], axis=1) for j in range(4)]
    kept = jnp.concatenate([cut[0], cut[2]], axis=1)
    kept = kept + swap(jnp.concatenate([cut[1], cut[3]], axis=1), count, stride)
    scores = scores + swap(scores, count, stride)
    products = kept[:, : 2 * wide] + swap(kept[:, 2 * wide :], count, 2 * stride)
    return products, scores + swap(scores, count, 2 * stride)


def merge_kernel(*refs):
    terms, outs = refs[:-4], refs[-4:]
    wide = outs[0].shape[1]
    for j, out in enumerate(outs):
        total = terms[0][:, j * wide : (j + 1) * wide]
        for ref in terms[1:]:
            total = total + ref[:, j * wide : (j + 1) * wide]
        out[...] = total


@dataclasses.dataclass(frozen=True)
class Plan:
    count: int
    radix: int
    stride: int
    rest: tuple
    width: int
    total: int
    markers: int


def body(genotypes, variants, weights, variance_ratio, panel, gene_sizes):
    count = lax.axis_size("samp")
    marks = lax.axis_size("mark")
    stages = stages_of(count)
    (radix, stride), later = stages[0], stages[1:]
    firsts = [digit * stride for digit in range(radix)]
    rest = offsets_of(later)
    local, samples = genotypes.shape
    width = up(-(-local // count), LANES)
    if count * width - local < 2:
        width += LANES
    plan = Plan(count, radix, stride, tuple(rest), width, local, local * marks)
    num_variants = variants.shape[0]
    rows = panel.shape[0]
    vmem = pl.BlockSpec(memory_space=VMEM)
    smem = pl.BlockSpec(memory_space=pltpu.SMEM)
    hbm = pl.BlockSpec(memory_space=pltpu.MemorySpace.HBM)
    genotypes, panel, weights = map(in_hbm, (genotypes, panel, weights))
    columns = len(rest) * width
    payload = VMEM((rows, columns), F32)
    window = VMEM((columns, samples), BF16)

    lead = radix - 1
    sent, genos = {}, {}
    sent[lead], genos[lead], diag, right, start, start_bf, weighted, stats = kernel(
        functools.partial(lead_kernel, plan, lead),
        out_shape=[
            payload,
            window,
            VMEM((8, samples), F32),
            VMEM((rows, samples), F32),
            VMEM((rows, samples), F32),
            VMEM((rows, samples), BF16),
            VMEM((2 * rows, samples), BF16),
            VMEM((rows, LANES), F32),
        ],
        in_specs=[hbm] * 4,
        out_specs=[vmem] * 8,
        scratch_shapes=[
            VMEM((samples,), F32),
            pltpu.SMEM((1,), F32),
            pltpu.SemaphoreType.DMA((len(rest),)),
            pltpu.SemaphoreType.DMA((3,)),
        ],
        name="scores_lead",
    )(variance_ratio, weights, panel, genotypes)
    diag, right, start = in_vmem(diag), in_vmem(right), in_vmem(start)
    after = sent[lead]
    start_bf, after = lax.optimization_barrier((start_bf, after))
    digits = tuple(range(1, lead))
    found = kernel(
        functools.partial(scores_kernel, plan, digits),
        out_shape=[payload] * len(digits) + [window] * len(digits),
        in_specs=[vmem] * 2 + [hbm],
        out_specs=[vmem] * (2 * len(digits)),
        scratch_shapes=[
            pltpu.SemaphoreType.DMA((len(digits) * len(rest),)),
        ],
        name="scores",
    )(in_vmem(start_bf), in_vmem(stats), genotypes)
    sent.update(zip(digits, found))
    genos.update(zip(digits, found[len(digits) :]))
    start_bf, after = lax.optimization_barrier((start_bf, found[0]))

    assert radix == 4 and all(r == 4 for r, _ in later)
    block = num_variants // count
    quarter = block * len(rest)
    assert 4 * quarter == num_variants
    half = GENE_MAX // 2
    own_shape = VMEM((half, quarter), F32)
    pass_shape = VMEM((half + 2 * rows, quarter), F32)
    send_shape = VMEM((half + rows, 2 * quarter), F32)
    sent[0], genos[0], *parts, send_x, send_y = kernel(
        functools.partial(cross_kernel, plan, block, 0),
        out_shape=[payload, window] + [own_shape] * 2 + [pass_shape] * 2 + [send_shape] * 2,
        in_specs=[smem] + [vmem] * 4 + [hbm, vmem],
        out_specs=[vmem] * 8,
        scratch_shapes=[
            VMEM((quarter, samples), BF16),
            pltpu.SemaphoreType.DMA((len(rest),)),
        ],
        name="scores_cross",
    )(gene_sizes, in_vmem(start_bf), in_vmem(stats), diag, in_vmem(weighted), genotypes, in_vmem(variants))

    terms = [sent[0]] + [swap(sent[d], count, firsts[d]) for d in range(1, radix)]
    wide = columns
    for r, s in later:
        wide //= r
        pieces = kernel(
            merge_kernel,
            out_shape=[VMEM((rows, wide), F32)] * r,
            in_specs=[vmem] * len(terms),
            out_specs=[vmem] * r,
            name="merge",
        )(*map(in_vmem, terms))
        terms = [pieces[0]] + [swap(pieces[d], count, d * s) for d in range(1, r)]
    got = terms[0]
    for one in terms[1:]:
        got = got + one
    for r, s in reversed(later):
        got = jnp.concatenate([got] + [swap(got, count, d * s) for d in range(1, r)], axis=1)
    arrays = [in_vmem(got)] + [in_vmem(swap(got, count, firsts[d])) for d in range(1, radix)]

    got_x = swap(send_x, count, firsts[1])
    got_y = swap(send_y, count, firsts[2])
    own_x, own_y, pass_x, pass_y = kernel(
        halves_kernel,
        out_shape=[own_shape] * 2 + [pass_shape] * 2,
        in_specs=[vmem] * 6,
        out_specs=[vmem] * 4,
        input_output_aliases={2 + i: i for i in range(4)},
        name="halves",
    )(*map(in_vmem, (got_x, got_y, *parts)))
    got_x, got_y = swap(pass_x, count, firsts[2]), swap(pass_y, count, firsts[1])
    (r, s), deeper = later[0], later[1:]
    wide = quarter // 2
    tall = half + 4 * rows
    kept, moved = kernel(
        split_kernel,
        out_shape=[VMEM((tall, quarter), F32)] * 2,
        in_specs=[vmem] * 6,
        out_specs=[vmem] * 2,
        name="split",
    )(*map(in_vmem, (own_x, own_y, pass_x, pass_y, got_x, got_y)))
    got_x = swap(moved, count, s)
    kept, moved = kernel(
        functools.partial(pair_kernel, half),
        out_shape=[VMEM((tall + 4 * rows, wide), F32)] * 2,
        in_specs=[vmem] * 2,
        out_specs=[vmem] * 2,
        name="pair",
    )(in_vmem(kept), in_vmem(got_x))
    sums = [kept, swap(moved, count, 2 * s)]
    if deeper:
        products, scores = sums[0] + sums[1], None
        products, scores = products[:half], products[half:]
        for r, s in deeper:
            products, scores = cut_by(products, scores, count, s)
        products = jnp.pad(products, ((0, 0), (0, wide - products.shape[1])))
        sums = [jnp.concatenate([products, scores], axis=0)]

    own = ()
    for d in range(radix):
        whole = kernel(
            functools.partial(terms_kernel, plan, d),
            out_shape=VMEM((rows, samples + LANES), F32),
            in_specs=[vmem] * (3 + len(own)),
            out_specs=vmem,
            name="terms",
        )(diag, arrays[d], in_vmem(genos[d]), *map(in_vmem, own))
        own = (whole,)
    (held,) = own
    assert marks & (marks - 1) == 0
    other = None
    offset = 1
    while offset < marks:
        other = swap(held, marks, offset, "mark")
        offset *= 2
        if offset < marks:
            kept = held[:, samples : samples + 2]
            held = held + other
            held = jnp.concatenate([held[:, :samples], kept, held[:, samples + 2 :]], axis=1)
    held = in_vmem(held)
    flat = VMEM((rows, LANES), F32)
    full = jax.ShapeDtypeStruct((rows, samples), F32)
    solution, residual, norm, alpha = kernel(
        update_kernel,
        out_shape=[VMEM((rows, samples), F32)] * 2 + [flat] * 2,
        in_specs=[vmem] * 5,
        out_specs=[vmem] * 4,
        name="update",
    )(diag, start, right, held, in_vmem(other))
    norms = [norm]
    for r, s in stages:
        total = norms[0]
        for one in norms[1:]:
            total = total + one
        norms = [total] + [swap(total, count, d * s) for d in range(1, r)]
    direction = kernel(
        direction_kernel,
        out_shape=full,
        in_specs=[vmem] * (4 + len(norms)),
        out_specs=vmem,
        name="direction",
    )(diag, start, held, *map(in_vmem, (residual, *norms)))
    gram_shape = (1, block, num_variants)
    solution, residual, gram = kernel(
        functools.partial(gram_kernel, samples * count),
        out_shape=[full] * 2 + [jax.ShapeDtypeStruct(gram_shape, F32)],
        in_specs=[smem] + [vmem] * (3 + len(sums)),
        out_specs=[hbm] * 3,
        scratch_shapes=[
            VMEM(gram_shape, F32),
            VMEM((rows, num_variants), F32),
            pltpu.SemaphoreType.DMA((3,)),
        ],
        name="gram",
    )(gene_sizes, *map(in_vmem, (alpha, solution, residual, *sums)))
    return solution, residual, direction, gram


def solution(mesh):
    return jax.shard_map(
        body,
        mesh=mesh,
        in_specs=(
            P("mark", "samp"),
            P("mark", "samp"),
            P("samp"),
            P(),
            P(None, "samp"),
            P("mark", None),
        ),
        out_specs=(P(None, "samp"), P(None, "samp"), P(None, "samp"), P("mark", "samp", None)),
        check_vma=False,
    )
```

```python
import dataclasses
import functools

import jax
import jax.numpy as jnp
from jax import lax
from jax.experimental import pallas as pl
from jax.experimental.pallas import tpu as pltpu
from jax.sharding import PartitionSpec as P


GENE_MAX = 400
LANES = 128
F32 = jnp.float32
BF16 = jnp.bfloat16
VMEM = pltpu.VMEM
NT = (((1,), (1,)), ((), ()))


def up(value, step):
    return -(-value // step) * step


def stages_of(count):
    found, stride = [], 1
    while stride < count:
        radix = 4 if count // stride % 4 == 0 else 2
        found.append((radix, stride))
        stride *= radix
    return found


def offsets_of(stages):
    found = [0]
    for radix, stride in stages:
        found = [base ^ (digit * stride) for base in found for digit in range(radix)]
    return found


def swap(array, count, offset, axis="samp"):
    return lax.ppermute(array, axis, [(i, i ^ offset) for i in range(count)])


def chunk_start(chunk, width, total):
    return pl.multiple_of(jnp.minimum(chunk * width, total - width), 16)


def fresh_lanes(chunk, width, total, rows):
    lane = lax.broadcasted_iota(jnp.int32, (rows, width), 1)
    return lane + jnp.minimum(chunk * width, total - width) >= chunk * width


def kernel(*args, grant=16 << 20, **kwargs):
    return pl.pallas_call(*args, compiler_params=pltpu.CompilerParams(vmem_limit_bytes=grant), **kwargs)


def in_vmem(array):
    return pltpu.with_memory_space_constraint(array, pltpu.VMEM)


def in_hbm(array):
    return pltpu.with_memory_space_constraint(array, pltpu.MemorySpace.HBM)


def fetch(copies):
    for copy in copies:
        copy.start()
    return copies


def geno_copies(plan, chunks, geno, held, sems, base=0):
    width, total = plan.width, plan.total
    return [
        pltpu.make_async_copy(
            geno.at[pl.ds(chunk_start(chunk, width, total), width), :],
            held.at[pl.ds(j * width, width), :],
            sems.at[base + j],
        )
        for j, chunk in enumerate(chunks)
    ]


def scores_begin(plan, digits, me, geno, helds, sems):
    begun, per = [], len(plan.rest)
    for at, (digit, held) in enumerate(zip(digits, helds)):
        chunks = [me ^ (digit * plan.stride) ^ r for r in plan.rest]
        begun.append((chunks, held, fetch(geno_copies(plan, chunks, geno, held, sems, at * per))))
    return begun


def scores_finish(plan, begun, start_bf, stats, outs, group=1):
    width, total = plan.width, plan.total
    for (chunks, held, copies), out in zip(begun, outs):
        for base in range(0, len(copies), group):
            near = range(base, min(base + group, len(copies)))
            for j in near:
                copies[j].wait()
            low, high = near[0] * width, (near[-1] + 1) * width
            parts = lax.dot_general(start_bf, held[low:high, :], NT, preferred_element_type=F32)
            for j in near:
                part = parts[:, j * width - low : (j + 1) * width - low]
                part = jnp.where(fresh_lanes(chunks[j], width, total, part.shape[0]), part, 0.0)
                out[:, j * width : (j + 1) * width] = part
                lane = lax.broadcasted_iota(jnp.int32, stats.shape, 1)
                head = jnp.where((lane < 2) & (chunks[j] == plan.count - 1), stats, part[:, :LANES])
                out[:, j * width : j * width + LANES] = head


def lead_kernel(plan, digit, ratio, weights, panel, geno, out, held, diag, right, start, start_bf, weighted, stats, *scratch):
    weights_held, ratio_held, sems, small = scratch
    first = fetch(
        [
            pltpu.make_async_copy(panel, right, small.at[0]),
            pltpu.make_async_copy(weights, weights_held, small.at[1]),
            pltpu.make_async_copy(ratio, ratio_held, small.at[2]),
        ]
    )
    begun = scores_begin(plan, (digit,), lax.axis_index("samp"), geno, (held,), sems)
    for copy in first:
        copy.wait()
    mu = weights_held[...].reshape(1, weights_held.shape[0])
    whole = 1.0 / mu + ratio_held[0]
    way = right[...] / whole
    diag[0:1, :] = whole
    diag[1:2, :] = mu
    diag[2:3, :] = jnp.full(mu.shape, ratio_held[0], F32)
    start[...] = way
    start_bf[...] = way.astype(BF16)
    exact = mu * way
    high = exact.astype(BF16)
    weighted[...] = jnp.concatenate([high, (exact - high.astype(F32)).astype(BF16)], axis=0)
    norm = jnp.sum(right[...] * way, axis=1, keepdims=True)
    own = jnp.sum(way * (way / mu), axis=1, keepdims=True)
    lane = lax.broadcasted_iota(jnp.int32, stats.shape, 1)
    stats[...] = jnp.where(lane == 0, norm, jnp.where(lane == 1, own, 0.0))
    scores_finish(plan, begun, start_bf[...], stats[...], (out,))


def scores_kernel(plan, digits, start_bf, stats, geno, *refs):
    *outs, sems = refs
    outs, helds = outs[: len(digits)], outs[len(digits) :]
    begun = scores_begin(plan, digits, lax.axis_index("samp"), geno, helds, sems)
    scores_finish(plan, begun, start_bf[...], stats[...], outs, 2)


def terms_kernel(plan, digit, diag, scores, held, *refs):
    *before, out = refs
    width, total = plan.width, plan.total
    me = lax.axis_index("samp")
    samples = held.shape[1]
    chunks = [me ^ (digit * plan.stride) ^ r for r in plan.rest]
    scale = diag[2:3, 0:1] / plan.markers
    terms = before[0][:, :samples] if before else jnp.zeros((out.shape[0], samples), F32)
    stats = before[0][:, samples:] if before else jnp.zeros((out.shape[0], LANES), F32)
    lane = lax.broadcasted_iota(jnp.int32, stats.shape, 1)
    for j in range(len(chunks)):
        raw = scores[:, j * width : (j + 1) * width]
        fresh = fresh_lanes(chunks[j], width, total, raw.shape[0])
        scaled = jnp.where(fresh, scale * raw, 0.0)
        square = jnp.sum(scaled * raw, axis=1, keepdims=True)
        stats = stats + jnp.where(lane == 2, square, jnp.where((lane < 2) & (chunks[j] == plan.count - 1), raw[:, :LANES], 0.0))
        terms = terms + jnp.dot(
            scaled.astype(BF16), held[j * width : (j + 1) * width, :], preferred_element_type=F32
        )
    out[:, :samples] = terms
    out[:, samples:] = stats


def update_kernel(diag, start, right, own, other, solution, residual, norm, alpha_out):
    samples = start.shape[1]
    total = own[...] + other[...]
    start_norm = own[:, samples : samples + 1]
    curvature = own[:, samples + 1 : samples + 2] + total[:, samples + 2 : samples + 3]
    alpha = start_norm / curvature
    image = start[...] / diag[1:2, :] + total[:, :samples]
    left = right[...] - alpha * image
    solution[...] = alpha * start[...]
    residual[...] = left
    norm[...] = jnp.broadcast_to(jnp.sum(left * (left / diag[0:1, :]), axis=1, keepdims=True), norm.shape)
    alpha_out[...] = jnp.broadcast_to(alpha, alpha_out.shape)


def gene_bounds(sizes, index, count):
    low = jnp.zeros(index.shape, jnp.int32)
    high = jnp.full(index.shape, count, jnp.int32)
    end = jnp.int32(0)
    for g in range(sizes.shape[1]):
        end = end + sizes[0, g]
        low = jnp.where(end <= index, end, low)
        high = jnp.where((end > index) & (end < high), end, high)
    return low, high


def cross_kernel(plan, block, digit, sizes, start_bf, stats, diag, weighted, geno, variants, *refs):
    out, held, *outs, scaled, sems = refs
    me = lax.axis_index("samp")
    begun = scores_begin(plan, (digit,), me, geno, (held,), sems)
    share_scores(variants, weighted, *outs)
    pass_x, pass_y, send_x, send_y = outs
    places = {
        1: ((send_x, 0), (pass_y, 0)),
        2: ((pass_x, 0), (send_y, 0)),
        3: ((send_x, 1), (send_y, 1)),
    }
    cross_products(plan, block, me, sizes, diag[1:2, :], variants, scaled, places)
    scores_finish(plan, begun, start_bf[...], stats[...], (out,))


def share_scores(variants, weighted, pass_x, pass_y, send_x, send_y):
    both = lax.dot_general(weighted[...], variants[...], NT, preferred_element_type=F32)
    rows = both.shape[0] // 2
    quarter = pass_x.shape[1]
    half = pass_x.shape[0] - 2 * rows
    beta = both[:rows] + both[rows:]
    for at, (sent, kept) in enumerate(((send_x, pass_x), (send_y, pass_y))):
        sent[half:, :] = beta[:, 2 * at * quarter : 2 * (at + 1) * quarter]
        for j in range(2):
            low = (2 * at + j) * quarter
            kept[half + j * rows : half + (j + 1) * rows, :] = beta[:, low : low + quarter]


def cross_products(plan, block, me, sizes, mu, variants, scaled, places):
    count = variants.shape[0]
    half = GENE_MAX // 2
    quarter = block * len(plan.rest)
    lane = lax.broadcasted_iota(jnp.int32, (1, quarter), 1)
    column = lax.broadcasted_iota(jnp.int32, (count, quarter), 0)
    for digit, homes in places.items():
        index = lane
        for j, r in enumerate(plan.rest):
            first = pl.multiple_of((me ^ (digit * plan.stride) ^ r) * block, block)
            mine = variants[pl.ds(first, block), :]
            scaled[j * block : (j + 1) * block, :] = (mine.astype(F32) * mu).astype(BF16)
            index = jnp.where(lane // block == j, first + lane - j * block, index)
        cross = lax.dot_general(variants[...], scaled[...], NT, preferred_element_type=F32)
        low, high = gene_bounds(sizes, index, count)
        cross = jnp.where((column >= low) & (column < high), cross, 0.0)
        for part, (out, at) in enumerate(homes):
            folded = None
            for base in range(part * half, count, GENE_MAX):
                piece = cross[base : min(base + half, count)]
                if piece.shape[0] < half:
                    piece = jnp.concatenate([piece, jnp.zeros((half - piece.shape[0], quarter), F32)], axis=0)
                folded = piece if folded is None else folded + piece
            out[:half, at * quarter : (at + 1) * quarter] = folded


def own_kernel(plan, block, sizes, diag, variants, own_x, own_y, scaled):
    places = {0: ((own_x, 0), (own_y, 0))}
    cross_products(plan, block, lax.axis_index("samp"), sizes, diag[1:2, :], variants, scaled, places)


def halves_kernel(got_x, got_y, *refs):
    before, after = refs[:4], refs[4:]
    half, quarter = before[0].shape
    rows = got_x.shape[0] - half
    for at, (old, new) in enumerate(zip(before, after)):
        got = (got_x, got_y)[at % 2]
        low = at // 2 * quarter
        new[:half, :] = old[:half, :] + got[:half, low : low + quarter]
        if at >= 2:
            for j in range(2):
                to = slice(half + j * rows, half + (j + 1) * rows)
                new[to, :] = old[to, :] + got[half:, j * quarter : (j + 1) * quarter]


def split_kernel(own_x, own_y, pass_x, pass_y, got_x, got_y, kept, sent):
    half, quarter = own_x.shape
    low, high = own_x[...] + got_x[:half, :], own_y[...] + got_y[:half, :]
    wide = quarter // 4
    cut = [part[:, j * wide : (j + 1) * wide] for j in range(4) for part in (low, high)]
    kept[:half, :] = jnp.concatenate(cut[0:2] + cut[4:6], axis=1)
    sent[:half, :] = jnp.concatenate(cut[2:4] + cut[6:8], axis=1)
    tall = pass_x.shape[0] - half
    for at, (mine, got) in enumerate(((pass_x, got_x), (pass_y, got_y))):
        beta = mine[half:, :] + got[half:, :]
        for out in (kept, sent):
            out[half + at * tall : half + (at + 1) * tall, :] = beta


def pair_kernel(half, kept, got, stay, sent):
    wide = kept.shape[1] // 2
    tall = kept.shape[0] - half
    total = kept[...] + got[...]
    stay[:half, :] = total[:half, :wide]
    sent[:half, :] = total[:half, wide:]
    for out in (stay, sent):
        for j in range(2):
            out[half + j * tall : half + (j + 1) * tall, :] = total[half:, j * wide : (j + 1) * wide]


def direction_kernel(diag, start, held, left, *refs):
    *norms, out = refs
    norm = norms[0][:, :1]
    for ref in norms[1:]:
        norm = norm + ref[:, :1]
    wide = start.shape[1]
    start_norm = held[:, wide : wide + 1]
    out[...] = left[...] / diag[0:1, :] + (norm / start_norm) * start[...]


def gram_kernel(samples, sizes, alpha, solved, left, *refs):
    *sums, solved_out, left_out, gram_out, out, full, sems = refs
    copies = fetch(
        [
            pltpu.make_async_copy(solved, solved_out, sems.at[0]),
            pltpu.make_async_copy(left, left_out, sems.at[1]),
        ]
    )
    me = lax.axis_index("samp")
    count = out.shape[2]
    block = out.shape[1]
    half = GENE_MAX // 2
    rows = full.shape[0]
    total = sums[0][...]
    for ref in sums[1:]:
        total = total + ref[...]
    parts = count // LANES
    for j in range(parts):
        low = half + (j % 2 * (parts // 2) + j // 2) * rows
        full[:, j * LANES : (j + 1) * LANES] = total[low : low + rows, :] * alpha[:, :1]
    cross = jnp.concatenate([total[:half, :block], total[:half, block : 2 * block]], axis=0).T
    cross = jnp.concatenate([cross] * (-(-count // GENE_MAX)), axis=1)[:, :count]
    first = me * block
    window = max(block, LANES)
    base = pl.multiple_of(first // window * window, window)
    wide = lax.dot_general(
        full[:, pl.ds(base, window)],
        full[...],
        (((0,), (0,)), ((), ())),
        precision=lax.Precision.HIGHEST,
        preferred_element_type=F32,
    )
    correction = wide[:block]
    for step in range(1, window // block):
        correction = jnp.where(first - base == step * block, wide[step * block : (step + 1) * block], correction)
    low, high = gene_bounds(sizes, first + lax.broadcasted_iota(jnp.int32, (block, LANES), 0), count)
    column = lax.broadcasted_iota(jnp.int32, (block, count), 1)
    same = (column >= low[:, :1]) & (column < high[:, :1])
    out[0] = jnp.where(same, (cross - correction) / samples, 0.0)
    copies += fetch([pltpu.make_async_copy(out, gram_out, sems.at[2])])
    for copy in copies:
        copy.wait()


def cut_by(products, scores, count, stride):
    wide = products.shape[1] // 8
    low, high = products[:, : 4 * wide], products[:, 4 * wide :]
    cut = [jnp.concatenate([p[:, j * wide : (j + 1) * wide] for p in (low, high)], axis=1) for j in range(4)]
    kept = jnp.concatenate([cut[0], cut[2]], axis=1)
    kept = kept + swap(jnp.concatenate([cut[1], cut[3]], axis=1), count, stride)
    scores = scores + swap(scores, count, stride)
    products = kept[:, : 2 * wide] + swap(kept[:, 2 * wide :], count, 2 * stride)
    return products, scores + swap(scores, count, 2 * stride)


def merge_kernel(*refs):
    terms, outs = refs[:-4], refs[-4:]
    wide = outs[0].shape[1]
    for j, out in enumerate(outs):
        total = terms[0][:, j * wide : (j + 1) * wide]
        for ref in terms[1:]:
            total = total + ref[:, j * wide : (j + 1) * wide]
        out[...] = total


@dataclasses.dataclass(frozen=True)
class Plan:
    count: int
    radix: int
    stride: int
    rest: tuple
    width: int
    total: int
    markers: int


def body(genotypes, variants, weights, variance_ratio, panel, gene_sizes):
    count = lax.axis_size("samp")
    marks = lax.axis_size("mark")
    stages = stages_of(count)
    (radix, stride), later = stages[0], stages[1:]
    firsts = [digit * stride for digit in range(radix)]
    rest = offsets_of(later)
    local, samples = genotypes.shape
    width = up(-(-local // count), LANES)
    if count * width - local < 2:
        width += LANES
    plan = Plan(count, radix, stride, tuple(rest), width, local, local * marks)
    num_variants = variants.shape[0]
    rows = panel.shape[0]
    vmem = pl.BlockSpec(memory_space=VMEM)
    smem = pl.BlockSpec(memory_space=pltpu.SMEM)
    hbm = pl.BlockSpec(memory_space=pltpu.MemorySpace.HBM)
    genotypes, panel, weights = map(in_hbm, (genotypes, panel, weights))
    columns = len(rest) * width
    payload = VMEM((rows, columns), F32)
    window = VMEM((columns, samples), BF16)

    lead = radix - 1
    sent, genos = {}, {}
    sent[lead], genos[lead], diag, right, start, start_bf, weighted, stats = kernel(
        functools.partial(lead_kernel, plan, lead),
        out_shape=[
            payload,
            window,
            VMEM((8, samples), F32),
            VMEM((rows, samples), F32),
            VMEM((rows, samples), F32),
            VMEM((rows, samples), BF16),
            VMEM((2 * rows, samples), BF16),
            VMEM((rows, LANES), F32),
        ],
        in_specs=[hbm] * 4,
        out_specs=[vmem] * 8,
        scratch_shapes=[
            VMEM((samples,), F32),
            pltpu.SMEM((1,), F32),
            pltpu.SemaphoreType.DMA((len(rest),)),
            pltpu.SemaphoreType.DMA((3,)),
        ],
        name="scores_lead",
    )(variance_ratio, weights, panel, genotypes)
    diag, right, start = in_vmem(diag), in_vmem(right), in_vmem(start)
    after = sent[lead]
    start_bf, after = lax.optimization_barrier((start_bf, after))
    digits = tuple(range(1, lead))
    found = kernel(
        functools.partial(scores_kernel, plan, digits),
        out_shape=[payload] * len(digits) + [window] * len(digits),
        in_specs=[vmem] * 2 + [hbm],
        out_specs=[vmem] * (2 * len(digits)),
        scratch_shapes=[
            pltpu.SemaphoreType.DMA((len(digits) * len(rest),)),
        ],
        name="scores",
    )(in_vmem(start_bf), in_vmem(stats), genotypes)
    sent.update(zip(digits, found))
    genos.update(zip(digits, found[len(digits) :]))
    start_bf, after = lax.optimization_barrier((start_bf, found[0]))

    assert radix == 4 and all(r == 4 for r, _ in later)
    block = num_variants // count
    quarter = block * len(rest)
    assert 4 * quarter == num_variants
    half = GENE_MAX // 2
    own_shape = VMEM((half, quarter), F32)
    pass_shape = VMEM((half + 2 * rows, quarter), F32)
    send_shape = VMEM((half + rows, 2 * quarter), F32)
    sent[0], genos[0], pass_x, pass_y, send_x, send_y = kernel(
        functools.partial(cross_kernel, plan, block, 0),
        out_shape=[payload, window] + [pass_shape] * 2 + [send_shape] * 2,
        in_specs=[smem] + [vmem] * 4 + [hbm, vmem],
        out_specs=[vmem] * 6,
        scratch_shapes=[
            VMEM((quarter, samples), BF16),
            pltpu.SemaphoreType.DMA((len(rest),)),
        ],
        name="scores_cross",
    )(gene_sizes, in_vmem(start_bf), in_vmem(stats), diag, in_vmem(weighted), genotypes, in_vmem(variants))
    own_x, own_y = kernel(
        functools.partial(own_kernel, plan, block),
        out_shape=[own_shape] * 2,
        in_specs=[smem] + [vmem] * 2,
        out_specs=[vmem] * 2,
        scratch_shapes=[VMEM((quarter, samples), BF16)],
        name="cross_own",
    )(gene_sizes, diag, in_vmem(variants))

    terms = [sent[0]] + [swap(sent[d], count, firsts[d]) for d in range(1, radix)]
    wide = columns
    for r, s in later:
        wide //= r
        pieces = kernel(
            merge_kernel,
            out_shape=[VMEM((rows, wide), F32)] * r,
            in_specs=[vmem] * len(terms),
            out_specs=[vmem] * r,
            name="merge",
        )(*map(in_vmem, terms))
        terms = [pieces[0]] + [swap(pieces[d], count, d * s) for d in range(1, r)]
    got = terms[0]
    for one in terms[1:]:
        got = got + one
    for r, s in reversed(later):
        got = jnp.concatenate([got] + [swap(got, count, d * s) for d in range(1, r)], axis=1)
    arrays = [in_vmem(got)] + [in_vmem(swap(got, count, firsts[d])) for d in range(1, radix)]

    got_x = swap(send_x, count, firsts[1])
    got_y = swap(send_y, count, firsts[2])
    own_x, own_y, pass_x, pass_y = kernel(
        halves_kernel,
        out_shape=[own_shape] * 2 + [pass_shape] * 2,
        in_specs=[vmem] * 6,
        out_specs=[vmem] * 4,
        input_output_aliases={2 + i: i for i in range(4)},
        name="halves",
    )(*map(in_vmem, (got_x, got_y, own_x, own_y, pass_x, pass_y)))
    got_x, got_y = swap(pass_x, count, firsts[2]), swap(pass_y, count, firsts[1])
    (r, s), deeper = later[0], later[1:]
    wide = quarter // 2
    tall = half + 4 * rows
    kept, moved = kernel(
        split_kernel,
        out_shape=[VMEM((tall, quarter), F32)] * 2,
        in_specs=[vmem] * 6,
        out_specs=[vmem] * 2,
        name="split",
    )(*map(in_vmem, (own_x, own_y, pass_x, pass_y, got_x, got_y)))
    got_x = swap(moved, count, s)
    kept, moved = kernel(
        functools.partial(pair_kernel, half),
        out_shape=[VMEM((tall + 4 * rows, wide), F32)] * 2,
        in_specs=[vmem] * 2,
        out_specs=[vmem] * 2,
        name="pair",
    )(in_vmem(kept), in_vmem(got_x))
    sums = [kept, swap(moved, count, 2 * s)]
    if deeper:
        products, scores = sums[0] + sums[1], None
        products, scores = products[:half], products[half:]
        for r, s in deeper:
            products, scores = cut_by(products, scores, count, s)
        products = jnp.pad(products, ((0, 0), (0, wide - products.shape[1])))
        sums = [jnp.concatenate([products, scores], axis=0)]

    own = ()
    for d in range(radix):
        whole = kernel(
            functools.partial(terms_kernel, plan, d),
            out_shape=VMEM((rows, samples + LANES), F32),
            in_specs=[vmem] * (3 + len(own)),
            out_specs=vmem,
            name="terms",
        )(diag, arrays[d], in_vmem(genos[d]), *map(in_vmem, own))
        own = (whole,)
    (held,) = own
    assert marks & (marks - 1) == 0
    other = None
    offset = 1
    while offset < marks:
        other = swap(held, marks, offset, "mark")
        offset *= 2
        if offset < marks:
            kept = held[:, samples : samples + 2]
            held = held + other
            held = jnp.concatenate([held[:, :samples], kept, held[:, samples + 2 :]], axis=1)
    held = in_vmem(held)
    flat = VMEM((rows, LANES), F32)
    full = jax.ShapeDtypeStruct((rows, samples), F32)
    solution, residual, norm, alpha = kernel(
        update_kernel,
        out_shape=[VMEM((rows, samples), F32)] * 2 + [flat] * 2,
        in_specs=[vmem] * 5,
        out_specs=[vmem] * 4,
        name="update",
    )(diag, start, right, held, in_vmem(other))
    norms = [norm]
    for r, s in stages:
        total = norms[0]
        for one in norms[1:]:
            total = total + one
        norms = [total] + [swap(total, count, d * s) for d in range(1, r)]
    direction = kernel(
        direction_kernel,
        out_shape=full,
        in_specs=[vmem] * (4 + len(norms)),
        out_specs=vmem,
        name="direction",
    )(diag, start, held, *map(in_vmem, (residual, *norms)))
    gram_shape = (1, block, num_variants)
    solution, residual, gram = kernel(
        functools.partial(gram_kernel, samples * count),
        out_shape=[full] * 2 + [jax.ShapeDtypeStruct(gram_shape, F32)],
        in_specs=[smem] + [vmem] * (3 + len(sums)),
        out_specs=[hbm] * 3,
        scratch_shapes=[
            VMEM(gram_shape, F32),
            VMEM((rows, num_variants), F32),
            pltpu.SemaphoreType.DMA((3,)),
        ],
        name="gram",
    )(gene_sizes, *map(in_vmem, (alpha, solution, residual, *sums)))
    return solution, residual, direction, gram


def solution(mesh):
    return jax.shard_map(
        body,
        mesh=mesh,
        in_specs=(
            P("mark", "samp"),
            P("mark", "samp"),
            P("samp"),
            P(),
            P(None, "samp"),
            P("mark", None),
        ),
        out_specs=(P(None, "samp"), P(None, "samp"), P(None, "samp"), P("mark", "samp", None)),
        check_vma=False,
    )
```

```python
import dataclasses
import functools

import jax
import jax.numpy as jnp
from jax import lax
from jax.experimental import pallas as pl
from jax.experimental.pallas import tpu as pltpu
from jax.sharding import PartitionSpec as P


GENE_MAX = 400
LANES = 128
F32 = jnp.float32
BF16 = jnp.bfloat16
VMEM = pltpu.VMEM
NT = (((1,), (1,)), ((), ()))


def up(value, step):
    return -(-value // step) * step


def stages_of(count):
    found, stride = [], 1
    while stride < count:
        radix = 4 if count // stride % 4 == 0 else 2
        found.append((radix, stride))
        stride *= radix
    return found


def offsets_of(stages):
    found = [0]
    for radix, stride in stages:
        found = [base ^ (digit * stride) for base in found for digit in range(radix)]
    return found


def swap(array, count, offset, axis="samp"):
    return lax.ppermute(array, axis, [(i, i ^ offset) for i in range(count)])


def chunk_start(chunk, width, total):
    return pl.multiple_of(jnp.minimum(chunk * width, total - width), 16)


def fresh_lanes(chunk, width, total, rows):
    lane = lax.broadcasted_iota(jnp.int32, (rows, width), 1)
    return lane + jnp.minimum(chunk * width, total - width) >= chunk * width


def kernel(*args, grant=16 << 20, **kwargs):
    return pl.pallas_call(*args, compiler_params=pltpu.CompilerParams(vmem_limit_bytes=grant), **kwargs)


def in_vmem(array):
    return pltpu.with_memory_space_constraint(array, pltpu.VMEM)


def in_hbm(array):
    return pltpu.with_memory_space_constraint(array, pltpu.MemorySpace.HBM)


def fetch(copies):
    for copy in copies:
        copy.start()
    return copies


def geno_copies(plan, chunks, geno, held, sems, base=0):
    width, total = plan.width, plan.total
    return [
        pltpu.make_async_copy(
            geno.at[pl.ds(chunk_start(chunk, width, total), width), :],
            held.at[pl.ds(j * width, width), :],
            sems.at[base + j],
        )
        for j, chunk in enumerate(chunks)
    ]


def scores_begin(plan, digits, me, geno, helds, sems):
    begun, per = [], len(plan.rest)
    for at, (digit, held) in enumerate(zip(digits, helds)):
        chunks = [me ^ (digit * plan.stride) ^ r for r in plan.rest]
        begun.append((chunks, held, fetch(geno_copies(plan, chunks, geno, held, sems, at * per))))
    return begun


def scores_finish(plan, begun, start_bf, stats, outs, group=1):
    width, total = plan.width, plan.total
    for (chunks, held, copies), out in zip(begun, outs):
        for base in range(0, len(copies), group):
            near = range(base, min(base + group, len(copies)))
            for j in near:
                copies[j].wait()
            low, high = near[0] * width, (near[-1] + 1) * width
            parts = lax.dot_general(start_bf, held[low:high, :], NT, preferred_element_type=F32)
            for j in near:
                part = parts[:, j * width - low : (j + 1) * width - low]
                part = jnp.where(fresh_lanes(chunks[j], width, total, part.shape[0]), part, 0.0)
                out[:, j * width : (j + 1) * width] = part
                lane = lax.broadcasted_iota(jnp.int32, stats.shape, 1)
                head = jnp.where((lane < 2) & (chunks[j] == plan.count - 1), stats, part[:, :LANES])
                out[:, j * width : j * width + LANES] = head


def lead_kernel(plan, digit, ratio, weights, panel, geno, out, held, diag, right, start, start_bf, weighted, stats, *scratch):
    weights_held, ratio_held, sems, small = scratch
    first = fetch(
        [
            pltpu.make_async_copy(panel, right, small.at[0]),
            pltpu.make_async_copy(weights, weights_held, small.at[1]),
            pltpu.make_async_copy(ratio, ratio_held, small.at[2]),
        ]
    )
    begun = scores_begin(plan, (digit,), lax.axis_index("samp"), geno, (held,), sems)
    for copy in first:
        copy.wait()
    mu = weights_held[...].reshape(1, weights_held.shape[0])
    whole = 1.0 / mu + ratio_held[0]
    way = right[...] / whole
    diag[0:1, :] = whole
    diag[1:2, :] = mu
    diag[2:3, :] = jnp.full(mu.shape, ratio_held[0], F32)
    start[...] = way
    start_bf[...] = way.astype(BF16)
    exact = mu * way
    high = exact.astype(BF16)
    weighted[...] = jnp.concatenate([high, (exact - high.astype(F32)).astype(BF16)], axis=0)
    norm = jnp.sum(right[...] * way, axis=1, keepdims=True)
    own = jnp.sum(way * (way / mu), axis=1, keepdims=True)
    lane = lax.broadcasted_iota(jnp.int32, stats.shape, 1)
    stats[...] = jnp.where(lane == 0, norm, jnp.where(lane == 1, own, 0.0))
    scores_finish(plan, begun, start_bf[...], stats[...], (out,))


def scores_kernel(plan, digits, start_bf, stats, geno, *refs):
    *outs, sems = refs
    outs, helds = outs[: len(digits)], outs[len(digits) :]
    begun = scores_begin(plan, digits, lax.axis_index("samp"), geno, helds, sems)
    scores_finish(plan, begun, start_bf[...], stats[...], outs, 2)


def terms_kernel(plan, digit, diag, scores, held, *refs):
    *before, out = refs
    width, total = plan.width, plan.total
    me = lax.axis_index("samp")
    samples = held.shape[1]
    chunks = [me ^ (digit * plan.stride) ^ r for r in plan.rest]
    scale = diag[2:3, 0:1] / plan.markers
    terms = before[0][:, :samples] if before else jnp.zeros((out.shape[0], samples), F32)
    stats = before[0][:, samples:] if before else jnp.zeros((out.shape[0], LANES), F32)
    lane = lax.broadcasted_iota(jnp.int32, stats.shape, 1)
    for j in range(len(chunks)):
        raw = scores[:, j * width : (j + 1) * width]
        fresh = fresh_lanes(chunks[j], width, total, raw.shape[0])
        scaled = jnp.where(fresh, scale * raw, 0.0)
        square = jnp.sum(scaled * raw, axis=1, keepdims=True)
        stats = stats + jnp.where(lane == 2, square, jnp.where((lane < 2) & (chunks[j] == plan.count - 1), raw[:, :LANES], 0.0))
        terms = terms + jnp.dot(
            scaled.astype(BF16), held[j * width : (j + 1) * width, :], preferred_element_type=F32
        )
    out[:, :samples] = terms
    out[:, samples:] = stats


def update_kernel(diag, start, right, own, other, solution, residual, norm, alpha_out):
    samples = start.shape[1]
    total = own[...] + other[...]
    start_norm = own[:, samples : samples + 1]
    curvature = own[:, samples + 1 : samples + 2] + total[:, samples + 2 : samples + 3]
    alpha = start_norm / curvature
    image = start[...] / diag[1:2, :] + total[:, :samples]
    left = right[...] - alpha * image
    solution[...] = alpha * start[...]
    residual[...] = left
    norm[...] = jnp.broadcast_to(jnp.sum(left * (left / diag[0:1, :]), axis=1, keepdims=True), norm.shape)
    alpha_out[...] = jnp.broadcast_to(alpha, alpha_out.shape)


def gene_bounds(sizes, index, count):
    low = jnp.zeros(index.shape, jnp.int32)
    high = jnp.full(index.shape, count, jnp.int32)
    end = jnp.int32(0)
    for g in range(sizes.shape[1]):
        end = end + sizes[0, g]
        low = jnp.where(end <= index, end, low)
        high = jnp.where((end > index) & (end < high), end, high)
    return low, high


def cross_kernel(plan, block, digit, sizes, start_bf, stats, diag, weighted, geno, variants, *refs):
    out, held, *outs, scaled, sems = refs
    me = lax.axis_index("samp")
    begun = scores_begin(plan, (digit,), me, geno, (held,), sems)
    share_scores(variants, weighted, *outs)
    pass_x, pass_y, send_x, send_y = outs
    places = {
        1: ((send_x, 0), (pass_y, 0)),
        2: ((pass_x, 0), (send_y, 0)),
        3: ((send_x, 1), (send_y, 1)),
    }
    cross_products(plan, block, me, sizes, diag[1:2, :], variants, scaled, places)
    scores_finish(plan, begun, start_bf[...], stats[...], (out,))


def share_scores(variants, weighted, pass_x, pass_y, send_x, send_y):
    both = lax.dot_general(weighted[...], variants[...], NT, preferred_element_type=F32)
    rows = both.shape[0] // 2
    quarter = pass_x.shape[1]
    half = pass_x.shape[0] - 2 * rows
    beta = both[:rows] + both[rows:]
    for at, (sent, kept) in enumerate(((send_x, pass_x), (send_y, pass_y))):
        sent[half:, :] = beta[:, 2 * at * quarter : 2 * (at + 1) * quarter]
        for j in range(2):
            low = (2 * at + j) * quarter
            kept[half + j * rows : half + (j + 1) * rows, :] = beta[:, low : low + quarter]


def cross_products(plan, block, me, sizes, mu, variants, scaled, places):
    count = variants.shape[0]
    half = GENE_MAX // 2
    quarter = block * len(plan.rest)
    lane = lax.broadcasted_iota(jnp.int32, (1, quarter), 1)
    column = lax.broadcasted_iota(jnp.int32, (count, quarter), 0)
    for digit, homes in places.items():
        index = lane
        for j, r in enumerate(plan.rest):
            first = pl.multiple_of((me ^ (digit * plan.stride) ^ r) * block, block)
            mine = variants[pl.ds(first, block), :]
            scaled[j * block : (j + 1) * block, :] = (mine.astype(F32) * mu).astype(BF16)
            index = jnp.where(lane // block == j, first + lane - j * block, index)
        cross = lax.dot_general(variants[...], scaled[...], NT, preferred_element_type=F32)
        low, high = gene_bounds(sizes, index, count)
        cross = jnp.where((column >= low) & (column < high), cross, 0.0)
        for part, (out, at) in enumerate(homes):
            folded = None
            for base in range(part * half, count, GENE_MAX):
                piece = cross[base : min(base + half, count)]
                if piece.shape[0] < half:
                    piece = jnp.concatenate([piece, jnp.zeros((half - piece.shape[0], quarter), F32)], axis=0)
                folded = piece if folded is None else folded + piece
            out[:half, at * quarter : (at + 1) * quarter] = folded


def own_kernel(plan, block, sizes, diag, variants, own_x, own_y, scaled):
    places = {0: ((own_x, 0), (own_y, 0))}
    cross_products(plan, block, lax.axis_index("samp"), sizes, diag[1:2, :], variants, scaled, places)


def halves_kernel(got_x, got_y, *refs):
    before, after = refs[:4], refs[4:]
    half, quarter = before[0].shape
    rows = got_x.shape[0] - half
    for at, (old, new) in enumerate(zip(before, after)):
        got = (got_x, got_y)[at % 2]
        low = at // 2 * quarter
        new[:half, :] = old[:half, :] + got[:half, low : low + quarter]
        if at >= 2:
            for j in range(2):
                to = slice(half + j * rows, half + (j + 1) * rows)
                new[to, :] = old[to, :] + got[half:, j * quarter : (j + 1) * quarter]


def split_kernel(own_x, own_y, pass_x, pass_y, got_x, got_y, kept, sent):
    half, quarter = own_x.shape
    low, high = own_x[...] + got_x[:half, :], own_y[...] + got_y[:half, :]
    wide = quarter // 4
    cut = [part[:, j * wide : (j + 1) * wide] for j in range(4) for part in (low, high)]
    kept[:half, :] = jnp.concatenate(cut[0:2] + cut[4:6], axis=1)
    sent[:half, :] = jnp.concatenate(cut[2:4] + cut[6:8], axis=1)
    tall = pass_x.shape[0] - half
    for at, (mine, got) in enumerate(((pass_x, got_x), (pass_y, got_y))):
        beta = mine[half:, :] + got[half:, :]
        for out in (kept, sent):
            out[half + at * tall : half + (at + 1) * tall, :] = beta


def pair_kernel(half, kept, got, stay, sent):
    wide = kept.shape[1] // 2
    tall = kept.shape[0] - half
    total = kept[...] + got[...]
    stay[:half, :] = total[:half, :wide]
    sent[:half, :] = total[:half, wide:]
    for out in (stay, sent):
        for j in range(2):
            out[half + j * tall : half + (j + 1) * tall, :] = total[half:, j * wide : (j + 1) * wide]


def direction_kernel(diag, start, held, left, *refs):
    *norms, out = refs
    norm = norms[0][:, :1]
    for ref in norms[1:]:
        norm = norm + ref[:, :1]
    wide = start.shape[1]
    start_norm = held[:, wide : wide + 1]
    out[...] = left[...] / diag[0:1, :] + (norm / start_norm) * start[...]


def gram_kernel(samples, sizes, alpha, solved, left, *refs):
    *sums, solved_out, left_out, gram_out, out, full, sems = refs
    copies = fetch(
        [
            pltpu.make_async_copy(solved, solved_out, sems.at[0]),
            pltpu.make_async_copy(left, left_out, sems.at[1]),
        ]
    )
    me = lax.axis_index("samp")
    count = out.shape[2]
    block = out.shape[1]
    half = GENE_MAX // 2
    rows = full.shape[0]
    total = sums[0][...]
    for ref in sums[1:]:
        total = total + ref[...]
    parts = count // LANES
    for j in range(parts):
        low = half + (j % 2 * (parts // 2) + j // 2) * rows
        full[:, j * LANES : (j + 1) * LANES] = total[low : low + rows, :] * alpha[:, :1]
    cross = jnp.concatenate([total[:half, :block], total[:half, block : 2 * block]], axis=0).T
    cross = jnp.concatenate([cross] * (-(-count // GENE_MAX)), axis=1)[:, :count]
    first = me * block
    window = max(block, LANES)
    base = pl.multiple_of(first // window * window, window)
    near = full[:, pl.ds(base, window)]
    mine = near[:, :block]
    for step in range(1, window // block):
        mine = jnp.where(first - base == step * block, near[:, step * block : (step + 1) * block], mine)
    low, high = gene_bounds(sizes, first + lax.broadcasted_iota(jnp.int32, (block, LANES), 0), count)
    wide = count // 2
    for at in range(2):
        here = slice(at * wide, (at + 1) * wide)
        correction = lax.dot_general(
            mine,
            full[:, here],
            (((0,), (0,)), ((), ())),
            precision=lax.Precision.HIGHEST,
            preferred_element_type=F32,
        )
        column = lax.broadcasted_iota(jnp.int32, (block, wide), 1) + at * wide
        same = (column >= low[:, :1]) & (column < high[:, :1])
        out[0, :, here] = jnp.where(same, (cross[:, here] - correction) / samples, 0.0)
        copies += fetch([pltpu.make_async_copy(out.at[:, :, here], gram_out.at[:, :, here], sems.at[2 + at])])
    for copy in copies:
        copy.wait()


def cut_by(products, scores, count, stride):
    wide = products.shape[1] // 8
    low, high = products[:, : 4 * wide], products[:, 4 * wide :]
    cut = [jnp.concatenate([p[:, j * wide : (j + 1) * wide] for p in (low, high)], axis=1) for j in range(4)]
    kept = jnp.concatenate([cut[0], cut[2]], axis=1)
    kept = kept + swap(jnp.concatenate([cut[1], cut[3]], axis=1), count, stride)
    scores = scores + swap(scores, count, stride)
    products = kept[:, : 2 * wide] + swap(kept[:, 2 * wide :], count, 2 * stride)
    return products, scores + swap(scores, count, 2 * stride)


def merge_kernel(*refs):
    terms, outs = refs[:-4], refs[-4:]
    wide = outs[0].shape[1]
    for j, out in enumerate(outs):
        total = terms[0][:, j * wide : (j + 1) * wide]
        for ref in terms[1:]:
            total = total + ref[:, j * wide : (j + 1) * wide]
        out[...] = total


@dataclasses.dataclass(frozen=True)
class Plan:
    count: int
    radix: int
    stride: int
    rest: tuple
    width: int
    total: int
    markers: int


def body(genotypes, variants, weights, variance_ratio, panel, gene_sizes):
    count = lax.axis_size("samp")
    marks = lax.axis_size("mark")
    stages = stages_of(count)
    (radix, stride), later = stages[0], stages[1:]
    firsts = [digit * stride for digit in range(radix)]
    rest = offsets_of(later)
    local, samples = genotypes.shape
    width = up(-(-local // count), LANES)
    if count * width - local < 2:
        width += LANES
    plan = Plan(count, radix, stride, tuple(rest), width, local, local * marks)
    num_variants = variants.shape[0]
    rows = panel.shape[0]
    vmem = pl.BlockSpec(memory_space=VMEM)
    smem = pl.BlockSpec(memory_space=pltpu.SMEM)
    hbm = pl.BlockSpec(memory_space=pltpu.MemorySpace.HBM)
    genotypes, panel, weights = map(in_hbm, (genotypes, panel, weights))
    columns = len(rest) * width
    payload = VMEM((rows, columns), F32)
    window = VMEM((columns, samples), BF16)

    lead = radix - 1
    sent, genos = {}, {}
    sent[lead], genos[lead], diag, right, start, start_bf, weighted, stats = kernel(
        functools.partial(lead_kernel, plan, lead),
        out_shape=[
            payload,
            window,
            VMEM((8, samples), F32),
            VMEM((rows, samples), F32),
            VMEM((rows, samples), F32),
            VMEM((rows, samples), BF16),
            VMEM((2 * rows, samples), BF16),
            VMEM((rows, LANES), F32),
        ],
        in_specs=[hbm] * 4,
        out_specs=[vmem] * 8,
        scratch_shapes=[
            VMEM((samples,), F32),
            pltpu.SMEM((1,), F32),
            pltpu.SemaphoreType.DMA((len(rest),)),
            pltpu.SemaphoreType.DMA((3,)),
        ],
        name="scores_lead",
    )(variance_ratio, weights, panel, genotypes)
    diag, right, start = in_vmem(diag), in_vmem(right), in_vmem(start)
    after = sent[lead]
    start_bf, after = lax.optimization_barrier((start_bf, after))
    digits = tuple(range(1, lead))
    found = kernel(
        functools.partial(scores_kernel, plan, digits),
        out_shape=[payload] * len(digits) + [window] * len(digits),
        in_specs=[vmem] * 2 + [hbm],
        out_specs=[vmem] * (2 * len(digits)),
        scratch_shapes=[
            pltpu.SemaphoreType.DMA((len(digits) * len(rest),)),
        ],
        name="scores",
    )(in_vmem(start_bf), in_vmem(stats), genotypes)
    sent.update(zip(digits, found))
    genos.update(zip(digits, found[len(digits) :]))
    start_bf, after = lax.optimization_barrier((start_bf, found[0]))

    assert radix == 4 and all(r == 4 for r, _ in later)
    block = num_variants // count
    quarter = block * len(rest)
    assert 4 * quarter == num_variants
    half = GENE_MAX // 2
    own_shape = VMEM((half, quarter), F32)
    pass_shape = VMEM((half + 2 * rows, quarter), F32)
    send_shape = VMEM((half + rows, 2 * quarter), F32)
    sent[0], genos[0], pass_x, pass_y, send_x, send_y = kernel(
        functools.partial(cross_kernel, plan, block, 0),
        out_shape=[payload, window] + [pass_shape] * 2 + [send_shape] * 2,
        in_specs=[smem] + [vmem] * 4 + [hbm, vmem],
        out_specs=[vmem] * 6,
        scratch_shapes=[
            VMEM((quarter, samples), BF16),
            pltpu.SemaphoreType.DMA((len(rest),)),
        ],
        name="scores_cross",
    )(gene_sizes, in_vmem(start_bf), in_vmem(stats), diag, in_vmem(weighted), genotypes, in_vmem(variants))
    own_x, own_y = kernel(
        functools.partial(own_kernel, plan, block),
        out_shape=[own_shape] * 2,
        in_specs=[smem] + [vmem] * 2,
        out_specs=[vmem] * 2,
        scratch_shapes=[VMEM((quarter, samples), BF16)],
        name="cross_own",
    )(gene_sizes, diag, in_vmem(variants))

    terms = [sent[0]] + [swap(sent[d], count, firsts[d]) for d in range(1, radix)]
    wide = columns
    for r, s in later:
        wide //= r
        pieces = kernel(
            merge_kernel,
            out_shape=[VMEM((rows, wide), F32)] * r,
            in_specs=[vmem] * len(terms),
            out_specs=[vmem] * r,
            name="merge",
        )(*map(in_vmem, terms))
        terms = [pieces[0]] + [swap(pieces[d], count, d * s) for d in range(1, r)]
    got = terms[0]
    for one in terms[1:]:
        got = got + one
    for r, s in reversed(later):
        got = jnp.concatenate([got] + [swap(got, count, d * s) for d in range(1, r)], axis=1)
    arrays = [in_vmem(got)] + [in_vmem(swap(got, count, firsts[d])) for d in range(1, radix)]

    got_x = swap(send_x, count, firsts[1])
    got_y = swap(send_y, count, firsts[2])
    own_x, own_y, pass_x, pass_y = kernel(
        halves_kernel,
        out_shape=[own_shape] * 2 + [pass_shape] * 2,
        in_specs=[vmem] * 6,
        out_specs=[vmem] * 4,
        input_output_aliases={2 + i: i for i in range(4)},
        name="halves",
    )(*map(in_vmem, (got_x, got_y, own_x, own_y, pass_x, pass_y)))
    got_x, got_y = swap(pass_x, count, firsts[2]), swap(pass_y, count, firsts[1])
    (r, s), deeper = later[0], later[1:]
    wide = quarter // 2
    tall = half + 4 * rows
    kept, moved = kernel(
        split_kernel,
        out_shape=[VMEM((tall, quarter), F32)] * 2,
        in_specs=[vmem] * 6,
        out_specs=[vmem] * 2,
        name="split",
    )(*map(in_vmem, (own_x, own_y, pass_x, pass_y, got_x, got_y)))
    got_x = swap(moved, count, s)
    kept, moved = kernel(
        functools.partial(pair_kernel, half),
        out_shape=[VMEM((tall + 4 * rows, wide), F32)] * 2,
        in_specs=[vmem] * 2,
        out_specs=[vmem] * 2,
        name="pair",
    )(in_vmem(kept), in_vmem(got_x))
    sums = [kept, swap(moved, count, 2 * s)]
    if deeper:
        products, scores = sums[0] + sums[1], None
        products, scores = products[:half], products[half:]
        for r, s in deeper:
            products, scores = cut_by(products, scores, count, s)
        products = jnp.pad(products, ((0, 0), (0, wide - products.shape[1])))
        sums = [jnp.concatenate([products, scores], axis=0)]

    own = ()
    for d in range(radix):
        whole = kernel(
            functools.partial(terms_kernel, plan, d),
            out_shape=VMEM((rows, samples + LANES), F32),
            in_specs=[vmem] * (3 + len(own)),
            out_specs=vmem,
            name="terms",
        )(diag, arrays[d], in_vmem(genos[d]), *map(in_vmem, own))
        own = (whole,)
    (held,) = own
    assert marks & (marks - 1) == 0
    other = None
    offset = 1
    while offset < marks:
        other = swap(held, marks, offset, "mark")
        offset *= 2
        if offset < marks:
            kept = held[:, samples : samples + 2]
            held = held + other
            held = jnp.concatenate([held[:, :samples], kept, held[:, samples + 2 :]], axis=1)
    held = in_vmem(held)
    flat = VMEM((rows, LANES), F32)
    full = jax.ShapeDtypeStruct((rows, samples), F32)
    solution, residual, norm, alpha = kernel(
        update_kernel,
        out_shape=[VMEM((rows, samples), F32)] * 2 + [flat] * 2,
        in_specs=[vmem] * 5,
        out_specs=[vmem] * 4,
        name="update",
    )(diag, start, right, held, in_vmem(other))
    norms = [norm]
    for r, s in stages:
        total = norms[0]
        for one in norms[1:]:
            total = total + one
        norms = [total] + [swap(total, count, d * s) for d in range(1, r)]
    direction = kernel(
        direction_kernel,
        out_shape=full,
        in_specs=[vmem] * (4 + len(norms)),
        out_specs=vmem,
        name="direction",
    )(diag, start, held, *map(in_vmem, (residual, *norms)))
    gram_shape = (1, block, num_variants)
    solution, residual, gram = kernel(
        functools.partial(gram_kernel, samples * count),
        out_shape=[full] * 2 + [jax.ShapeDtypeStruct(gram_shape, F32)],
        in_specs=[smem] + [vmem] * (3 + len(sums)),
        out_specs=[hbm] * 3,
        scratch_shapes=[
            VMEM(gram_shape, F32),
            VMEM((rows, num_variants), F32),
            pltpu.SemaphoreType.DMA((4,)),
        ],
        name="gram",
    )(gene_sizes, *map(in_vmem, (alpha, solution, residual, *sums)))
    return solution, residual, direction, gram


def solution(mesh):
    return jax.shard_map(
        body,
        mesh=mesh,
        in_specs=(
            P("mark", "samp"),
            P("mark", "samp"),
            P("samp"),
            P(),
            P(None, "samp"),
            P("mark", None),
        ),
        out_specs=(P(None, "samp"), P(None, "samp"), P(None, "samp"), P("mark", "samp", None)),
        check_vma=False,
    )
```

```python
import dataclasses
import functools

import jax
import jax.numpy as jnp
from jax import lax
from jax.experimental import pallas as pl
from jax.experimental.pallas import tpu as pltpu
from jax.sharding import PartitionSpec as P


GENE_MAX = 400
LANES = 128
F32 = jnp.float32
BF16 = jnp.bfloat16
VMEM = pltpu.VMEM
NT = (((1,), (1,)), ((), ()))


def up(value, step):
    return -(-value // step) * step


def stages_of(count):
    found, stride = [], 1
    while stride < count:
        radix = 4 if count // stride % 4 == 0 else 2
        found.append((radix, stride))
        stride *= radix
    return found


def offsets_of(stages):
    found = [0]
    for radix, stride in stages:
        found = [base ^ (digit * stride) for base in found for digit in range(radix)]
    return found


def swap(array, count, offset, axis="samp"):
    return lax.ppermute(array, axis, [(i, i ^ offset) for i in range(count)])


def chunk_start(chunk, width, total):
    return pl.multiple_of(jnp.minimum(chunk * width, total - width), 16)


def fresh_lanes(chunk, width, total, rows):
    lane = lax.broadcasted_iota(jnp.int32, (rows, width), 1)
    return lane + jnp.minimum(chunk * width, total - width) >= chunk * width


def kernel(*args, grant=16 << 20, **kwargs):
    return pl.pallas_call(*args, compiler_params=pltpu.CompilerParams(vmem_limit_bytes=grant), **kwargs)


def in_vmem(array):
    return pltpu.with_memory_space_constraint(array, pltpu.VMEM)


def in_hbm(array):
    return pltpu.with_memory_space_constraint(array, pltpu.MemorySpace.HBM)


def fetch(copies):
    for copy in copies:
        copy.start()
    return copies


def geno_copies(plan, chunks, geno, held, sems, base=0):
    width, total = plan.width, plan.total
    return [
        pltpu.make_async_copy(
            geno.at[pl.ds(chunk_start(chunk, width, total), width), :],
            held.at[pl.ds(j * width, width), :],
            sems.at[base + j],
        )
        for j, chunk in enumerate(chunks)
    ]


def scores_begin(plan, digits, me, geno, helds, sems):
    begun, per = [], len(plan.rest)
    for at, (digit, held) in enumerate(zip(digits, helds)):
        chunks = [me ^ (digit * plan.stride) ^ r for r in plan.rest]
        begun.append((chunks, held, fetch(geno_copies(plan, chunks, geno, held, sems, at * per))))
    return begun


def scores_finish(plan, begun, start_bf, stats, outs, group=1):
    width, total = plan.width, plan.total
    for (chunks, held, copies), out in zip(begun, outs):
        for base in range(0, len(copies), group):
            near = range(base, min(base + group, len(copies)))
            for j in near:
                copies[j].wait()
            low, high = near[0] * width, (near[-1] + 1) * width
            parts = lax.dot_general(start_bf, held[low:high, :], NT, preferred_element_type=F32)
            for j in near:
                part = parts[:, j * width - low : (j + 1) * width - low]
                part = jnp.where(fresh_lanes(chunks[j], width, total, part.shape[0]), part, 0.0)
                out[:, j * width : (j + 1) * width] = part
                lane = lax.broadcasted_iota(jnp.int32, stats.shape, 1)
                head = jnp.where((lane < 2) & (chunks[j] == plan.count - 1), stats, part[:, :LANES])
                out[:, j * width : j * width + LANES] = head
        group = len(copies)


def lead_kernel(plan, digit, ratio, weights, panel, geno, out, held, diag, right, start, start_bf, weighted, stats, *scratch):
    weights_held, ratio_held, sems, small = scratch
    first = fetch(
        [
            pltpu.make_async_copy(panel, right, small.at[0]),
            pltpu.make_async_copy(weights, weights_held, small.at[1]),
            pltpu.make_async_copy(ratio, ratio_held, small.at[2]),
        ]
    )
    begun = scores_begin(plan, (digit,), lax.axis_index("samp"), geno, (held,), sems)
    for copy in first:
        copy.wait()
    mu = weights_held[...].reshape(1, weights_held.shape[0])
    whole = 1.0 / mu + ratio_held[0]
    way = right[...] / whole
    diag[0:1, :] = whole
    diag[1:2, :] = mu
    diag[2:3, :] = jnp.full(mu.shape, ratio_held[0], F32)
    start[...] = way
    start_bf[...] = way.astype(BF16)
    exact = mu * way
    high = exact.astype(BF16)
    weighted[...] = jnp.concatenate([high, (exact - high.astype(F32)).astype(BF16)], axis=0)
    norm = jnp.sum(right[...] * way, axis=1, keepdims=True)
    own = jnp.sum(way * (way / mu), axis=1, keepdims=True)
    lane = lax.broadcasted_iota(jnp.int32, stats.shape, 1)
    stats[...] = jnp.where(lane == 0, norm, jnp.where(lane == 1, own, 0.0))
    scores_finish(plan, begun, start_bf[...], stats[...], (out,))


def scores_kernel(plan, digits, start_bf, stats, geno, *refs):
    *outs, sems = refs
    outs, helds = outs[: len(digits)], outs[len(digits) :]
    begun = scores_begin(plan, digits, lax.axis_index("samp"), geno, helds, sems)
    scores_finish(plan, begun, start_bf[...], stats[...], outs, 2)


def terms_kernel(plan, digit, diag, scores, held, *refs):
    *before, out = refs
    width, total = plan.width, plan.total
    me = lax.axis_index("samp")
    samples = held.shape[1]
    chunks = [me ^ (digit * plan.stride) ^ r for r in plan.rest]
    scale = diag[2:3, 0:1] / plan.markers
    terms = before[0][:, :samples] if before else jnp.zeros((out.shape[0], samples), F32)
    stats = before[0][:, samples:] if before else jnp.zeros((out.shape[0], LANES), F32)
    lane = lax.broadcasted_iota(jnp.int32, stats.shape, 1)
    for j in range(len(chunks)):
        raw = scores[:, j * width : (j + 1) * width]
        fresh = fresh_lanes(chunks[j], width, total, raw.shape[0])
        scaled = jnp.where(fresh, scale * raw, 0.0)
        square = jnp.sum(scaled * raw, axis=1, keepdims=True)
        stats = stats + jnp.where(lane == 2, square, jnp.where((lane < 2) & (chunks[j] == plan.count - 1), raw[:, :LANES], 0.0))
        terms = terms + jnp.dot(
            scaled.astype(BF16), held[j * width : (j + 1) * width, :], preferred_element_type=F32
        )
    out[:, :samples] = terms
    out[:, samples:] = stats


def update_kernel(diag, start, right, own, other, solution, residual, norm, alpha_out):
    samples = start.shape[1]
    total = own[...] + other[...]
    start_norm = own[:, samples : samples + 1]
    curvature = own[:, samples + 1 : samples + 2] + total[:, samples + 2 : samples + 3]
    alpha = start_norm / curvature
    image = start[...] / diag[1:2, :] + total[:, :samples]
    left = right[...] - alpha * image
    solution[...] = alpha * start[...]
    residual[...] = left
    norm[...] = jnp.broadcast_to(jnp.sum(left * (left / diag[0:1, :]), axis=1, keepdims=True), norm.shape)
    alpha_out[...] = jnp.broadcast_to(alpha, alpha_out.shape)


def gene_bounds(sizes, index, count):
    low = jnp.zeros(index.shape, jnp.int32)
    high = jnp.full(index.shape, count, jnp.int32)
    end = jnp.int32(0)
    for g in range(sizes.shape[1]):
        end = end + sizes[0, g]
        low = jnp.where(end <= index, end, low)
        high = jnp.where((end > index) & (end < high), end, high)
    return low, high


def cross_kernel(plan, block, sizes, diag, weighted, variants, *refs):
    *outs, scaled = refs
    me = lax.axis_index("samp")
    share_scores(variants, weighted, *outs)
    pass_x, pass_y, send_x, send_y = outs
    places = {
        1: ((send_x, 0), (pass_y, 0)),
        2: ((pass_x, 0), (send_y, 0)),
        3: ((send_x, 1), (send_y, 1)),
    }
    cross_products(plan, block, me, sizes, diag[1:2, :], variants, scaled, places)


def share_scores(variants, weighted, pass_x, pass_y, send_x, send_y):
    both = lax.dot_general(weighted[...], variants[...], NT, preferred_element_type=F32)
    rows = both.shape[0] // 2
    quarter = pass_x.shape[1]
    half = pass_x.shape[0] - 2 * rows
    beta = both[:rows] + both[rows:]
    for at, (sent, kept) in enumerate(((send_x, pass_x), (send_y, pass_y))):
        sent[half:, :] = beta[:, 2 * at * quarter : 2 * (at + 1) * quarter]
        for j in range(2):
            low = (2 * at + j) * quarter
            kept[half + j * rows : half + (j + 1) * rows, :] = beta[:, low : low + quarter]


def cross_products(plan, block, me, sizes, mu, variants, scaled, places):
    count = variants.shape[0]
    half = GENE_MAX // 2
    quarter = block * len(plan.rest)
    lane = lax.broadcasted_iota(jnp.int32, (1, quarter), 1)
    column = lax.broadcasted_iota(jnp.int32, (count, quarter), 0)
    for digit, homes in places.items():
        index = lane
        for j, r in enumerate(plan.rest):
            first = pl.multiple_of((me ^ (digit * plan.stride) ^ r) * block, block)
            mine = variants[pl.ds(first, block), :]
            scaled[j * block : (j + 1) * block, :] = (mine.astype(F32) * mu).astype(BF16)
            index = jnp.where(lane // block == j, first + lane - j * block, index)
        cross = lax.dot_general(variants[...], scaled[...], NT, preferred_element_type=F32)
        low, high = gene_bounds(sizes, index, count)
        cross = jnp.where((column >= low) & (column < high), cross, 0.0)
        for part, (out, at) in enumerate(homes):
            folded = None
            for base in range(part * half, count, GENE_MAX):
                piece = cross[base : min(base + half, count)]
                if piece.shape[0] < half:
                    piece = jnp.concatenate([piece, jnp.zeros((half - piece.shape[0], quarter), F32)], axis=0)
                folded = piece if folded is None else folded + piece
            out[:half, at * quarter : (at + 1) * quarter] = folded


def own_kernel(plan, block, sizes, diag, variants, own_x, own_y, scaled):
    places = {0: ((own_x, 0), (own_y, 0))}
    cross_products(plan, block, lax.axis_index("samp"), sizes, diag[1:2, :], variants, scaled, places)


def halves_kernel(got_x, got_y, *refs):
    before, after = refs[:4], refs[4:]
    half, quarter = before[0].shape
    rows = got_x.shape[0] - half
    for at, (old, new) in enumerate(zip(before, after)):
        got = (got_x, got_y)[at % 2]
        low = at // 2 * quarter
        new[:half, :] = old[:half, :] + got[:half, low : low + quarter]
        if at >= 2:
            for j in range(2):
                to = slice(half + j * rows, half + (j + 1) * rows)
                new[to, :] = old[to, :] + got[half:, j * quarter : (j + 1) * quarter]


def split_kernel(own_x, own_y, pass_x, pass_y, got_x, got_y, kept, sent):
    half, quarter = own_x.shape
    low, high = own_x[...] + got_x[:half, :], own_y[...] + got_y[:half, :]
    wide = quarter // 4
    cut = [part[:, j * wide : (j + 1) * wide] for j in range(4) for part in (low, high)]
    kept[:half, :] = jnp.concatenate(cut[0:2] + cut[4:6], axis=1)
    sent[:half, :] = jnp.concatenate(cut[2:4] + cut[6:8], axis=1)
    tall = pass_x.shape[0] - half
    for at, (mine, got) in enumerate(((pass_x, got_x), (pass_y, got_y))):
        beta = mine[half:, :] + got[half:, :]
        for out in (kept, sent):
            out[half + at * tall : half + (at + 1) * tall, :] = beta


def pair_kernel(half, kept, got, stay, sent):
    wide = kept.shape[1] // 2
    tall = kept.shape[0] - half
    total = kept[...] + got[...]
    stay[:half, :] = total[:half, :wide]
    sent[:half, :] = total[:half, wide:]
    for out in (stay, sent):
        for j in range(2):
            out[half + j * tall : half + (j + 1) * tall, :] = total[half:, j * wide : (j + 1) * wide]


def direction_kernel(diag, start, held, left, *refs):
    *norms, out = refs
    norm = norms[0][:, :1]
    for ref in norms[1:]:
        norm = norm + ref[:, :1]
    wide = start.shape[1]
    start_norm = held[:, wide : wide + 1]
    out[...] = left[...] / diag[0:1, :] + (norm / start_norm) * start[...]


def gram_kernel(samples, sizes, alpha, solved, left, *refs):
    *sums, solved_out, left_out, gram_out, out, full, sems = refs
    copies = fetch(
        [
            pltpu.make_async_copy(solved, solved_out, sems.at[0]),
            pltpu.make_async_copy(left, left_out, sems.at[1]),
        ]
    )
    me = lax.axis_index("samp")
    count = out.shape[2]
    block = out.shape[1]
    half = GENE_MAX // 2
    rows = full.shape[0]
    total = sums[0][...]
    for ref in sums[1:]:
        total = total + ref[...]
    parts = count // LANES
    for j in range(parts):
        low = half + (j % 2 * (parts // 2) + j // 2) * rows
        full[:, j * LANES : (j + 1) * LANES] = total[low : low + rows, :] * alpha[:, :1]
    cross = jnp.concatenate([total[:half, :block], total[:half, block : 2 * block]], axis=0).T
    cross = jnp.concatenate([cross] * (-(-count // GENE_MAX)), axis=1)[:, :count]
    first = me * block
    window = max(block, LANES)
    base = pl.multiple_of(first // window * window, window)
    near = full[:, pl.ds(base, window)]
    mine = near[:, :block]
    for step in range(1, window // block):
        mine = jnp.where(first - base == step * block, near[:, step * block : (step + 1) * block], mine)
    low, high = gene_bounds(sizes, first + lax.broadcasted_iota(jnp.int32, (block, LANES), 0), count)
    wide = count // 2
    for at in range(2):
        here = slice(at * wide, (at + 1) * wide)
        correction = lax.dot_general(
            mine,
            full[:, here],
            (((0,), (0,)), ((), ())),
            precision=lax.Precision.HIGHEST,
            preferred_element_type=F32,
        )
        column = lax.broadcasted_iota(jnp.int32, (block, wide), 1) + at * wide
        same = (column >= low[:, :1]) & (column < high[:, :1])
        out[0, :, here] = jnp.where(same, (cross[:, here] - correction) / samples, 0.0)
        copies += fetch([pltpu.make_async_copy(out.at[:, :, here], gram_out.at[:, :, here], sems.at[2 + at])])
    for copy in copies:
        copy.wait()


def cut_by(products, scores, count, stride):
    wide = products.shape[1] // 8
    low, high = products[:, : 4 * wide], products[:, 4 * wide :]
    cut = [jnp.concatenate([p[:, j * wide : (j + 1) * wide] for p in (low, high)], axis=1) for j in range(4)]
    kept = jnp.concatenate([cut[0], cut[2]], axis=1)
    kept = kept + swap(jnp.concatenate([cut[1], cut[3]], axis=1), count, stride)
    scores = scores + swap(scores, count, stride)
    products = kept[:, : 2 * wide] + swap(kept[:, 2 * wide :], count, 2 * stride)
    return products, scores + swap(scores, count, 2 * stride)


def merge_kernel(*refs):
    terms, outs = refs[:-4], refs[-4:]
    wide = outs[0].shape[1]
    for j, out in enumerate(outs):
        total = terms[0][:, j * wide : (j + 1) * wide]
        for ref in terms[1:]:
            total = total + ref[:, j * wide : (j + 1) * wide]
        out[...] = total


@dataclasses.dataclass(frozen=True)
class Plan:
    count: int
    radix: int
    stride: int
    rest: tuple
    width: int
    total: int
    markers: int


def body(genotypes, variants, weights, variance_ratio, panel, gene_sizes):
    count = lax.axis_size("samp")
    marks = lax.axis_size("mark")
    stages = stages_of(count)
    (radix, stride), later = stages[0], stages[1:]
    firsts = [digit * stride for digit in range(radix)]
    rest = offsets_of(later)
    local, samples = genotypes.shape
    width = up(-(-local // count), LANES)
    if count * width - local < 2:
        width += LANES
    plan = Plan(count, radix, stride, tuple(rest), width, local, local * marks)
    num_variants = variants.shape[0]
    rows = panel.shape[0]
    vmem = pl.BlockSpec(memory_space=VMEM)
    smem = pl.BlockSpec(memory_space=pltpu.SMEM)
    hbm = pl.BlockSpec(memory_space=pltpu.MemorySpace.HBM)
    genotypes, panel, weights = map(in_hbm, (genotypes, panel, weights))
    columns = len(rest) * width
    payload = VMEM((rows, columns), F32)
    window = VMEM((columns, samples), BF16)

    lead = radix - 1
    sent, genos = {}, {}
    sent[lead], genos[lead], diag, right, start, start_bf, weighted, stats = kernel(
        functools.partial(lead_kernel, plan, lead),
        out_shape=[
            payload,
            window,
            VMEM((8, samples), F32),
            VMEM((rows, samples), F32),
            VMEM((rows, samples), F32),
            VMEM((rows, samples), BF16),
            VMEM((2 * rows, samples), BF16),
            VMEM((rows, LANES), F32),
        ],
        in_specs=[hbm] * 4,
        out_specs=[vmem] * 8,
        scratch_shapes=[
            VMEM((samples,), F32),
            pltpu.SMEM((1,), F32),
            pltpu.SemaphoreType.DMA((len(rest),)),
            pltpu.SemaphoreType.DMA((3,)),
        ],
        name="scores_lead",
    )(variance_ratio, weights, panel, genotypes)
    diag, right, start = in_vmem(diag), in_vmem(right), in_vmem(start)
    after = sent[lead]
    start_bf, after = lax.optimization_barrier((start_bf, after))
    digits = (*range(1, lead), 0)
    found = kernel(
        functools.partial(scores_kernel, plan, digits),
        out_shape=[payload] * len(digits) + [window] * len(digits),
        in_specs=[vmem] * 2 + [hbm],
        out_specs=[vmem] * (2 * len(digits)),
        scratch_shapes=[
            pltpu.SemaphoreType.DMA((len(digits) * len(rest),)),
        ],
        name="scores",
    )(in_vmem(start_bf), in_vmem(stats), genotypes)
    sent.update(zip(digits, found))
    genos.update(zip(digits, found[len(digits) :]))
    weighted, after = lax.optimization_barrier((weighted, found[0]))

    assert radix == 4 and all(r == 4 for r, _ in later)
    block = num_variants // count
    quarter = block * len(rest)
    assert 4 * quarter == num_variants
    half = GENE_MAX // 2
    own_shape = VMEM((half, quarter), F32)
    pass_shape = VMEM((half + 2 * rows, quarter), F32)
    send_shape = VMEM((half + rows, 2 * quarter), F32)
    pass_x, pass_y, send_x, send_y = kernel(
        functools.partial(cross_kernel, plan, block),
        out_shape=[pass_shape] * 2 + [send_shape] * 2,
        in_specs=[smem] + [vmem] * 3,
        out_specs=[vmem] * 4,
        scratch_shapes=[VMEM((quarter, samples), BF16)],
        name="cross_sent",
    )(gene_sizes, diag, in_vmem(weighted), in_vmem(variants))
    own_x, own_y = kernel(
        functools.partial(own_kernel, plan, block),
        out_shape=[own_shape] * 2,
        in_specs=[smem] + [vmem] * 2,
        out_specs=[vmem] * 2,
        scratch_shapes=[VMEM((quarter, samples), BF16)],
        name="cross_own",
    )(gene_sizes, diag, in_vmem(variants))

    terms = [sent[0]] + [swap(sent[d], count, firsts[d]) for d in range(1, radix)]
    wide = columns
    for r, s in later:
        wide //= r
        pieces = kernel(
            merge_kernel,
            out_shape=[VMEM((rows, wide), F32)] * r,
            in_specs=[vmem] * len(terms),
            out_specs=[vmem] * r,
            name="merge",
        )(*map(in_vmem, terms))
        terms = [pieces[0]] + [swap(pieces[d], count, d * s) for d in range(1, r)]
    got = terms[0]
    for one in terms[1:]:
        got = got + one
    for r, s in reversed(later):
        got = jnp.concatenate([got] + [swap(got, count, d * s) for d in range(1, r)], axis=1)
    arrays = [in_vmem(got)] + [in_vmem(swap(got, count, firsts[d])) for d in range(1, radix)]

    got_x = swap(send_x, count, firsts[1])
    got_y = swap(send_y, count, firsts[2])
    own_x, own_y, pass_x, pass_y = kernel(
        halves_kernel,
        out_shape=[own_shape] * 2 + [pass_shape] * 2,
        in_specs=[vmem] * 6,
        out_specs=[vmem] * 4,
        input_output_aliases={2 + i: i for i in range(4)},
        name="halves",
    )(*map(in_vmem, (got_x, got_y, own_x, own_y, pass_x, pass_y)))
    got_x, got_y = swap(pass_x, count, firsts[2]), swap(pass_y, count, firsts[1])
    (r, s), deeper = later[0], later[1:]
    wide = quarter // 2
    tall = half + 4 * rows
    kept, moved = kernel(
        split_kernel,
        out_shape=[VMEM((tall, quarter), F32)] * 2,
        in_specs=[vmem] * 6,
        out_specs=[vmem] * 2,
        name="split",
    )(*map(in_vmem, (own_x, own_y, pass_x, pass_y, got_x, got_y)))
    got_x = swap(moved, count, s)
    kept, moved = kernel(
        functools.partial(pair_kernel, half),
        out_shape=[VMEM((tall + 4 * rows, wide), F32)] * 2,
        in_specs=[vmem] * 2,
        out_specs=[vmem] * 2,
        name="pair",
    )(in_vmem(kept), in_vmem(got_x))
    sums = [kept, swap(moved, count, 2 * s)]
    if deeper:
        products, scores = sums[0] + sums[1], None
        products, scores = products[:half], products[half:]
        for r, s in deeper:
            products, scores = cut_by(products, scores, count, s)
        products = jnp.pad(products, ((0, 0), (0, wide - products.shape[1])))
        sums = [jnp.concatenate([products, scores], axis=0)]

    own = ()
    for d in range(radix):
        whole = kernel(
            functools.partial(terms_kernel, plan, d),
            out_shape=VMEM((rows, samples + LANES), F32),
            in_specs=[vmem] * (3 + len(own)),
            out_specs=vmem,
            name="terms",
        )(diag, arrays[d], in_vmem(genos[d]), *map(in_vmem, own))
        own = (whole,)
    (held,) = own
    assert marks & (marks - 1) == 0
    other = None
    offset = 1
    while offset < marks:
        other = swap(held, marks, offset, "mark")
        offset *= 2
        if offset < marks:
            kept = held[:, samples : samples + 2]
            held = held + other
            held = jnp.concatenate([held[:, :samples], kept, held[:, samples + 2 :]], axis=1)
    held = in_vmem(held)
    flat = VMEM((rows, LANES), F32)
    full = jax.ShapeDtypeStruct((rows, samples), F32)
    solution, residual, norm, alpha = kernel(
        update_kernel,
        out_shape=[VMEM((rows, samples), F32)] * 2 + [flat] * 2,
        in_specs=[vmem] * 5,
        out_specs=[vmem] * 4,
        name="update",
    )(diag, start, right, held, in_vmem(other))
    norms = [norm]
    for r, s in stages:
        total = norms[0]
        for one in norms[1:]:
            total = total + one
        norms = [total] + [swap(total, count, d * s) for d in range(1, r)]
    direction = kernel(
        direction_kernel,
        out_shape=full,
        in_specs=[vmem] * (4 + len(norms)),
        out_specs=vmem,
        name="direction",
    )(diag, start, held, *map(in_vmem, (residual, *norms)))
    gram_shape = (1, block, num_variants)
    solution, residual, gram = kernel(
        functools.partial(gram_kernel, samples * count),
        out_shape=[full] * 2 + [jax.ShapeDtypeStruct(gram_shape, F32)],
        in_specs=[smem] + [vmem] * (3 + len(sums)),
        out_specs=[hbm] * 3,
        scratch_shapes=[
            VMEM(gram_shape, F32),
            VMEM((rows, num_variants), F32),
            pltpu.SemaphoreType.DMA((4,)),
        ],
        name="gram",
    )(gene_sizes, *map(in_vmem, (alpha, solution, residual, *sums)))
    return solution, residual, direction, gram


def solution(mesh):
    return jax.shard_map(
        body,
        mesh=mesh,
        in_specs=(
            P("mark", "samp"),
            P("mark", "samp"),
            P("samp"),
            P(),
            P(None, "samp"),
            P("mark", None),
        ),
        out_specs=(P(None, "samp"), P(None, "samp"), P(None, "samp"), P("mark", "samp", None)),
        check_vma=False,
    )
```
